32 devices in a mesh: expert: 8 (over z, y), dp: 4 (over x, core).
Axes of the slice: x: 2, y: 2, z: 4, core: 2. Of those that a mesh axis runs over, the one named last changes fastest.
Arguments:
- tokens: bfloat16 [4096, 4096], P(('expert', 'dp')), may hold values from -6 to 6
- expert_ids: int32 [4096, 2], P(('expert', 'dp')), may hold values from 0 to 15, all different within a row; in each aligned block of 128 rows (0 to 127, 128 to 255, ...) at most 48 rows name the same one
- gate_codes: int32 [4096, 2], P(('expert', 'dp')), may hold values from 1 to 255
- first_shared: bfloat16 [64, 64, 64], P('dp'), may hold values from -0.75 to 0.75
- second_shared: bfloat16 [64, 64, 256], P('dp'), may hold values from -0.75 to 0.75
- third_shared: bfloat16 [64, 256, 64], P('dp'), may hold values from -0.375 to 0.375
- fourth_shared: bfloat16 [64, 64, 64], P('dp'), may hold values from -0.75 to 0.75
- first_routed: bfloat16 [16, 64, 64, 64], P('expert'), may hold values from -0.75 to 0.75
- second_routed: bfloat16 [16, 64, 64, 256], P('expert'), may hold values from -0.75 to 0.75
- third_routed: bfloat16 [16, 64, 256, 64], P('expert'), may hold values from -0.375 to 0.375
- fourth_routed: bfloat16 [16, 64, 64, 64], P('expert'), may hold values from -0.75 to 0.75
Outputs:
- mixed: bfloat16 [4096, 4096], P(('expert', 'dp'))
The draws below stay inside these ranges and needn't reach their ends.
Inputs may be any that keep to these rules, and one draw needn't show every extreme that they name: `expert_ids`: each token names two different experts; among the 128 tokens of one device no expert is named more than 48 times.
All inputs are finite; a program needn't handle non-finite values.
Results may differ from the reference program's by a relative error of at most 0.0075.
Values may be sent and summed in bfloat16 or wider, within the bound.
A program may use at most 128 MiB of HBM per device.

```python
import math
import jax
import jax.numpy as jnp
import numpy as np
from jax import lax

D = 4096
NB = 64
DB = 64
HB = 256
EXPERTS = 16
TOK_DEV = 128
TOKENS = 4096
MOST = 48


def set_ends(drawn, own_key, least, top_value):
    extent = drawn.shape
    index_at = [jax.random.randint(jax.random.fold_in(own_key, axis), (), 0, extent[axis]) for axis in range(len(extent))]
    drawn = drawn.at[tuple(index_at)].set(least)
    longest = extent.index(max(extent))
    index_at[longest] = (index_at[longest] + 1) % extent[longest]
    return drawn.at[tuple(index_at)].set(top_value)


def block_scale(own_key, dims, shards, low, top_value):
    gain, own = 1.0, jax.random.fold_in(own_key, 6)
    for dim, blocks in shards:
        heights = jnp.exp(jax.random.uniform(jax.random.fold_in(own, dim), (blocks,), jnp.float32, low / len(shards), top_value / len(shards)))
        gain = gain * jnp.repeat(heights, dims[dim] // blocks).reshape([-1 if axis == dim else 1 for axis in range(len(dims))])
    return gain


def deal_out(stream_key, own, number, rows, number_of, top, limit, lean):
    order = jax.random.permutation(stream_key, number_of)
    packed, ordinary = portions_of(number_of, rows * top, limit, lean, True), portions_of(number_of, rows * top, limit, lean, False)
    places = jnp.arange(number_of)

    def named(lengths, rotation):
        used = int((lengths > 0).sum())
        fixed = max(1, used // 4)
        shifted = fixed + (places - fixed + rotation * (used - fixed)) % max(1, number_of - fixed)
        return jnp.zeros((number_of,), jnp.int32).at[order[jnp.where(places < fixed, places, shifted)]].set(jnp.asarray(lengths, jnp.int32))

    lengths = jnp.where(number % 4 == 0, named(packed, number // 4), named(ordinary, number - number // 4 - 1))
    mixed = jax.random.permutation(jax.random.fold_in(own, 3), number_of)
    donor, taker = mixed[0:number_of // 2 * 2:2], mixed[1:number_of // 2 * 2:2]
    room = jnp.minimum(lengths[donor] - 1, limit - lengths[taker]) // 2
    room = jnp.where((donor == order[0]) | (taker == order[0]) | (lengths[taker] == 0), 0, jnp.maximum(room, 0))
    shifted = jax.random.randint(jax.random.fold_in(own, 4), (number_of // 2,), 0, 1 << 20) % (room + 1)
    lengths = lengths.at[donor].add(-shifted).at[taker].add(shifted)
    labels = jnp.searchsorted(jnp.cumsum(lengths), jnp.arange(rows * top), side="right").astype(jnp.int32)
    listing = labels.reshape(top, rows).T
    listing = listing[jax.random.permutation(jax.random.fold_in(own, 1), rows)]
    rotation = jax.random.randint(jax.random.fold_in(own, 2), (rows, 1), 0, top)
    return jnp.take_along_axis(listing, (jnp.arange(top)[None, :] + rotation) % top, axis=1)


def portions_of(count, total, reach, lean, full):
    portions = [(1 << 20) // math.isqrt(standing ** lean) + 1 for standing in range(1, count + 1)]
    largest = reach if full else min(reach, max(-(-total // count), total * portions[0] // sum(portions)))
    least = 1 if total - largest >= count - 1 else 0
    given, spare = [largest] + [least] * (count - 1), total - largest - least * (count - 1)
    while spare > 0:
        free = [i for i in range(1, count) if given[i] < largest] or [i for i in range(1, count) if given[i] < reach]
        pool, remaining = sum([portions[i] for i in free]), spare
        for i in free:
            extra = min(reach - given[i], max(1, remaining * portions[i] // pool), spare)
            given[i] = given[i] + extra
            spare = spare - extra
    return np.array(given)


def centred(own_key, dims, spread, reach, shards=(), held_as=jnp.bfloat16):
    loudness = block_scale(own_key, dims, shards, -0.22, 0.18) if shards else 1.0
    values = jax.random.normal(own_key, dims, jnp.float32) * spread * loudness
    return jnp.minimum(jnp.maximum(values, -reach), reach).astype(held_as)


def setup_inputs(seed: int = 0) -> dict:
    seeds = jax.random.split(jax.random.key(seed), 12)
    tokens = centred(seeds[0], (TOKENS, D), 1.0, 6.0, ((0, 32),))
    expert_ids_keys = jax.random.split(jax.random.fold_in(seeds[1], 1), TOKENS // TOK_DEV)
    expert_ids_turns = jax.random.permutation(jax.random.fold_in(seeds[1], 3), TOKENS // TOK_DEV)
    expert_ids = jax.vmap(lambda own, number: deal_out(jax.random.fold_in(seeds[1], 2), own, number, TOK_DEV, EXPERTS, 2, MOST, 2))(expert_ids_keys, expert_ids_turns).reshape((TOKENS, 2))
    gate_codes = set_ends(jax.random.randint(seeds[2], (TOKENS, 2), 1, 256), jax.random.fold_in(seeds[2], 1), 1, 255).astype(jnp.int32)
    first_shared = centred(seeds[3], (NB, DB, NB), DB ** -0.5, 0.75, ((0, 4),))
    second_shared = centred(seeds[4], (NB, NB, HB), NB ** -0.5, 0.75, ((0, 4),))
    third_shared = centred(seeds[5], (NB, HB, NB), HB ** -0.5, 0.375, ((0, 4),))
    fourth_shared = centred(seeds[6], (NB, NB, DB), NB ** -0.5, 0.75, ((0, 4),))
    first_routed = centred(seeds[7], (EXPERTS, NB, DB, NB), DB ** -0.5, 0.75, ((0, 8),))
    second_routed = centred(seeds[8], (EXPERTS, NB, NB, HB), NB ** -0.5, 0.75, ((0, 8),))
    third_routed = centred(seeds[9], (EXPERTS, NB, HB, NB), HB ** -0.5, 0.375, ((0, 8),))
    fourth_routed = centred(seeds[10], (EXPERTS, NB, NB, DB), NB ** -0.5, 0.75, ((0, 8),))
    return dict(tokens=tokens, expert_ids=expert_ids, gate_codes=gate_codes, first_shared=first_shared, second_shared=second_shared, third_shared=third_shared, fourth_shared=fourth_shared, first_routed=first_routed, second_routed=second_routed, third_routed=third_routed, fourth_routed=fourth_routed)


row_block = 512


def expand(rows, first, second):
    blocks = rows.reshape(rows.shape[0], NB, DB).astype(jnp.float32)
    first_out = jnp.einsum("rab,abj->raj", blocks, first.astype(jnp.float32)).astype(jnp.bfloat16)
    first_out = lax.optimization_barrier(first_out)
    hidden = jnp.einsum("raj,jac->rjc", first_out.astype(jnp.float32), second.astype(jnp.float32))
    return jax.nn.gelu(hidden, approximate=False).astype(jnp.bfloat16)


def contract(hidden, third, fourth):
    hidden = lax.optimization_barrier(hidden)
    inner = jnp.einsum("rjc,jck->rjk", hidden.astype(jnp.float32), third.astype(jnp.float32)).astype(jnp.bfloat16)
    inner = lax.optimization_barrier(inner)
    output = jnp.einsum("rjk,kjm->rkm", inner.astype(jnp.float32), fourth.astype(jnp.float32))
    return output.reshape(output.shape[0], D).astype(jnp.bfloat16)


def monarch(rows, factors):
    return contract(expand(rows, factors[0], factors[1]), factors[2], factors[3])


def reference(tokens, expert_ids, gate_codes, first_shared, second_shared, third_shared, fourth_shared,
              first_routed, second_routed, third_routed, fourth_routed):
    shared = (first_shared, second_shared, third_shared, fourth_shared)
    routed = (first_routed, second_routed, third_routed, fourth_routed)
    blocksize = math.gcd(TOKENS, row_block)

    def shared_block(rows):
        return monarch(rows, shared)

    shared_out = lax.map(shared_block, tokens.reshape(TOKENS // blocksize, blocksize, D)).reshape(TOKENS, D)

    picks = expert_ids.reshape(-1).astype(jnp.int32)
    pair_count = picks.shape[0]
    ordering = jnp.argsort(picks, stable=True).astype(jnp.int32)
    counts = jnp.sum((picks[:, None] == jnp.arange(EXPERTS, dtype=jnp.int32)[None, :]).astype(jnp.int32), axis=0)
    starts = (jnp.cumsum(counts) - counts).astype(jnp.int32)
    padded_order = jnp.concatenate([ordering, jnp.zeros((row_block,), jnp.int32)])
    outputs = jnp.zeros((pair_count, D), jnp.bfloat16)

    def expert_step(number, outputs):
        factors = tuple(lax.dynamic_index_in_dim(weight, number, 0, keepdims=False) for weight in routed)
        begin = starts[number]
        amount = counts[number]
        nblocks = (amount + row_block - 1) // row_block

        def block_step(position, outputs):
            offset = (begin + position * row_block).astype(jnp.int32)
            indexes = lax.dynamic_slice_in_dim(padded_order, offset, row_block)
            valid = (offset + jnp.arange(row_block, dtype=jnp.int32)) < begin + amount
            rows = tokens[indexes // 2]
            values = monarch(rows, factors)
            target = jnp.where(valid, indexes, pair_count).astype(jnp.int32)
            return outputs.at[target].set(values, mode="drop")

        return lax.fori_loop(0, nblocks, block_step, outputs)

    outputs = lax.fori_loop(0, EXPERTS, expert_step, outputs)
    routed_out = outputs.reshape(TOKENS, 2, D).astype(jnp.float32)
    codes = gate_codes.astype(jnp.float32)
    gates = codes / jnp.sum(codes, axis=1, keepdims=True)
    total = shared_out.astype(jnp.float32) + gates[:, 0:1] * routed_out[:, 0] + gates[:, 1:2] * routed_out[:, 1]
    return total.astype(jnp.bfloat16)
```

```python
import functools
import math

import jax
import jax.numpy as jnp
from jax import lax
from jax.experimental import pallas as pl
from jax.experimental.pallas import tpu as pltpu
from jax.sharding import PartitionSpec as P

D = 4096
NB = 64
DB = 64
HB = 256
T = 128
F32 = jnp.float32
BF16 = jnp.bfloat16


def tile_monarch(x_ref, lanes, w1_ref, w2_ref, w3_ref, w4_ref, z_refs, u_refs, store):
    def spread(refs, rows, value):
        for i in range(lanes):
            refs[i][rows, :] = value[:, i * T : (i + 1) * T]

    def strided(refs, start):
        parts = [refs[i][pl.ds(start, NB, stride=NB), :] for i in range(lanes)]
        return jnp.concatenate(parts, axis=1).astype(BF16)

    def up(a, carry):
        rows = pl.ds(pl.multiple_of(a * DB, DB), DB)
        x = x_ref[rows, : lanes * T]
        spread(z_refs, rows, jnp.dot(w1_ref[0, a], x, preferred_element_type=F32))
        return carry

    lax.fori_loop(0, NB, up, 0, unroll=8)

    def middle(j, carry):
        hidden = jnp.dot(w2_ref[0, j], strided(z_refs, j), preferred_element_type=F32)
        hidden = (0.5 * hidden) * (1.0 + lax.erf(hidden * (0.5**0.5)))
        u = jnp.dot(w3_ref[0, j], hidden.astype(BF16), preferred_element_type=F32)
        spread(u_refs, pl.ds(pl.multiple_of(j * NB, NB), NB), u)
        return carry

    lax.fori_loop(0, NB, middle, 0, unroll=4)

    def down(k, carry):
        rows = pl.ds(pl.multiple_of(k * DB, DB), DB)
        store(rows, jnp.dot(w4_ref[0, k], strided(u_refs, k), preferred_element_type=F32))
        return carry

    lax.fori_loop(0, NB, down, 0, unroll=8)


def shared_kernel(x_ref, w1_ref, w2_ref, w3_ref, w4_ref, o_ref, z_ref, u_ref):
    def store(rows, value):
        o_ref[rows, :] = value.astype(BF16)

    tile_monarch(x_ref, 1, w1_ref, w2_ref, w3_ref, w4_ref, (z_ref,), (u_ref,), store)


def routed_kernel(
    counts_ref, pos_ref, gate_ref, x_ref, w1_ref, w2_ref, w3_ref, w4_ref,
    o_ref, x_scr, z0_ref, z1_ref, u0_ref, u1_ref,
):
    expert, tile = pl.program_id(0), pl.program_id(1)
    left = counts_ref[expert] - tile * 2 * T
    sources = x_ref.shape[0]

    @pl.when(left <= T)
    def _():
        o_ref[...] = jnp.zeros_like(o_ref)

    def serve(lanes):
        width = lanes * T
        wanted = lax.broadcasted_iota(jnp.int32, (width, 2 * T), 0) + tile * 2 * T
        step = D // 8

        for part in range(8):
            rows = pl.ds(part * step, step)

            def pick(pair, total):
                both = jnp.concatenate([x_ref[2 * pair, rows, :], x_ref[2 * pair + 1, rows, :]], axis=1)
                onehot = (wanted == pos_ref[0, pair, :, :]).astype(F32).astype(BF16)
                return total + lax.dot_general(
                    both, onehot, (((1,), (1,)), ((), ())), preferred_element_type=F32
                )

            total = lax.fori_loop(0, sources // 2, pick, jnp.zeros((step, width), F32))
            x_scr[rows, :width] = total.astype(BF16)

        gate = gate_ref[0, 0][:, :width]

        def store(rows, value):
            o_ref[rows, :width] = (value * gate).astype(BF16)

        tile_monarch(
            x_scr, lanes, w1_ref, w2_ref, w3_ref, w4_ref, (z0_ref, z1_ref), (u0_ref, u1_ref), store
        )

    @pl.when(left > T)
    def _():
        serve(2)

    @pl.when(jnp.logical_and(left > 0, left <= T))
    def _():
        serve(1)


def weight_specs(index_map, buffers=2):
    shapes = ((NB, DB), (HB, NB), (NB, HB), (DB, NB))
    mode = pl.Buffered(buffers)
    return [pl.BlockSpec((1, NB) + shape, index_map, pipeline_mode=mode) for shape in shapes]


def turned(factors):
    return tuple(jnp.swapaxes(w, -1, -2) for w in factors)


def shared_call(x_t, factors):
    return pl.pallas_call(
        shared_kernel,
        out_shape=jax.ShapeDtypeStruct((D, T), BF16),
        grid=(1,),
        in_specs=[pl.BlockSpec((D, T), lambda i: (0, 0))] + weight_specs(lambda i: (0, 0, 0, 0)),
        out_specs=pl.BlockSpec((D, T), lambda i: (0, 0)),
        scratch_shapes=[pltpu.VMEM((D, T), F32), pltpu.VMEM((D, T), F32)],
        compiler_params=pltpu.CompilerParams(vmem_limit_bytes=56 * 2**20),
        cost_estimate=pl.CostEstimate(flops=10**10, bytes_accessed=10**7, transcendentals=0),
        name="shared_expert",
    )(x_t, *factors)


def routed_call(counts, pos, slot_gates, x_all, factors, tiles):
    residents = pos.shape[0]
    sources = x_all.shape[0]
    grid_spec = pltpu.PrefetchScalarGridSpec(
        num_scalar_prefetch=1,
        grid=(residents, tiles),
        in_specs=[
            pl.BlockSpec((1, sources // 2, 1, 2 * T), lambda e, i, c: (e, 0, 0, 0)),
            pl.BlockSpec((1, 1, 1, 2 * T), lambda e, i, c: (e, i, 0, 0)),
            pl.BlockSpec((sources, x_all.shape[1], T), lambda e, i, c: (0, 0, 0), pipeline_mode=pl.Buffered(1)),
        ]
        + weight_specs(lambda e, i, c: (e, 0, 0, 0), 2 if sources <= 8 else 1),
        out_specs=pl.BlockSpec((D, 2 * T), lambda e, i, c: (0, e * tiles + i)),
        scratch_shapes=[pltpu.VMEM((D, 2 * T), BF16)] + [pltpu.VMEM((D, T), F32)] * 4,
    )
    return pl.pallas_call(
        routed_kernel,
        out_shape=jax.ShapeDtypeStruct((D, residents * tiles * 2 * T), BF16),
        grid_spec=grid_spec,
        compiler_params=pltpu.CompilerParams(vmem_limit_bytes=62 * 2**20),
        cost_estimate=pl.CostEstimate(flops=4 * 10**10, bytes_accessed=2 * 10**7, transcendentals=0),
        name="routed_experts",
    )(counts, pos, slot_gates, x_all, *factors)


def combine_kernel(depth, window, starts_ref, pos_ref, o_ref, y_ref):
    residents = starts_ref.shape[0]
    pair = pl.program_id(0)
    wanted = lax.broadcasted_iota(jnp.int32, (window, 2 * T), 0)
    begins = [pl.multiple_of(starts_ref[e, pair] * T, T) for e in range(residents)]
    hots = [
        (wanted + begins[e] == pos_ref[e, 0, :, :]).astype(F32).astype(BF16) for e in range(residents)
    ]
    hot = jnp.concatenate(hots, axis=0)
    step = 512

    def part(i, carry):
        rows = pl.ds(pl.multiple_of(i * step, step), step)
        near = [
            o_ref[rows, pl.ds(pl.multiple_of(begins[e] + e * depth, T), window)] for e in range(residents)
        ]
        total = jnp.dot(jnp.concatenate(near, axis=1), hot, preferred_element_type=F32).astype(BF16)
        y_ref[0, rows, :] = total[:, :T]
        y_ref[1, rows, :] = total[:, T:]
        return carry

    lax.fori_loop(0, D // step, part, 0)


def combine_call(starts, pos, outs, sources, depth, window):
    residents = pos.shape[0]
    grid_spec = pltpu.PrefetchScalarGridSpec(
        num_scalar_prefetch=1,
        grid=(sources // 2,),
        in_specs=[
            pl.BlockSpec((residents, 1, 1, 2 * T), lambda s, c: (0, s, 0, 0)),
            pl.BlockSpec((D, residents * depth), lambda s, c: (0, 0), pipeline_mode=pl.Buffered(1)),
        ],
        out_specs=pl.BlockSpec((2, D, T), lambda s, c: (s, 0, 0)),
    )
    return pl.pallas_call(
        functools.partial(combine_kernel, depth, window),
        out_shape=jax.ShapeDtypeStruct((sources, D, T), BF16),
        grid_spec=grid_spec,
        compiler_params=pltpu.CompilerParams(vmem_limit_bytes=48 * 2**20),
        name="combine",
    )(starts, pos, outs)


def grid_of(count):
    side = math.isqrt(count // 2)
    return count // side, side


def greet(z, y, nz, ny):
    barrier = pltpu.get_barrier_semaphore()
    for other in range(1, ny):
        pl.semaphore_signal(barrier, inc=1, device_id={"expert": z * ny + lax.rem(y + other, ny)})

    @pl.when(z > 0)
    def _():
        pl.semaphore_signal(barrier, inc=1, device_id={"expert": (z - 1) * ny + y})

    @pl.when(z < nz - 1)
    def _():
        pl.semaphore_signal(barrier, inc=1, device_id={"expert": (z + 1) * ny + y})

    peers = ny - 1 + jnp.where(z > 0, 1, 0) + jnp.where(z < nz - 1, 1, 0)
    pl.semaphore_wait(barrier, peers)


def gather_kernel(nz, x_ref, out_ref, own_sem, up_sem, down_sem, side_sem, recv_sem):
    ny = 2
    me = lax.axis_index("expert")
    z, y = me // ny, lax.rem(me, ny)
    beside = z * ny + (1 - y)

    def send(block, src, sem, target):
        return pltpu.make_async_remote_copy(
            src_ref=src, dst_ref=out_ref.at[block], send_sem=sem.at[block],
            recv_sem=recv_sem.at[block], device_id={"expert": target},
        )

    def arrived(block):
        send(block, out_ref.at[block], side_sem, beside).wait_recv()

    greet(z, y, nz, ny)
    own = pltpu.make_async_copy(x_ref, out_ref.at[me], own_sem)
    own.start()

    @pl.when(z < nz - 1)
    def _():
        send(me, x_ref, up_sem, me + ny).start()

    @pl.when(z > 0)
    def _():
        send(me, x_ref, down_sem, me - ny).start()

    send(me, x_ref, side_sem, beside).start()

    for k in range(1, nz):
        block = me - k * ny

        @pl.when(z >= k)
        def _():
            arrived(block)

            @pl.when(z < nz - 1)
            def _():
                send(block, out_ref.at[block], up_sem, me + ny).start()

            send(block, out_ref.at[block], side_sem, beside).start()

        later = me + k * ny

        @pl.when(z + k < nz)
        def _():
            arrived(later)

            @pl.when(z > 0)
            def _():
                send(later, out_ref.at[later], down_sem, me - ny).start()

            send(later, out_ref.at[later], side_sem, beside).start()

    for other in range(nz):
        arrived(other * ny + (1 - y))
    own.wait()
    for other in range(nz):
        block = other * ny + y
        send(block, out_ref.at[block], side_sem, beside).wait_send()

        @pl.when(jnp.logical_and(other <= z, z < nz - 1))
        def _():
            send(block, out_ref.at[block], up_sem, me + ny).wait_send()

        @pl.when(jnp.logical_and(other >= z, z > 0))
        def _():
            send(block, out_ref.at[block], down_sem, me - ny).wait_send()


def gather_tokens(x_t):
    count = lax.axis_size("expert")
    nz, ny = grid_of(count)
    if ny != 2:
        return lax.all_gather(x_t, "expert", axis=0, tiled=False)
    sems = pltpu.SemaphoreType.DMA((count,))
    return pl.pallas_call(
        functools.partial(gather_kernel, nz),
        out_shape=jax.ShapeDtypeStruct((count,) + x_t.shape, x_t.dtype),
        in_specs=[pl.BlockSpec(memory_space=pl.ANY)],
        out_specs=pl.BlockSpec(memory_space=pl.ANY),
        scratch_shapes=[pltpu.SemaphoreType.DMA, sems, sems, sems, sems],
        compiler_params=pltpu.CompilerParams(collective_id=0, has_side_effects=True),
        cost_estimate=pl.CostEstimate(flops=10**11, bytes_accessed=3 * 10**8, transcendentals=0),
        name="gather_tokens",
    )(x_t)


def scatter_kernel(
    nz, y_hbm, out_ref, held, beside_in, below_in, above_in,
    load_sem, side_sem, side_recv, up_sem, up_recv, down_sem, down_recv,
):
    ny = 2
    me = lax.axis_index("expert")
    z, y = me // ny, lax.rem(me, ny)
    beside = z * ny + (1 - y)

    def load(target):
        return pltpu.make_async_copy(y_hbm.at[target * ny + y], held.at[target], load_sem.at[target])

    def side(target):
        return pltpu.make_async_remote_copy(
            src_ref=y_hbm.at[target * ny + (1 - y)], dst_ref=beside_in.at[target],
            send_sem=side_sem.at[target], recv_sem=side_recv.at[target],
            device_id={"expert": beside},
        )

    def up(target):
        return pltpu.make_async_remote_copy(
            src_ref=held.at[target], dst_ref=below_in.at[target], send_sem=up_sem.at[target],
            recv_sem=up_recv.at[target], device_id={"expert": me + ny},
        )

    def down(target):
        return pltpu.make_async_remote_copy(
            src_ref=held.at[target], dst_ref=above_in.at[target], send_sem=down_sem.at[target],
            recv_sem=down_recv.at[target], device_id={"expert": me - ny},
        )

    def add(target, ref):
        step = 512

        def body(i, carry):
            rows = pl.ds(pl.multiple_of(i * step, step), step)
            total = held[target, rows, :].astype(F32) + ref[target, rows, :].astype(F32)
            held[target, rows, :] = total.astype(BF16)
            return carry

        lax.fori_loop(0, D // step, body, 0)

    greet(z, y, nz, ny)
    for k in range(nz - 1, -1, -1):
        @pl.when(z + k < nz)
        def _():
            side(z + k).start()

        if k > 0:
            @pl.when(z - k >= 0)
            def _():
                side(z - k).start()

    for target in range(nz):
        load(target).start()
    for target in range(nz):
        load(target).wait()
    for k in range(nz - 1, 0, -1):
        target = z + k

        @pl.when(z + k < nz)
        def _():
            side(target).wait_recv()
            add(target, beside_in)

            @pl.when(z > 0)
            def _():
                up(target).wait_recv()
                add(target, below_in)

            up(target).start()

        lower = z - k

        @pl.when(z - k >= 0)
        def _():
            side(lower).wait_recv()
            add(lower, beside_in)

            @pl.when(z < nz - 1)
            def _():
                down(lower).wait_recv()
                add(lower, above_in)

            down(lower).start()

    side(z).wait_recv()
    add(z, beside_in)

    @pl.when(z > 0)
    def _():
        up(z).wait_recv()
        add(z, below_in)

    @pl.when(z < nz - 1)
    def _():
        down(z).wait_recv()
        add(z, above_in)

    out_ref[...] = held[z]
    for target in range(nz):
        side(target).wait_send()

        @pl.when(target > z)
        def _():
            up(target).wait_send()

        @pl.when(target < z)
        def _():
            down(target).wait_send()


def scatter_sums(sums):
    count = lax.axis_size("expert")
    nz, ny = grid_of(count)
    if ny != 2:
        return lax.psum_scatter(sums, "expert", scatter_dimension=0, tiled=False)
    block = pltpu.VMEM((nz,) + sums.shape[1:], sums.dtype)
    sems = pltpu.SemaphoreType.DMA((nz,))
    return pl.pallas_call(
        functools.partial(scatter_kernel, nz),
        out_shape=jax.ShapeDtypeStruct(sums.shape[1:], sums.dtype),
        in_specs=[pl.BlockSpec(memory_space=pl.ANY)],
        out_specs=pl.BlockSpec(memory_space=pltpu.VMEM),
        scratch_shapes=[block] * 4 + [sems] * 7,
        compiler_params=pltpu.CompilerParams(
            collective_id=1, has_side_effects=True, vmem_limit_bytes=40 * 2**20
        ),
        cost_estimate=pl.CostEstimate(flops=10**11, bytes_accessed=3 * 10**8, transcendentals=0),
        name="scatter_sums",
    )(sums)


ROWS = D + 16
CAP = 48
CHUNK = 1024
SPANS = ((0, 1024), (1024, 1024), (2048, 1024), (3072, ROWS - 3072))
PARTS = ((0, 0, 32), (1, 0, 16), (1, 16, 16), (2, 0, 16), (2, 16, 16), (3, 0, 32))


def dot(a, b):
    return jnp.dot(a, b, preferred_element_type=F32)


def dot_turned(w, x):
    return lax.dot_general(w, x, (((0,), (0,)), ((), ())), preferred_element_type=F32)


def gelu(hidden):
    return ((0.5 * hidden) * (1.0 + lax.erf(hidden * (0.5**0.5)))).astype(BF16)


def aligned(start, step):
    return pl.ds(pl.multiple_of(start, step), step)


def monarch_tiles(tiles, load, weights, z_ref, u_ref, store):
    w1, w2, w3, w4 = weights

    def spread(ref, rows, value):
        for i in range(tiles):
            ref[i, rows, :] = value[:, i * T : (i + 1) * T]

    def strided(ref, start):
        parts = [ref[i, pl.ds(start, NB, stride=NB), :].astype(BF16) for i in range(tiles)]
        return parts[0] if tiles == 1 else jnp.concatenate(parts, axis=1)

    def up(i, carry):
        for q in range(8):
            rows = aligned((i * 8 + q) * DB, DB)
            spread(z_ref, rows, dot_turned(w1[i * 8 + q], load(rows)))
        return carry

    lax.fori_loop(0, NB // 8, up, 0)
    batch = 8 if tiles == 1 else 4

    def middle(i, carry):
        blocks = [i * batch + q for q in range(batch)]
        hidden = [gelu(dot_turned(w2[j], strided(z_ref, j))) for j in blocks]
        for j, h in zip(blocks, hidden):
            spread(u_ref, aligned(j * NB, NB), dot(w3[j], h))
        return carry

    lax.fori_loop(0, NB // batch, middle, 0)

    def down(i, carry):
        for q in range(8):
            k = i * 8 + q
            store(aligned(k * DB, DB), dot_turned(w4[k], strided(u_ref, k)))
        return carry

    lax.fori_loop(0, NB // 8, down, 0)


def layer_kernel(
    x_hbm, r1, r2, r3, r4, s1, s2, s3, s4, out_ref,
    x_all, a1, a2, a3, a4, b1, b2, b3, b4, c1, c2, c3, c4,
    slots, z_ref, u_ref, hot, share, shared_out, core_in, y_in, z_in,
    local_sem, x_send, x_recv, b_send, b_recv, c_send, c_recv, sum_send, sum_recv,
):
    e, d = lax.axis_index("expert"), lax.axis_index("dp")
    z, y, x, c = e // 2, lax.rem(e, 2), d // 2, lax.rem(d, 2)
    near_z = e + 2 - 4 * lax.rem(z, 2)
    on_far = {"expert": lax.rem(e + 4, 8), "dp": d}
    on_near = {"expert": near_z, "dp": d}
    on_y = {"expert": e + 1 - 2 * y, "dp": d}
    on_core = {"expert": e, "dp": d + 1 - 2 * c}
    on_x = {"expert": e, "dp": lax.rem(d + 2, 4)}
    own_a, own_b, own_s = (a1, a2, a3, a4), (b1, b2, b3, b4), (c1, c2, c3, c4)
    routed = (r1.at[c], r2.at[c], r3, r4.at[c])
    shared = (s1, s2, s3, s4)

    def remote(src, dst, send, recv, target):
        return pltpu.make_async_remote_copy(
            src_ref=src, dst_ref=dst, send_sem=send, recv_sem=recv, device_id=target
        )

    def x_copy(number, src, slot, rows, target):
        return remote(
            src.at[rows], x_all.at[slot, rows], x_send.at[number], x_recv.at[number], target
        )

    whole = pl.ds(0, ROWS)
    spans = [pl.ds(*s) for s in SPANS]
    x_core = x_copy(0, x_hbm, 1, whole, on_core)
    x_y = x_copy(1, x_hbm, 2, whole, on_y)
    x_far = [x_copy(2 + i, x_hbm, 4, rows, on_far) for i, rows in enumerate(spans)]
    x_y_core = x_copy(6, x_all.at[2], 3, whole, on_core)
    x_far_core = [x_copy(7 + i, x_all.at[4], 5, rows, on_core) for i, rows in enumerate(spans)]
    x_far_y = [x_copy(11 + i, x_all.at[4], 6, rows, on_y) for i, rows in enumerate(spans)]
    x_last = [x_copy(15 + i, x_all.at[6], 7, rows, on_core) for i, rows in enumerate(spans)]

    def b_copy(number, part, mine, first):
        w, start, size = PARTS[part]
        half = x if mine else 1 - x
        rows = pl.ds(half * 32 + start, size)
        src = routed[w] if first else own_b[w]
        return remote(
            src.at[rows], own_b[w].at[rows], b_send.at[number], b_recv.at[number],
            on_near if first else on_x,
        )

    def quarter(src, w, rows, number, target):
        return remote(src.at[rows[0]], own_s[w].at[rows[1]], c_send.at[number], c_recv.at[number], target)

    mine, theirs = pl.ds(d * 16, 16), pl.ds(lax.rem(d + 2, 4) * 16, 16)
    all16 = pl.ds(0, 16)
    c_core = [quarter(shared[w], w, (all16, mine), w, on_core) for w in range(4)]
    c_x = [quarter(shared[w], w, (all16, mine), 4 + w, on_x) for w in range(4)]
    c_fwd = [quarter(own_s[w], w, (theirs, theirs), 8 + w, on_core) for w in range(4)]

    barrier = pltpu.get_barrier_semaphore()
    for target in (on_far, on_near, on_y, on_core, on_x):
        pl.semaphore_signal(barrier, inc=1, device_id=target)
    pl.semaphore_wait(barrier, 5)

    x_own = pltpu.make_async_copy(x_hbm, x_all.at[0], local_sem.at[0])
    a_own = [pltpu.make_async_copy(routed[w], own_a[w], local_sem.at[1 + w]) for w in range(4)]
    c_own = [pltpu.make_async_copy(shared[w], own_s[w].at[mine], local_sem.at[5 + w]) for w in range(4)]
    x_y.start()
    for copy in x_far:
        copy.start()
    x_core.start()
    b_near = [b_copy(p, p, True, True) for p in range(len(PARTS))]
    b_x = [b_copy(6 + p, p, True, False) for p in range(len(PARTS))]
    b_there = [b_copy(6 + p, p, False, False) for p in range(len(PARTS))]
    for copy in b_near:
        copy.start()
    for copy in c_x + c_core:
        copy.start()
    x_own.start()
    for copy in a_own + c_own:
        copy.start()

    ids_a = (2 * e + c).astype(F32)
    ids_b = (2 * near_z + c).astype(F32)

    def prepare(q):
        extra = jnp.concatenate(
            [x_all[2 * q, D:ROWS, :].astype(F32), x_all[2 * q + 1, D:ROWS, :].astype(F32)], axis=1
        )
        id0, id1, code0, code1 = (extra[i : i + 1] for i in range(4))
        lane = lax.broadcasted_iota(jnp.int32, (1, 2 * T), 1)
        before = lax.broadcasted_iota(jnp.int32, (2 * T, 2 * T), 0)
        after = lax.broadcasted_iota(jnp.int32, (2 * T, 2 * T), 1)
        tri = jnp.logical_and(before < after, (before < T) == (after < T))
        tri = tri.astype(F32).astype(BF16)
        row8 = lax.broadcasted_iota(jnp.int32, (8, 2 * T), 0)
        picks = [jnp.logical_or(id0 == n, id1 == n) for n in (ids_a, ids_b)]
        names = [jnp.where(p, 1.0, 0.0) for p in picks]
        codes = [jnp.where(id0 == n, code0, code1) for n in (ids_a, ids_b)]
        stacked = jnp.where(row8 == 0, names[0], jnp.where(row8 == 1, names[1], 0.0))
        ranks = dot(stacked.astype(BF16), tri)
        base = jnp.where(lane < T, 2 * q * CAP, (2 * q + 1) * CAP).astype(F32)
        places = [
            jnp.where(picks[n], ranks[n : n + 1] + base, -1000.0).astype(jnp.int32) for n in range(2)
        ]
        for tile, half in ((q, 0), (q - 1, 1)):
            if not 0 <= tile < 3:
                continue
            wanted = lax.broadcasted_iota(jnp.int32, (T, 2 * T), 0) + tile * T
            for n in range(2):
                own = (wanted == places[n]).astype(F32).astype(BF16)
                hot[tile, half, n * T : (n + 1) * T, :] = own
                values = jnp.where(
                    row8 == 0, codes[n], jnp.where(row8 == 1, code0, jnp.where(row8 == 2, code1, 0.0))
                )
                got = lax.dot_general(
                    values.astype(BF16), own, (((1,), (1,)), ((), ())), preferred_element_type=F32
                )
                if half == 0:
                    share[n, tile] = got
                else:
                    share[n, tile] += got

    def pick(tile):
        def some(i, carry):
            rows = aligned(i * 256, 256)
            total = None
            for half in range(2):
                q = tile + half
                both = jnp.concatenate([x_all[2 * q, rows, :], x_all[2 * q + 1, rows, :]], axis=1)
                got = lax.dot_general(
                    both, hot[tile, half], (((1,), (1,)), ((), ())), preferred_element_type=F32
                )
                total = got if total is None else total + got
            total = total.astype(BF16)
            slots[0, tile, rows, :] = total[:, :T]
            slots[1, tile, rows, :] = total[:, T:]
            return carry

        lax.fori_loop(0, D // 256, some, 0)

    def serve(n, first, count, weights):
        gates = []
        for i in range(count):
            got = share[n, first + i]
            under = got[1:2] + got[2:3]
            gates.append(jnp.where(under > 0.0, got[0:1] / jnp.maximum(under, 1.0), 0.0))
        gates = [jnp.broadcast_to(g, (DB, T)) for g in gates]

        def load(rows):
            parts = [slots[n, first + i, rows, :] for i in range(count)]
            return parts[0] if count == 1 else jnp.concatenate(parts, axis=1)

        def store(rows, value):
            for i in range(count):
                slots[n, first + i, rows, :] = (value[:, i * T : (i + 1) * T] * gates[i]).astype(BF16)

        monarch_tiles(count, load, weights, z_ref, u_ref, store)

    def forward(i):
        x_far[i].wait_recv()
        x_far_y[i].start()
        x_far_core[i].start()

    x_own.wait()
    x_core.wait_recv()
    prepare(0)
    x_y.wait_recv()
    x_y_core.start()
    forward(0)
    forward(1)
    x_y_core.wait_recv()
    prepare(1)
    pick(0)
    for copy in a_own:
        copy.wait()
    forward(2)
    for copy in c_x:
        copy.wait_recv()
    for copy in c_fwd:
        copy.start()
    for i in (0, 1):
        b_near[i].wait_recv()
        b_x[i].start()
    serve(0, 0, 1, own_a)
    forward(3)
    for i in (2, 3):
        b_near[i].wait_recv()
        b_x[i].start()
    for i in range(4):
        x_far_y[i].wait_recv()
        x_last[i].start()
    for copy in x_far_core:
        copy.wait_recv()
    prepare(2)
    for copy in x_last:
        copy.wait_recv()
    prepare(3)
    pick(1)
    pick(2)
    for i in (4, 5):
        b_near[i].wait_recv()
        b_x[i].start()
    serve(0, 1, 2, own_a)
    for copy in c_own:
        copy.wait()
    for copy in c_core + c_fwd:
        copy.wait_recv()

    def keep_shared(rows, value):
        shared_out[rows, :] = value.astype(BF16)

    monarch_tiles(1, lambda rows: x_all[0, rows, :], own_s, z_ref, u_ref, keep_shared)
    for copy in b_there:
        copy.wait_recv()
    serve(1, 0, 3, own_b)

    for copy in [x_core, x_y, x_y_core] + x_far + x_far_core + x_far_y + x_last:
        copy.wait_send()

    def sum_copy(number, src, dst, i, target):
        rows = pl.ds(i * CHUNK, CHUNK)
        return remote(
            src.at[rows], dst.at[rows], sum_send.at[number * 4 + i], sum_recv.at[number * 4 + i], target
        )

    chunks = range(D // CHUNK)
    to_core = [[sum_copy(q, x_all.at[2 * q + 1], core_in.at[q], i, on_core) for i in chunks] for q in range(4)]
    to_y = {q: [sum_copy(4 + q // 2, x_all.at[2 * q], y_in.at[q // 2], i, on_y) for i in chunks] for q in (1, 3)}
    to_far = [sum_copy(6, x_all.at[4], z_in, i, on_far) for i in chunks]

    def combine(q, i):
        where = [(tile, half) for tile, half in ((q, 0), (q - 1, 1)) if 0 <= tile < 3]

        def some(j, carry):
            rows = aligned(i * CHUNK + j * 256, 256)
            total = None
            for tile, half in where:
                both = jnp.concatenate([slots[0, tile, rows, :], slots[1, tile, rows, :]], axis=1)
                got = dot(both, hot[tile, half])
                total = got if total is None else total + got
            total = total.astype(BF16)
            x_all[2 * q, rows, :] = total[:, :T]
            x_all[2 * q + 1, rows, :] = total[:, T:]
            return carry

        lax.fori_loop(0, CHUNK // 256, some, 0)

    def add(q, ref, i):
        def some(j, carry):
            rows = aligned(i * CHUNK + j * 256, 256)
            total = x_all[2 * q, rows, :].astype(F32) + ref[rows, :].astype(F32)
            x_all[2 * q, rows, :] = total.astype(BF16)
            return carry

        lax.fori_loop(0, CHUNK // 256, some, 0)

    for i in chunks:
        combine(3, i)
        to_core[3][i].start()
    for i in chunks:
        combine(2, i)
        to_core[2][i].start()
        to_core[3][i].wait_recv()
        add(3, core_in.at[3], i)
        to_y[3][i].start()
    for i in chunks:
        to_core[2][i].wait_recv()
        add(2, core_in.at[2], i)
    for i in chunks:
        combine(1, i)
        to_core[1][i].start()
        to_y[3][i].wait_recv()
        add(2, y_in.at[1], i)
        to_far[i].start()
    for i in chunks:
        to_core[1][i].wait_recv()
        add(1, core_in.at[1], i)
        to_y[1][i].start()
        combine(0, i)
        to_core[0][i].start()
    for i in chunks:
        to_core[0][i].wait_recv()
        to_y[1][i].wait_recv()
        to_far[i].wait_recv()

        def last(j, carry):
            rows = aligned(i * CHUNK + j * 256, 256)
            total = x_all[0, rows, :].astype(F32) + shared_out[rows, :].astype(F32)
            total += core_in[0, rows, :].astype(F32) + y_in[0, rows, :].astype(F32)
            out_ref[rows, :] = (total + z_in[rows, :].astype(F32)).astype(BF16)
            return carry

        lax.fori_loop(0, CHUNK // 256, last, 0)

    for copy in b_near + b_x + c_core + c_x + c_fwd:
        copy.wait_send()
    for copies in to_core + [to_y[1], to_y[3], to_far]:
        for copy in copies:
            copy.wait_send()


def layer_call(x_t, routed, shared):
    hbm = pl.BlockSpec(memory_space=pl.ANY)
    weights = [
        pltpu.VMEM((NB, DB, NB), BF16), pltpu.VMEM((NB, NB, HB), BF16),
        pltpu.VMEM((NB, NB, HB), BF16), pltpu.VMEM((NB, NB, DB), BF16),
    ]
    sems = pltpu.SemaphoreType.DMA
    block = pltpu.VMEM((D, T), BF16)
    return pl.pallas_call(
        layer_kernel,
        out_shape=jax.ShapeDtypeStruct((D, T), BF16),
        in_specs=[hbm] * 9,
        out_specs=pl.BlockSpec(memory_space=pltpu.VMEM),
        scratch_shapes=[pltpu.VMEM((8, ROWS, T), BF16)]
        + weights * 3
        + [
            pltpu.VMEM((2, 3, D, T), BF16),
            pltpu.VMEM((3, D, T), F32),
            pltpu.VMEM((3, D, T), F32),
            pltpu.VMEM((3, 2, 2 * T, 2 * T), BF16),
            pltpu.VMEM((2, 3, 8, T), F32),
            block,
            pltpu.VMEM((4, D, T), BF16),
            pltpu.VMEM((2, D, T), BF16),
            block,
            sems((9,)), sems((19,)), sems((19,)), sems((12,)), sems((12,)),
            sems((12,)), sems((12,)), sems((28,)), sems((28,)),
        ],
        compiler_params=pltpu.CompilerParams(
            collective_id=2, has_side_effects=True, vmem_limit_bytes=62 * 2**20
        ),
        cost_estimate=pl.CostEstimate(flops=10**11, bytes_accessed=3 * 10**8, transcendentals=0),
        name="layer",
    )(x_t, *routed, *shared)


def cube_layer(tokens, expert_ids, gate_codes, shared, routed):
    extra = jnp.concatenate([expert_ids, gate_codes], axis=1).T.astype(BF16)
    extra = jnp.pad(extra, ((0, ROWS - D - extra.shape[0]), (0, 0)))
    x_t = jnp.concatenate([tokens.T, extra], axis=0)
    core = lax.rem(lax.axis_index("dp"), 2)
    third = lax.dynamic_index_in_dim(routed[2], core, 0, keepdims=False)
    own = (routed[0], routed[1], jnp.swapaxes(third, -1, -2), routed[3])
    everyone = (shared[0], shared[1], jnp.swapaxes(shared[2], -1, -2), shared[3])
    return layer_call(x_t, own, everyone).T


def running(ones, width):
    groups = ones.reshape(ones.shape[0], -1, width).astype(F32)
    inside = jnp.einsum("rgt,tu->rgu", groups, jnp.triu(jnp.ones((width, width), F32)))
    count = groups.shape[1]
    earlier = jnp.triu(jnp.ones((count, count), F32), 1)
    before = jnp.einsum("rg,gh->rh", inside[:, :, -1], earlier, precision=lax.Precision.HIGHEST)
    return (inside + before[:, :, None]).reshape(ones.shape).astype(jnp.int32)


def shards(tokens, expert_ids, gate_codes, *factors):
    shared, routed = factors[:4], factors[4:]
    residents = routed[0].shape[0]
    sources = lax.axis_size("expert")
    tok_rows = tokens.shape[0]
    if sources == 8 and lax.axis_size("dp") == 4 and residents == 2:
        return cube_layer(tokens, expert_ids, gate_codes, shared, routed)
    experts_all = residents * sources
    capacity = max(2, 6 * tok_rows // experts_all)
    tiles = -(-sources * capacity // (2 * T))
    depth = tiles * 2 * T
    window = min(depth, -(-(T - 1 + 2 * capacity) // T) * T)

    extra = jnp.concatenate([expert_ids, gate_codes], axis=1).T.astype(BF16)
    extra = jnp.pad(extra, ((0, 16 - extra.shape[0]), (0, 0)))
    x_t = jnp.concatenate([tokens.T, extra], axis=0)
    x_all = gather_tokens(x_t)
    ids_all = x_all[:, D : D + 2].astype(jnp.int32)
    codes = x_all[:, D + 2 : D + 4].astype(F32)
    gates_all = codes / jnp.sum(codes, axis=1, keepdims=True)
    mine = lax.axis_index("expert") * residents + jnp.arange(residents, dtype=jnp.int32)
    match = ids_all[None] == mine[:, None, None, None]
    picked = jnp.any(match, axis=2).reshape(residents, sources * tok_rows)
    gate = jnp.sum(jnp.where(match, gates_all[None], 0.0), axis=2).reshape(residents, sources * tok_rows)
    ones = picked.astype(jnp.int32)
    ranks = running(ones, tok_rows)
    counts = ranks[:, -1]
    starts = (ranks - ones).reshape(residents, sources // 2, 2 * T)[:, :, 0]
    starts = jnp.minimum(starts, depth - window) // T
    pos = jnp.where(picked, ranks - 1, -1)
    slots = jnp.arange(depth, dtype=jnp.int32)
    slot_gates = jnp.sum(
        jnp.where(pos[:, None, :] == slots[None, :, None], gate[:, None, :], 0.0), axis=2
    ).reshape(residents, tiles, 1, 2 * T)
    pos = pos.reshape(residents, sources // 2, 1, 2 * T)

    outs = routed_call(counts, pos, slot_gates, x_all, turned(routed), tiles)
    y = combine_call(starts, pos, outs, sources, depth, window)
    sums = scatter_sums(y)
    whole = tuple(lax.all_gather(w, "dp", axis=0, tiled=True)[None] for w in turned(shared))
    shared_t = shared_call(x_t, whole)
    total = shared_t.astype(F32) + sums.astype(F32)
    return total.astype(BF16).T


def solution(mesh):
    in_specs = (
        P(("expert", "dp"), None),
        P(("expert", "dp"), None),
        P(("expert", "dp"), None),
        P("dp", None, None),
        P("dp", None, None),
        P("dp", None, None),
        P("dp", None, None),
        P("expert", None, None, None),
        P("expert", None, None, None),
        P("expert", None, None, None),
        P("expert", None, None, None),
    )
    out_specs = P(("expert", "dp"), None)
    return jax.shard_map(shards, mesh=mesh, in_specs=in_specs, out_specs=out_specs, check_vma=False)
```

```python
import functools
import math

import jax
import jax.numpy as jnp
from jax import lax
from jax.experimental import pallas as pl
from jax.experimental.pallas import tpu as pltpu
from jax.sharding import PartitionSpec as P

D = 4096
NB = 64
DB = 64
HB = 256
T = 128
F32 = jnp.float32
BF16 = jnp.bfloat16


def tile_monarch(x_ref, lanes, w1_ref, w2_ref, w3_ref, w4_ref, z_refs, u_refs, store):
    def spread(refs, rows, value):
        for i in range(lanes):
            refs[i][rows, :] = value[:, i * T : (i + 1) * T]

    def strided(refs, start):
        parts = [refs[i][pl.ds(start, NB, stride=NB), :] for i in range(lanes)]
        return jnp.concatenate(parts, axis=1).astype(BF16)

    def up(a, carry):
        rows = pl.ds(pl.multiple_of(a * DB, DB), DB)
        x = x_ref[rows, : lanes * T]
        spread(z_refs, rows, jnp.dot(w1_ref[0, a], x, preferred_element_type=F32))
        return carry

    lax.fori_loop(0, NB, up, 0, unroll=8)

    def middle(j, carry):
        hidden = jnp.dot(w2_ref[0, j], strided(z_refs, j), preferred_element_type=F32)
        hidden = (0.5 * hidden) * (1.0 + lax.erf(hidden * (0.5**0.5)))
        u = jnp.dot(w3_ref[0, j], hidden.astype(BF16), preferred_element_type=F32)
        spread(u_refs, pl.ds(pl.multiple_of(j * NB, NB), NB), u)
        return carry

    lax.fori_loop(0, NB, middle, 0, unroll=4)

    def down(k, carry):
        rows = pl.ds(pl.multiple_of(k * DB, DB), DB)
        store(rows, jnp.dot(w4_ref[0, k], strided(u_refs, k), preferred_element_type=F32))
        return carry

    lax.fori_loop(0, NB, down, 0, unroll=8)


def shared_kernel(x_ref, w1_ref, w2_ref, w3_ref, w4_ref, o_ref, z_ref, u_ref):
    def store(rows, value):
        o_ref[rows, :] = value.astype(BF16)

    tile_monarch(x_ref, 1, w1_ref, w2_ref, w3_ref, w4_ref, (z_ref,), (u_ref,), store)


def routed_kernel(
    counts_ref, pos_ref, gate_ref, x_ref, w1_ref, w2_ref, w3_ref, w4_ref,
    o_ref, x_scr, z0_ref, z1_ref, u0_ref, u1_ref,
):
    expert, tile = pl.program_id(0), pl.program_id(1)
    left = counts_ref[expert] - tile * 2 * T
    sources = x_ref.shape[0]

    @pl.when(left <= T)
    def _():
        o_ref[...] = jnp.zeros_like(o_ref)

    def serve(lanes):
        width = lanes * T
        wanted = lax.broadcasted_iota(jnp.int32, (width, 2 * T), 0) + tile * 2 * T
        step = D // 8

        for part in range(8):
            rows = pl.ds(part * step, step)

            def pick(pair, total):
                both = jnp.concatenate([x_ref[2 * pair, rows, :], x_ref[2 * pair + 1, rows, :]], axis=1)
                onehot = (wanted == pos_ref[0, pair, :, :]).astype(F32).astype(BF16)
                return total + lax.dot_general(
                    both, onehot, (((1,), (1,)), ((), ())), preferred_element_type=F32
                )

            total = lax.fori_loop(0, sources // 2, pick, jnp.zeros((step, width), F32))
            x_scr[rows, :width] = total.astype(BF16)

        gate = gate_ref[0, 0][:, :width]

        def store(rows, value):
            o_ref[rows, :width] = (value * gate).astype(BF16)

        tile_monarch(
            x_scr, lanes, w1_ref, w2_ref, w3_ref, w4_ref, (z0_ref, z1_ref), (u0_ref, u1_ref), store
        )

    @pl.when(left > T)
    def _():
        serve(2)

    @pl.when(jnp.logical_and(left > 0, left <= T))
    def _():
        serve(1)


def weight_specs(index_map, buffers=2):
    shapes = ((NB, DB), (HB, NB), (NB, HB), (DB, NB))
    mode = pl.Buffered(buffers)
    return [pl.BlockSpec((1, NB) + shape, index_map, pipeline_mode=mode) for shape in shapes]


def turned(factors):
    return tuple(jnp.swapaxes(w, -1, -2) for w in factors)


def shared_call(x_t, factors):
    return pl.pallas_call(
        shared_kernel,
        out_shape=jax.ShapeDtypeStruct((D, T), BF16),
        grid=(1,),
        in_specs=[pl.BlockSpec((D, T), lambda i: (0, 0))] + weight_specs(lambda i: (0, 0, 0, 0)),
        out_specs=pl.BlockSpec((D, T), lambda i: (0, 0)),
        scratch_shapes=[pltpu.VMEM((D, T), F32), pltpu.VMEM((D, T), F32)],
        compiler_params=pltpu.CompilerParams(vmem_limit_bytes=56 * 2**20),
        cost_estimate=pl.CostEstimate(flops=10**10, bytes_accessed=10**7, transcendentals=0),
        name="shared_expert",
    )(x_t, *factors)


def routed_call(counts, pos, slot_gates, x_all, factors, tiles):
    residents = pos.shape[0]
    sources = x_all.shape[0]
    grid_spec = pltpu.PrefetchScalarGridSpec(
        num_scalar_prefetch=1,
        grid=(residents, tiles),
        in_specs=[
            pl.BlockSpec((1, sources // 2, 1, 2 * T), lambda e, i, c: (e, 0, 0, 0)),
            pl.BlockSpec((1, 1, 1, 2 * T), lambda e, i, c: (e, i, 0, 0)),
            pl.BlockSpec((sources, x_all.shape[1], T), lambda e, i, c: (0, 0, 0), pipeline_mode=pl.Buffered(1)),
        ]
        + weight_specs(lambda e, i, c: (e, 0, 0, 0), 2 if sources <= 8 else 1),
        out_specs=pl.BlockSpec((D, 2 * T), lambda e, i, c: (0, e * tiles + i)),
        scratch_shapes=[pltpu.VMEM((D, 2 * T), BF16)] + [pltpu.VMEM((D, T), F32)] * 4,
    )
    return pl.pallas_call(
        routed_kernel,
        out_shape=jax.ShapeDtypeStruct((D, residents * tiles * 2 * T), BF16),
        grid_spec=grid_spec,
        compiler_params=pltpu.CompilerParams(vmem_limit_bytes=62 * 2**20),
        cost_estimate=pl.CostEstimate(flops=4 * 10**10, bytes_accessed=2 * 10**7, transcendentals=0),
        name="routed_experts",
    )(counts, pos, slot_gates, x_all, *factors)


def combine_kernel(depth, window, starts_ref, pos_ref, o_ref, y_ref):
    residents = starts_ref.shape[0]
    pair = pl.program_id(0)
    wanted = lax.broadcasted_iota(jnp.int32, (window, 2 * T), 0)
    begins = [pl.multiple_of(starts_ref[e, pair] * T, T) for e in range(residents)]
    hots = [
        (wanted + begins[e] == pos_ref[e, 0, :, :]).astype(F32).astype(BF16) for e in range(residents)
    ]
    hot = jnp.concatenate(hots, axis=0)
    step = 512

    def part(i, carry):
        rows = pl.ds(pl.multiple_of(i * step, step), step)
        near = [
            o_ref[rows, pl.ds(pl.multiple_of(begins[e] + e * depth, T), window)] for e in range(residents)
        ]
        total = jnp.dot(jnp.concatenate(near, axis=1), hot, preferred_element_type=F32).astype(BF16)
        y_ref[0, rows, :] = total[:, :T]
        y_ref[1, rows, :] = total[:, T:]
        return carry

    lax.fori_loop(0, D // step, part, 0)


def combine_call(starts, pos, outs, sources, depth, window):
    residents = pos.shape[0]
    grid_spec = pltpu.PrefetchScalarGridSpec(
        num_scalar_prefetch=1,
        grid=(sources // 2,),
        in_specs=[
            pl.BlockSpec((residents, 1, 1, 2 * T), lambda s, c: (0, s, 0, 0)),
            pl.BlockSpec((D, residents * depth), lambda s, c: (0, 0), pipeline_mode=pl.Buffered(1)),
        ],
        out_specs=pl.BlockSpec((2, D, T), lambda s, c: (s, 0, 0)),
    )
    return pl.pallas_call(
        functools.partial(combine_kernel, depth, window),
        out_shape=jax.ShapeDtypeStruct((sources, D, T), BF16),
        grid_spec=grid_spec,
        compiler_params=pltpu.CompilerParams(vmem_limit_bytes=48 * 2**20),
        name="combine",
    )(starts, pos, outs)


def grid_of(count):
    side = math.isqrt(count // 2)
    return count // side, side


def greet(z, y, nz, ny):
    barrier = pltpu.get_barrier_semaphore()
    for other in range(1, ny):
        pl.semaphore_signal(barrier, inc=1, device_id={"expert": z * ny + lax.rem(y + other, ny)})

    @pl.when(z > 0)
    def _():
        pl.semaphore_signal(barrier, inc=1, device_id={"expert": (z - 1) * ny + y})

    @pl.when(z < nz - 1)
    def _():
        pl.semaphore_signal(barrier, inc=1, device_id={"expert": (z + 1) * ny + y})

    peers = ny - 1 + jnp.where(z > 0, 1, 0) + jnp.where(z < nz - 1, 1, 0)
    pl.semaphore_wait(barrier, peers)


def gather_kernel(nz, x_ref, out_ref, own_sem, up_sem, down_sem, side_sem, recv_sem):
    ny = 2
    me = lax.axis_index("expert")
    z, y = me // ny, lax.rem(me, ny)
    beside = z * ny + (1 - y)

    def send(block, src, sem, target):
        return pltpu.make_async_remote_copy(
            src_ref=src, dst_ref=out_ref.at[block], send_sem=sem.at[block],
            recv_sem=recv_sem.at[block], device_id={"expert": target},
        )

    def arrived(block):
        send(block, out_ref.at[block], side_sem, beside).wait_recv()

    greet(z, y, nz, ny)
    own = pltpu.make_async_copy(x_ref, out_ref.at[me], own_sem)
    own.start()

    @pl.when(z < nz - 1)
    def _():
        send(me, x_ref, up_sem, me + ny).start()

    @pl.when(z > 0)
    def _():
        send(me, x_ref, down_sem, me - ny).start()

    send(me, x_ref, side_sem, beside).start()

    for k in range(1, nz):
        block = me - k * ny

        @pl.when(z >= k)
        def _():
            arrived(block)

            @pl.when(z < nz - 1)
            def _():
                send(block, out_ref.at[block], up_sem, me + ny).start()

            send(block, out_ref.at[block], side_sem, beside).start()

        later = me + k * ny

        @pl.when(z + k < nz)
        def _():
            arrived(later)

            @pl.when(z > 0)
            def _():
                send(later, out_ref.at[later], down_sem, me - ny).start()

            send(later, out_ref.at[later], side_sem, beside).start()

    for other in range(nz):
        arrived(other * ny + (1 - y))
    own.wait()
    for other in range(nz):
        block = other * ny + y
        send(block, out_ref.at[block], side_sem, beside).wait_send()

        @pl.when(jnp.logical_and(other <= z, z < nz - 1))
        def _():
            send(block, out_ref.at[block], up_sem, me + ny).wait_send()

        @pl.when(jnp.logical_and(other >= z, z > 0))
        def _():
            send(block, out_ref.at[block], down_sem, me - ny).wait_send()


def gather_tokens(x_t):
    count = lax.axis_size("expert")
    nz, ny = grid_of(count)
    if ny != 2:
        return lax.all_gather(x_t, "expert", axis=0, tiled=False)
    sems = pltpu.SemaphoreType.DMA((count,))
    return pl.pallas_call(
        functools.partial(gather_kernel, nz),
        out_shape=jax.ShapeDtypeStruct((count,) + x_t.shape, x_t.dtype),
        in_specs=[pl.BlockSpec(memory_space=pl.ANY)],
        out_specs=pl.BlockSpec(memory_space=pl.ANY),
        scratch_shapes=[pltpu.SemaphoreType.DMA, sems, sems, sems, sems],
        compiler_params=pltpu.CompilerParams(collective_id=0, has_side_effects=True),
        cost_estimate=pl.CostEstimate(flops=10**11, bytes_accessed=3 * 10**8, transcendentals=0),
        name="gather_tokens",
    )(x_t)


def scatter_kernel(
    nz, y_hbm, out_ref, held, beside_in, below_in, above_in,
    load_sem, side_sem, side_recv, up_sem, up_recv, down_sem, down_recv,
):
    ny = 2
    me = lax.axis_index("expert")
    z, y = me // ny, lax.rem(me, ny)
    beside = z * ny + (1 - y)

    def load(target):
        return pltpu.make_async_copy(y_hbm.at[target * ny + y], held.at[target], load_sem.at[target])

    def side(target):
        return pltpu.make_async_remote_copy(
            src_ref=y_hbm.at[target * ny + (1 - y)], dst_ref=beside_in.at[target],
            send_sem=side_sem.at[target], recv_sem=side_recv.at[target],
            device_id={"expert": beside},
        )

    def up(target):
        return pltpu.make_async_remote_copy(
            src_ref=held.at[target], dst_ref=below_in.at[target], send_sem=up_sem.at[target],
            recv_sem=up_recv.at[target], device_id={"expert": me + ny},
        )

    def down(target):
        return pltpu.make_async_remote_copy(
            src_ref=held.at[target], dst_ref=above_in.at[target], send_sem=down_sem.at[target],
            recv_sem=down_recv.at[target], device_id={"expert": me - ny},
        )

    def add(target, ref):
        step = 512

        def body(i, carry):
            rows = pl.ds(pl.multiple_of(i * step, step), step)
            total = held[target, rows, :].astype(F32) + ref[target, rows, :].astype(F32)
            held[target, rows, :] = total.astype(BF16)
            return carry

        lax.fori_loop(0, D // step, body, 0)

    greet(z, y, nz, ny)
    for k in range(nz - 1, -1, -1):
        @pl.when(z + k < nz)
        def _():
            side(z + k).start()

        if k > 0:
            @pl.when(z - k >= 0)
            def _():
                side(z - k).start()

    for target in range(nz):
        load(target).start()
    for target in range(nz):
        load(target).wait()
    for k in range(nz - 1, 0, -1):
        target = z + k

        @pl.when(z + k < nz)
        def _():
            side(target).wait_recv()
            add(target, beside_in)

            @pl.when(z > 0)
            def _():
                up(target).wait_recv()
                add(target, below_in)

            up(target).start()

        lower = z - k

        @pl.when(z - k >= 0)
        def _():
            side(lower).wait_recv()
            add(lower, beside_in)

            @pl.when(z < nz - 1)
            def _():
                down(lower).wait_recv()
                add(lower, above_in)

            down(lower).start()

    side(z).wait_recv()
    add(z, beside_in)

    @pl.when(z > 0)
    def _():
        up(z).wait_recv()
        add(z, below_in)

    @pl.when(z < nz - 1)
    def _():
        down(z).wait_recv()
        add(z, above_in)

    out_ref[...] = held[z]
    for target in range(nz):
        side(target).wait_send()

        @pl.when(target > z)
        def _():
            up(target).wait_send()

        @pl.when(target < z)
        def _():
            down(target).wait_send()


def scatter_sums(sums):
    count = lax.axis_size("expert")
    nz, ny = grid_of(count)
    if ny != 2:
        return lax.psum_scatter(sums, "expert", scatter_dimension=0, tiled=False)
    block = pltpu.VMEM((nz,) + sums.shape[1:], sums.dtype)
    sems = pltpu.SemaphoreType.DMA((nz,))
    return pl.pallas_call(
        functools.partial(scatter_kernel, nz),
        out_shape=jax.ShapeDtypeStruct(sums.shape[1:], sums.dtype),
        in_specs=[pl.BlockSpec(memory_space=pl.ANY)],
        out_specs=pl.BlockSpec(memory_space=pltpu.VMEM),
        scratch_shapes=[block] * 4 + [sems] * 7,
        compiler_params=pltpu.CompilerParams(
            collective_id=1, has_side_effects=True, vmem_limit_bytes=40 * 2**20
        ),
        cost_estimate=pl.CostEstimate(flops=10**11, bytes_accessed=3 * 10**8, transcendentals=0),
        name="scatter_sums",
    )(sums)


ROWS = D + 16
CAP = 48
CHUNK = 1024
SPANS = ((0, 1024), (1024, 1024), (2048, 1024), (3072, ROWS - 3072))
LEGS = ((0, 0, 16), (3, 0, 16)) + tuple((w, 8 * i, 8) for i in range(4) for w in (1, 2))


def dot(a, b):
    return jnp.dot(a, b, preferred_element_type=F32)


def dot_turned(w, x):
    return lax.dot_general(w, x, (((0,), (0,)), ((), ())), preferred_element_type=F32)


def gelu(hidden):
    return ((0.5 * hidden) * (1.0 + lax.erf(hidden * (0.5**0.5)))).astype(BF16)


def aligned(start, step):
    return pl.ds(pl.multiple_of(start, step), step)


def apart(upper, lower):
    top, bottom = [], []
    for a, b in zip(upper, lower):
        top += [a, jnp.zeros_like(a)]
        bottom += [jnp.zeros_like(b), b]
    return jnp.concatenate([jnp.concatenate(top, axis=1), jnp.concatenate(bottom, axis=1)], axis=0)


def strided(ref, tiles, start):
    return [ref[i, pl.ds(start, NB, stride=NB), :].astype(BF16) for i in range(tiles)]


def up(tiles, load, w1, z_ref):
    def some(i, carry):
        for q in range(4):
            p = i * 4 + q
            parts = load(aligned(p * 2 * DB, 2 * DB))
            value = dot(w1[p], apart([x[:DB] for x in parts], [x[DB:] for x in parts]))
            for t in range(tiles):
                for side in range(2):
                    at = 2 * t + side
                    z_ref[t, aligned((2 * p + side) * DB, DB), :] = value[:, at * T : (at + 1) * T]
        return carry

    lax.fori_loop(0, NB // 8, some, 0)


def middle(tiles, w2, w3, z_ref, u_ref, first, count):
    batch = 8 if tiles == 1 else 4

    def some(i, carry):
        blocks = [first + i * batch + q for q in range(batch)]
        hidden = []
        for j in blocks:
            parts = strided(z_ref, tiles, j)
            rows = parts[0] if tiles == 1 else jnp.concatenate(parts, axis=1)
            hidden.append(gelu(dot_turned(w2[j], rows)))
        for j, h in zip(blocks, hidden):
            value = dot(w3[j], h)
            for t in range(tiles):
                u_ref[t, aligned(j * NB, NB), :] = value[:, t * T : (t + 1) * T]
        return carry

    lax.fori_loop(0, count // batch, some, 0)


def down(tiles, w4, u_ref, store, first, count):
    def some(i, carry):
        for q in range(4):
            p = first + i * 4 + q
            value = dot(w4[p], apart(strided(u_ref, tiles, 2 * p), strided(u_ref, tiles, 2 * p + 1)))
            for side in range(2):
                parts = [value[:, (2 * t + side) * T : (2 * t + side + 1) * T] for t in range(tiles)]
                store(aligned((2 * p + side) * DB, DB), parts)
        return carry

    lax.fori_loop(0, count // 4, some, 0)


def pack_pairs(src, dst, first, count):
    def some(i, carry):
        for q in range(4):
            p = i * 4 + q
            both = jnp.concatenate([src[2 * p], src[2 * p + 1]], axis=0)
            dst[first + p] = both.T
        return carry

    lax.fori_loop(0, count // 4, some, 0)


def pack_turned(src, start, dst, first, count):
    def some(i, carry):
        for q in range(4):
            dst[first + i * 4 + q] = src[start + i * 4 + q].T
        return carry

    lax.fori_loop(0, count // 4, some, 0)


def layer_kernel(
    tok, ids, codes, r1, r2, r3, r4, s1, s2, s3, s4, out_ref,
    x_all, a1, a2, a3, a4, b1, b2, b3, b4, c1, c2, c3, c4,
    slots, z_ref, u_ref, hot, share, shared_out, core_in, y_in, z_in,
    tok_in, r1_in, r3_in, r4_in, s1_in, s3_in, s4_in,
    local_sem, x_send, x_recv, b_send, b_recv, c_send, c_recv, sum_send, sum_recv,
):
    e, d = lax.axis_index("expert"), lax.axis_index("dp")
    z, y, x, c = e // 2, lax.rem(e, 2), d // 2, lax.rem(d, 2)
    near_z = e + 2 - 4 * lax.rem(z, 2)
    on_far = {"expert": lax.rem(e + 4, 8), "dp": d}
    on_near = {"expert": near_z, "dp": d}
    on_y = {"expert": e + 1 - 2 * y, "dp": d}
    on_core = {"expert": e, "dp": d + 1 - 2 * c}
    on_x = {"expert": e, "dp": lax.rem(d + 2, 4)}
    own_a, own_b, own_s = (a1, a2, a3, a4), (b1, b2, b3, b4), (c1, c2, c3, c4)

    def remote(src, dst, send, recv, target):
        return pltpu.make_async_remote_copy(
            src_ref=src, dst_ref=dst, send_sem=send, recv_sem=recv, device_id=target
        )

    def x_copy(number, source, slot, rows, target):
        return remote(
            x_all.at[source, rows], x_all.at[slot, rows], x_send.at[number], x_recv.at[number], target
        )

    whole = pl.ds(0, ROWS)
    spans = [pl.ds(*s) for s in SPANS]
    x_core = x_copy(0, 0, 1, whole, on_core)
    x_y = x_copy(1, 0, 2, whole, on_y)
    x_far = [x_copy(2 + i, 0, 4, rows, on_far) for i, rows in enumerate(spans)]
    x_y_core = x_copy(6, 2, 3, whole, on_core)
    x_far_core = [x_copy(7 + i, 4, 5, rows, on_core) for i, rows in enumerate(spans)]
    x_far_y = [x_copy(11 + i, 4, 6, rows, on_y) for i, rows in enumerate(spans)]
    x_last = [x_copy(15 + i, 6, 7, rows, on_core) for i, rows in enumerate(spans)]

    def leg(number, half, first):
        w, start, size = LEGS[number]
        rows = pl.ds(half * (16 if w in (0, 3) else 32) + start, size)
        src = (r2.at[c] if w == 1 else own_a[w]) if first else own_b[w]
        at = number if first else number + len(LEGS)
        return remote(
            src.at[rows], own_b[w].at[rows], b_send.at[at], b_recv.at[at], on_near if first else on_x
        )

    b_near = [leg(n, x, True) for n in range(len(LEGS))]
    b_x = [leg(n, x, False) for n in range(len(LEGS))]
    b_there = [leg(n, 1 - x, False) for n in range(len(LEGS))]

    def quarter(w, at, number, target, src=None):
        size = 8 if w in (0, 3) else 16
        rows = pl.ds(at * size, size)
        src = own_s[w].at[rows] if src is None else src
        return remote(src, own_s[w].at[rows], c_send.at[number], c_recv.at[number], target)

    sources = (None, s2, None, None)
    c_core = [quarter(w, d, w, on_core, sources[w]) for w in range(4)]
    c_x = [quarter(w, d, 4 + w, on_x, sources[w]) for w in range(4)]
    c_fwd = [quarter(w, lax.rem(d + 2, 4), 8 + w, on_core) for w in range(4)]

    def local(number, src, dst):
        return pltpu.make_async_copy(src, dst, local_sem.at[number])

    tok_load = local(0, tok, tok_in)
    r1_load = local(1, r1.at[c], r1_in)
    r4_load = local(2, r4.at[c], r4_in)
    r3_load = local(3, r3.at[c, pl.ds(x * 32, 32)], r3_in)
    r3_more = local(4, r3.at[c, pl.ds(32 - x * 32, 32)], r3_in)
    r2_load = local(5, r2.at[c], a2)
    s_loads = [local(6, s1, s1_in), local(7, s3, s3_in), local(8, s4, s4_in)]
    s2_load = local(9, s2, c2.at[pl.ds(d * 16, 16)])
    for copy in [tok_load, r1_load, r4_load, r3_load] + s_loads + [s2_load, r2_load]:
        copy.start()

    barrier = pltpu.get_barrier_semaphore()
    for target in (on_far, on_near, on_y, on_core, on_x):
        pl.semaphore_signal(barrier, inc=1, device_id=target)
    pl.semaphore_wait(barrier, 5)

    eye_a = lax.broadcasted_iota(jnp.int32, (T, T), 0)
    eye_b = lax.broadcasted_iota(jnp.int32, (T, T), 1)
    eye = (eye_a == eye_b).astype(F32).astype(BF16)
    pairs = [dot_turned(ref[...].astype(F32).astype(BF16), eye) for ref in (ids, codes)]
    extra = jnp.concatenate(pairs + [jnp.zeros((ROWS - D - 4, T), F32)], axis=0)
    x_all[0, D:ROWS, :] = extra.astype(BF16)
    tok_load.wait()
    for i in range(4):
        for q in range(4):
            at = i * CHUNK + q * 256
            x_all[0, at : at + 256, :] = tok_in[:, at : at + 256].T
        x_far[i].start()
    x_y.start()
    x_core.start()
    r1_load.wait()
    pack_pairs(r1_in, a1, 0, 32)
    b_near[0].start()
    r4_load.wait()
    pack_pairs(r4_in, a4, 0, 32)
    b_near[1].start()
    r3_load.wait()
    for i in range(4):
        pack_turned(r3_in, 8 * i, a3, x * 32 + 8 * i, 8)
        b_near[2 + 2 * i].start()
        b_near[3 + 2 * i].start()
    r3_more.start()
    for copy in s_loads:
        copy.wait()
    pack_pairs(s1_in, c1, d * 8, 8)
    pack_pairs(s4_in, c4, d * 8, 8)
    pack_turned(s3_in, 0, c3, d * 16, 16)
    for w in (0, 1, 2, 3):
        c_x[w].start()
        c_core[w].start()
    r3_more.wait()
    pack_turned(r3_in, 0, a3, 32 - x * 32, 32)

    ids_a = (2 * e + c).astype(F32)
    ids_b = (2 * near_z + c).astype(F32)

    def prepare(q):
        extra = jnp.concatenate(
            [x_all[2 * q, D:ROWS, :].astype(F32), x_all[2 * q + 1, D:ROWS, :].astype(F32)], axis=1
        )
        id0, id1, code0, code1 = (extra[i : i + 1] for i in range(4))
        lane = lax.broadcasted_iota(jnp.int32, (1, 2 * T), 1)
        before = lax.broadcasted_iota(jnp.int32, (2 * T, 2 * T), 0)
        after = lax.broadcasted_iota(jnp.int32, (2 * T, 2 * T), 1)
        tri = jnp.logical_and(before < after, (before < T) == (after < T))
        tri = tri.astype(F32).astype(BF16)
        row8 = lax.broadcasted_iota(jnp.int32, (8, 2 * T), 0)
        picks = [jnp.logical_or(id0 == n, id1 == n) for n in (ids_a, ids_b)]
        names = [jnp.where(p, 1.0, 0.0) for p in picks]
        codes = [jnp.where(id0 == n, code0, code1) for n in (ids_a, ids_b)]
        stacked = jnp.where(row8 == 0, names[0], jnp.where(row8 == 1, names[1], 0.0))
        ranks = dot(stacked.astype(BF16), tri)
        base = jnp.where(lane < T, 2 * q * CAP, (2 * q + 1) * CAP).astype(F32)
        places = [
            jnp.where(picks[n], ranks[n : n + 1] + base, -1000.0).astype(jnp.int32) for n in range(2)
        ]
        for tile, half in ((q, 0), (q - 1, 1)):
            if not 0 <= tile < 3:
                continue
            wanted = lax.broadcasted_iota(jnp.int32, (T, 2 * T), 0) + tile * T
            for n in range(2):
                own = (wanted == places[n]).astype(F32).astype(BF16)
                hot[tile, half, n * T : (n + 1) * T, :] = own
                values = jnp.where(
                    row8 == 0, codes[n], jnp.where(row8 == 1, code0, jnp.where(row8 == 2, code1, 0.0))
                )
                got = lax.dot_general(
                    values.astype(BF16), own, (((1,), (1,)), ((), ())), preferred_element_type=F32
                )
                if half == 0:
                    share[n, tile] = got
                else:
                    share[n, tile] += got

    def pick(tile):
        def some(i, carry):
            rows = aligned(i * 256, 256)
            total = None
            for half in range(2):
                q = tile + half
                both = jnp.concatenate([x_all[2 * q, rows, :], x_all[2 * q + 1, rows, :]], axis=1)
                got = lax.dot_general(
                    both, hot[tile, half], (((1,), (1,)), ((), ())), preferred_element_type=F32
                )
                total = got if total is None else total + got
            total = total.astype(BF16)
            slots[0, tile, rows, :] = total[:, :T]
            slots[1, tile, rows, :] = total[:, T:]
            return carry

        lax.fori_loop(0, D // 256, some, 0)

    def slot_loader(n, first, count):
        return lambda rows: [slots[n, first + i, rows, :] for i in range(count)]

    def slot_storer(n, first, count):
        gates = []
        for i in range(count):
            got = share[n, first + i]
            under = got[1:2] + got[2:3]
            gates.append(jnp.where(under > 0.0, got[0:1] / jnp.maximum(under, 1.0), 0.0))
        gates = [jnp.broadcast_to(g, (DB, T)) for g in gates]

        def store(rows, parts):
            for i in range(count):
                slots[n, first + i, rows, :] = (parts[i] * gates[i]).astype(BF16)

        return store

    def forward(i):
        x_far[i].wait_recv()
        x_far_y[i].start()
        x_far_core[i].start()

    def relay(*numbers):
        for n in numbers:
            b_near[n].wait_recv()
            b_x[n].start()

    x_core.wait_recv()
    prepare(0)
    x_y.wait_recv()
    x_y_core.start()
    relay(0, 1)
    forward(0)
    x_y_core.wait_recv()
    prepare(1)
    pick(0)
    r2_load.wait()
    forward(1)
    up(1, slot_loader(0, 0, 1), a1, z_ref)
    middle(1, a2, a3, z_ref, u_ref, 0, NB)
    down(1, a4, u_ref, slot_storer(0, 0, 1), 0, NB // 2)
    forward(2)
    for copy in c_x:
        copy.wait_recv()
    for copy in c_fwd:
        copy.start()
    relay(2, 3)
    s2_load.wait()
    for copy in c_core + c_fwd:
        copy.wait_recv()

    def keep_shared(rows, parts):
        shared_out[rows, :] = parts[0].astype(BF16)

    up(1, lambda rows: [x_all[0, rows, :]], c1, z_ref)
    forward(3)
    middle(1, c2, c3, z_ref, u_ref, 0, NB)
    x_far_y[0].wait_recv()
    x_last[0].start()
    x_far_y[1].wait_recv()
    x_last[1].start()
    down(1, c4, u_ref, keep_shared, 0, NB // 2)
    relay(4, 5)
    for i in (2, 3):
        x_far_y[i].wait_recv()
        x_last[i].start()
    for copy in x_far_core:
        copy.wait_recv()
    prepare(2)
    for copy in x_last:
        copy.wait_recv()
    prepare(3)
    pick(1)
    pick(2)
    up(2, slot_loader(0, 1, 2), a1, z_ref)
    middle(2, a2, a3, z_ref, u_ref, 0, NB)
    relay(6, 7)
    down(2, a4, u_ref, slot_storer(0, 1, 2), 0, NB // 2)
    b_there[0].wait_recv()
    b_there[1].wait_recv()
    up(3, slot_loader(1, 0, 3), b1, z_ref)
    here, there = x * 32, 32 - x * 32
    for i in range(4):
        if i == 2:
            relay(8, 9)
        middle(3, b2, b3, z_ref, u_ref, here + 8 * i, 8)
        b_there[2 + 2 * i].wait_recv()
        b_there[3 + 2 * i].wait_recv()
        middle(3, b2, b3, z_ref, u_ref, there + 8 * i, 8)

    for copy in [x_core, x_y, x_y_core] + x_far + x_far_core + x_far_y + x_last:
        copy.wait_send()

    def sum_copy(number, src, dst, i, target):
        rows = pl.ds(i * CHUNK, CHUNK)
        return remote(
            src.at[rows], dst.at[rows], sum_send.at[number * 4 + i], sum_recv.at[number * 4 + i], target
        )

    chunks = range(D // CHUNK)
    to_core = [[sum_copy(q, x_all.at[2 * q + 1], core_in.at[q], i, on_core) for i in chunks] for q in range(4)]
    to_y = {q: [sum_copy(4 + q // 2, x_all.at[2 * q], y_in.at[q // 2], i, on_y) for i in chunks] for q in (1, 3)}
    to_far = [sum_copy(6, x_all.at[4], z_in, i, on_far) for i in chunks]

    def combine(q, i):
        where = [(tile, half) for tile, half in ((q, 0), (q - 1, 1)) if 0 <= tile < 3]

        def some(j, carry):
            rows = aligned(i * CHUNK + j * 256, 256)
            total = None
            for tile, half in where:
                both = jnp.concatenate([slots[0, tile, rows, :], slots[1, tile, rows, :]], axis=1)
                got = dot(both, hot[tile, half])
                total = got if total is None else total + got
            total = total.astype(BF16)
            x_all[2 * q, rows, :] = total[:, :T]
            x_all[2 * q + 1, rows, :] = total[:, T:]
            return carry

        lax.fori_loop(0, CHUNK // 256, some, 0)
        to_core[q][i].start()

    def add(q, refs, i):
        def some(j, carry):
            rows = aligned(i * CHUNK + j * 256, 256)
            total = x_all[2 * q, rows, :].astype(F32)
            for ref in refs:
                total += ref[rows, :].astype(F32)
            x_all[2 * q, rows, :] = total.astype(BF16)
            return carry

        lax.fori_loop(0, CHUNK // 256, some, 0)

    def pass_on(q, i):
        to_core[q][i].wait_recv()
        add(q, [core_in.at[q]], i)
        to_y[q][i].start()

    store_b = slot_storer(1, 0, 3)
    for i in chunks:
        down(3, b4, u_ref, store_b, 8 * i, 8)
        combine(3, i)
        if i > 0:
            pass_on(3, i - 1)
    pass_on(3, 3)
    for i in chunks:
        combine(2, i)
    for i in chunks:
        combine(1, i)
        to_core[2][i].wait_recv()
        to_y[3][i].wait_recv()
        add(2, [core_in.at[2], y_in.at[1]], i)
        to_far[i].start()
    for i in chunks:
        pass_on(1, i)
        combine(0, i)
    for i in chunks:
        to_core[0][i].wait_recv()
        to_y[1][i].wait_recv()
        add(0, [core_in.at[0], y_in.at[0], shared_out], i)
    for i in chunks:
        to_far[i].wait_recv()
        for q in range(4):
            at = i * CHUNK + q * 256
            total = x_all[0, at : at + 256, :].astype(F32) + z_in[at : at + 256, :].astype(F32)
            out_ref[:, at : at + 256] = total.T.astype(BF16)

    for copy in b_near + b_x + c_core + c_x + c_fwd:
        copy.wait_send()
    for copies in to_core + [to_y[1], to_y[3], to_far]:
        for copy in copies:
            copy.wait_send()


def layer_call(tokens, expert_ids, gate_codes, shared, routed):
    hbm = pl.BlockSpec(memory_space=pl.ANY)
    vmem = pl.BlockSpec(memory_space=pltpu.VMEM)
    weights = [
        pltpu.VMEM((NB // 2, NB, 2 * DB), BF16), pltpu.VMEM((NB, NB, HB), BF16),
        pltpu.VMEM((NB, NB, HB), BF16), pltpu.VMEM((NB // 2, DB, 2 * NB), BF16),
    ]
    sems = pltpu.SemaphoreType.DMA
    block = pltpu.VMEM((D, T), BF16)
    legs = 2 * len(LEGS)
    return pl.pallas_call(
        layer_kernel,
        out_shape=jax.ShapeDtypeStruct((T, D), BF16),
        in_specs=[hbm, vmem, vmem] + [hbm] * 8,
        out_specs=vmem,
        scratch_shapes=[pltpu.VMEM((8, ROWS, T), BF16)]
        + weights * 3
        + [
            pltpu.VMEM((2, 3, D, T), BF16),
            pltpu.VMEM((3, D, T), F32),
            pltpu.VMEM((3, D, T), F32),
            pltpu.VMEM((3, 2, 2 * T, 2 * T), BF16),
            pltpu.VMEM((2, 3, 8, T), F32),
            block,
            pltpu.VMEM((4, D, T), BF16),
            pltpu.VMEM((2, D, T), BF16),
            block,
            pltpu.VMEM((T, D), BF16),
            pltpu.VMEM((NB, DB, NB), BF16),
            pltpu.VMEM((NB // 2, HB, NB), BF16),
            pltpu.VMEM((NB, NB, DB), BF16),
            pltpu.VMEM((NB // 4, DB, NB), BF16),
            pltpu.VMEM((NB // 4, HB, NB), BF16),
            pltpu.VMEM((NB // 4, NB, DB), BF16),
            sems((10,)), sems((19,)), sems((19,)), sems((legs,)), sems((legs,)),
            sems((12,)), sems((12,)), sems((28,)), sems((28,)),
        ],
        compiler_params=pltpu.CompilerParams(
            collective_id=2, has_side_effects=True, vmem_limit_bytes=63 * 2**20
        ),
        cost_estimate=pl.CostEstimate(flops=10**11, bytes_accessed=3 * 10**8, transcendentals=0),
        name="layer",
    )(tokens, expert_ids, gate_codes, *routed, *shared)


def running(ones, width):
    groups = ones.reshape(ones.shape[0], -1, width).astype(F32)
    inside = jnp.einsum("rgt,tu->rgu", groups, jnp.triu(jnp.ones((width, width), F32)))
    count = groups.shape[1]
    earlier = jnp.triu(jnp.ones((count, count), F32), 1)
    before = jnp.einsum("rg,gh->rh", inside[:, :, -1], earlier, precision=lax.Precision.HIGHEST)
    return (inside + before[:, :, None]).reshape(ones.shape).astype(jnp.int32)


def shards(tokens, expert_ids, gate_codes, *factors):
    shared, routed = factors[:4], factors[4:]
    residents = routed[0].shape[0]
    sources = lax.axis_size("expert")
    tok_rows = tokens.shape[0]
    if sources == 8 and lax.axis_size("dp") == 4 and residents == 2:
        return layer_call(tokens, expert_ids, gate_codes, shared, routed)
    experts_all = residents * sources
    capacity = max(2, 6 * tok_rows // experts_all)
    tiles = -(-sources * capacity // (2 * T))
    depth = tiles * 2 * T
    window = min(depth, -(-(T - 1 + 2 * capacity) // T) * T)

    extra = jnp.concatenate([expert_ids, gate_codes], axis=1).T.astype(BF16)
    extra = jnp.pad(extra, ((0, 16 - extra.shape[0]), (0, 0)))
    x_t = jnp.concatenate([tokens.T, extra], axis=0)
    x_all = gather_tokens(x_t)
    ids_all = x_all[:, D : D + 2].astype(jnp.int32)
    codes = x_all[:, D + 2 : D + 4].astype(F32)
    gates_all = codes / jnp.sum(codes, axis=1, keepdims=True)
    mine = lax.axis_index("expert") * residents + jnp.arange(residents, dtype=jnp.int32)
    match = ids_all[None] == mine[:, None, None, None]
    picked = jnp.any(match, axis=2).reshape(residents, sources * tok_rows)
    gate = jnp.sum(jnp.where(match, gates_all[None], 0.0), axis=2).reshape(residents, sources * tok_rows)
    ones = picked.astype(jnp.int32)
    ranks = running(ones, tok_rows)
    counts = ranks[:, -1]
    starts = (ranks - ones).reshape(residents, sources // 2, 2 * T)[:, :, 0]
    starts = jnp.minimum(starts, depth - window) // T
    pos = jnp.where(picked, ranks - 1, -1)
    slots = jnp.arange(depth, dtype=jnp.int32)
    slot_gates = jnp.sum(
        jnp.where(pos[:, None, :] == slots[None, :, None], gate[:, None, :], 0.0), axis=2
    ).reshape(residents, tiles, 1, 2 * T)
    pos = pos.reshape(residents, sources // 2, 1, 2 * T)

    outs = routed_call(counts, pos, slot_gates, x_all, turned(routed), tiles)
    y = combine_call(starts, pos, outs, sources, depth, window)
    sums = scatter_sums(y)
    whole = tuple(lax.all_gather(w, "dp", axis=0, tiled=True)[None] for w in turned(shared))
    shared_t = shared_call(x_t, whole)
    total = shared_t.astype(F32) + sums.astype(F32)
    return total.astype(BF16).T


def solution(mesh):
    in_specs = (
        P(("expert", "dp"), None),
        P(("expert", "dp"), None),
        P(("expert", "dp"), None),
        P("dp", None, None),
        P("dp", None, None),
        P("dp", None, None),
        P("dp", None, None),
        P("expert", None, None, None),
        P("expert", None, None, None),
        P("expert", None, None, None),
        P("expert", None, None, None),
    )
    out_specs = P(("expert", "dp"), None)
    return jax.shard_map(shards, mesh=mesh, in_specs=in_specs, out_specs=out_specs, check_vma=False)
```

```python
import functools
import math

import jax
import jax.numpy as jnp
from jax import lax
from jax.experimental import pallas as pl
from jax.experimental.pallas import tpu as pltpu
from jax.sharding import PartitionSpec as P

D = 4096
NB = 64
DB = 64
HB = 256
T = 128
F32 = jnp.float32
BF16 = jnp.bfloat16


def tile_monarch(x_ref, lanes, w1_ref, w2_ref, w3_ref, w4_ref, z_refs, u_refs, store):
    def spread(refs, rows, value):
        for i in range(lanes):
            refs[i][rows, :] = value[:, i * T : (i + 1) * T]

    def strided(refs, start):
        parts = [refs[i][pl.ds(start, NB, stride=NB), :] for i in range(lanes)]
        return jnp.concatenate(parts, axis=1).astype(BF16)

    def up(a, carry):
        rows = pl.ds(pl.multiple_of(a * DB, DB), DB)
        x = x_ref[rows, : lanes * T]
        spread(z_refs, rows, jnp.dot(w1_ref[0, a], x, preferred_element_type=F32))
        return carry

    lax.fori_loop(0, NB, up, 0, unroll=8)

    def middle(j, carry):
        hidden = jnp.dot(w2_ref[0, j], strided(z_refs, j), preferred_element_type=F32)
        hidden = (0.5 * hidden) * (1.0 + lax.erf(hidden * (0.5**0.5)))
        u = jnp.dot(w3_ref[0, j], hidden.astype(BF16), preferred_element_type=F32)
        spread(u_refs, pl.ds(pl.multiple_of(j * NB, NB), NB), u)
        return carry

    lax.fori_loop(0, NB, middle, 0, unroll=4)

    def down(k, carry):
        rows = pl.ds(pl.multiple_of(k * DB, DB), DB)
        store(rows, jnp.dot(w4_ref[0, k], strided(u_refs, k), preferred_element_type=F32))
        return carry

    lax.fori_loop(0, NB, down, 0, unroll=8)


def shared_kernel(x_ref, w1_ref, w2_ref, w3_ref, w4_ref, o_ref, z_ref, u_ref):
    def store(rows, value):
        o_ref[rows, :] = value.astype(BF16)

    tile_monarch(x_ref, 1, w1_ref, w2_ref, w3_ref, w4_ref, (z_ref,), (u_ref,), store)


def routed_kernel(
    counts_ref, pos_ref, gate_ref, x_ref, w1_ref, w2_ref, w3_ref, w4_ref,
    o_ref, x_scr, z0_ref, z1_ref, u0_ref, u1_ref,
):
    expert, tile = pl.program_id(0), pl.program_id(1)
    left = counts_ref[expert] - tile * 2 * T
    sources = x_ref.shape[0]

    @pl.when(left <= T)
    def _():
        o_ref[...] = jnp.zeros_like(o_ref)

    def serve(lanes):
        width = lanes * T
        wanted = lax.broadcasted_iota(jnp.int32, (width, 2 * T), 0) + tile * 2 * T
        step = D // 8

        for part in range(8):
            rows = pl.ds(part * step, step)

            def pick(pair, total):
                both = jnp.concatenate([x_ref[2 * pair, rows, :], x_ref[2 * pair + 1, rows, :]], axis=1)
                onehot = (wanted == pos_ref[0, pair, :, :]).astype(F32).astype(BF16)
                return total + lax.dot_general(
                    both, onehot, (((1,), (1,)), ((), ())), preferred_element_type=F32
                )

            total = lax.fori_loop(0, sources // 2, pick, jnp.zeros((step, width), F32))
            x_scr[rows, :width] = total.astype(BF16)

        gate = gate_ref[0, 0][:, :width]

        def store(rows, value):
            o_ref[rows, :width] = (value * gate).astype(BF16)

        tile_monarch(
            x_scr, lanes, w1_ref, w2_ref, w3_ref, w4_ref, (z0_ref, z1_ref), (u0_ref, u1_ref), store
        )

    @pl.when(left > T)
    def _():
        serve(2)

    @pl.when(jnp.logical_and(left > 0, left <= T))
    def _():
        serve(1)


def weight_specs(index_map, buffers=2):
    shapes = ((NB, DB), (HB, NB), (NB, HB), (DB, NB))
    mode = pl.Buffered(buffers)
    return [pl.BlockSpec((1, NB) + shape, index_map, pipeline_mode=mode) for shape in shapes]


def turned(factors):
    return tuple(jnp.swapaxes(w, -1, -2) for w in factors)


def shared_call(x_t, factors):
    return pl.pallas_call(
        shared_kernel,
        out_shape=jax.ShapeDtypeStruct((D, T), BF16),
        grid=(1,),
        in_specs=[pl.BlockSpec((D, T), lambda i: (0, 0))] + weight_specs(lambda i: (0, 0, 0, 0)),
        out_specs=pl.BlockSpec((D, T), lambda i: (0, 0)),
        scratch_shapes=[pltpu.VMEM((D, T), F32), pltpu.VMEM((D, T), F32)],
        compiler_params=pltpu.CompilerParams(vmem_limit_bytes=56 * 2**20),
        cost_estimate=pl.CostEstimate(flops=10**10, bytes_accessed=10**7, transcendentals=0),
        name="shared_expert",
    )(x_t, *factors)


def routed_call(counts, pos, slot_gates, x_all, factors, tiles):
    residents = pos.shape[0]
    sources = x_all.shape[0]
    grid_spec = pltpu.PrefetchScalarGridSpec(
        num_scalar_prefetch=1,
        grid=(residents, tiles),
        in_specs=[
            pl.BlockSpec((1, sources // 2, 1, 2 * T), lambda e, i, c: (e, 0, 0, 0)),
            pl.BlockSpec((1, 1, 1, 2 * T), lambda e, i, c: (e, i, 0, 0)),
            pl.BlockSpec((sources, x_all.shape[1], T), lambda e, i, c: (0, 0, 0), pipeline_mode=pl.Buffered(1)),
        ]
        + weight_specs(lambda e, i, c: (e, 0, 0, 0), 2 if sources <= 8 else 1),
        out_specs=pl.BlockSpec((D, 2 * T), lambda e, i, c: (0, e * tiles + i)),
        scratch_shapes=[pltpu.VMEM((D, 2 * T), BF16)] + [pltpu.VMEM((D, T), F32)] * 4,
    )
    return pl.pallas_call(
        routed_kernel,
        out_shape=jax.ShapeDtypeStruct((D, residents * tiles * 2 * T), BF16),
        grid_spec=grid_spec,
        compiler_params=pltpu.CompilerParams(vmem_limit_bytes=62 * 2**20),
        cost_estimate=pl.CostEstimate(flops=4 * 10**10, bytes_accessed=2 * 10**7, transcendentals=0),
        name="routed_experts",
    )(counts, pos, slot_gates, x_all, *factors)


def combine_kernel(depth, window, starts_ref, pos_ref, o_ref, y_ref):
    residents = starts_ref.shape[0]
    pair = pl.program_id(0)
    wanted = lax.broadcasted_iota(jnp.int32, (window, 2 * T), 0)
    begins = [pl.multiple_of(starts_ref[e, pair] * T, T) for e in range(residents)]
    hots = [
        (wanted + begins[e] == pos_ref[e, 0, :, :]).astype(F32).astype(BF16) for e in range(residents)
    ]
    hot = jnp.concatenate(hots, axis=0)
    step = 512

    def part(i, carry):
        rows = pl.ds(pl.multiple_of(i * step, step), step)
        near = [
            o_ref[rows, pl.ds(pl.multiple_of(begins[e] + e * depth, T), window)] for e in range(residents)
        ]
        total = jnp.dot(jnp.concatenate(near, axis=1), hot, preferred_element_type=F32).astype(BF16)
        y_ref[0, rows, :] = total[:, :T]
        y_ref[1, rows, :] = total[:, T:]
        return carry

    lax.fori_loop(0, D // step, part, 0)


def combine_call(starts, pos, outs, sources, depth, window):
    residents = pos.shape[0]
    grid_spec = pltpu.PrefetchScalarGridSpec(
        num_scalar_prefetch=1,
        grid=(sources // 2,),
        in_specs=[
            pl.BlockSpec((residents, 1, 1, 2 * T), lambda s, c: (0, s, 0, 0)),
            pl.BlockSpec((D, residents * depth), lambda s, c: (0, 0), pipeline_mode=pl.Buffered(1)),
        ],
        out_specs=pl.BlockSpec((2, D, T), lambda s, c: (s, 0, 0)),
    )
    return pl.pallas_call(
        functools.partial(combine_kernel, depth, window),
        out_shape=jax.ShapeDtypeStruct((sources, D, T), BF16),
        grid_spec=grid_spec,
        compiler_params=pltpu.CompilerParams(vmem_limit_bytes=48 * 2**20),
        name="combine",
    )(starts, pos, outs)


def grid_of(count):
    side = math.isqrt(count // 2)
    return count // side, side


def greet(z, y, nz, ny):
    barrier = pltpu.get_barrier_semaphore()
    for other in range(1, ny):
        pl.semaphore_signal(barrier, inc=1, device_id={"expert": z * ny + lax.rem(y + other, ny)})

    @pl.when(z > 0)
    def _():
        pl.semaphore_signal(barrier, inc=1, device_id={"expert": (z - 1) * ny + y})

    @pl.when(z < nz - 1)
    def _():
        pl.semaphore_signal(barrier, inc=1, device_id={"expert": (z + 1) * ny + y})

    peers = ny - 1 + jnp.where(z > 0, 1, 0) + jnp.where(z < nz - 1, 1, 0)
    pl.semaphore_wait(barrier, peers)


def gather_kernel(nz, x_ref, out_ref, own_sem, up_sem, down_sem, side_sem, recv_sem):
    ny = 2
    me = lax.axis_index("expert")
    z, y = me // ny, lax.rem(me, ny)
    beside = z * ny + (1 - y)

    def send(block, src, sem, target):
        return pltpu.make_async_remote_copy(
            src_ref=src, dst_ref=out_ref.at[block], send_sem=sem.at[block],
            recv_sem=recv_sem.at[block], device_id={"expert": target},
        )

    def arrived(block):
        send(block, out_ref.at[block], side_sem, beside).wait_recv()

    greet(z, y, nz, ny)
    own = pltpu.make_async_copy(x_ref, out_ref.at[me], own_sem)
    own.start()

    @pl.when(z < nz - 1)
    def _():
        send(me, x_ref, up_sem, me + ny).start()

    @pl.when(z > 0)
    def _():
        send(me, x_ref, down_sem, me - ny).start()

    send(me, x_ref, side_sem, beside).start()

    for k in range(1, nz):
        block = me - k * ny

        @pl.when(z >= k)
        def _():
            arrived(block)

            @pl.when(z < nz - 1)
            def _():
                send(block, out_ref.at[block], up_sem, me + ny).start()

            send(block, out_ref.at[block], side_sem, beside).start()

        later = me + k * ny

        @pl.when(z + k < nz)
        def _():
            arrived(later)

            @pl.when(z > 0)
            def _():
                send(later, out_ref.at[later], down_sem, me - ny).start()

            send(later, out_ref.at[later], side_sem, beside).start()

    for other in range(nz):
        arrived(other * ny + (1 - y))
    own.wait()
    for other in range(nz):
        block = other * ny + y
        send(block, out_ref.at[block], side_sem, beside).wait_send()

        @pl.when(jnp.logical_and(other <= z, z < nz - 1))
        def _():
            send(block, out_ref.at[block], up_sem, me + ny).wait_send()

        @pl.when(jnp.logical_and(other >= z, z > 0))
        def _():
            send(block, out_ref.at[block], down_sem, me - ny).wait_send()


def gather_tokens(x_t):
    count = lax.axis_size("expert")
    nz, ny = grid_of(count)
    if ny != 2:
        return lax.all_gather(x_t, "expert", axis=0, tiled=False)
    sems = pltpu.SemaphoreType.DMA((count,))
    return pl.pallas_call(
        functools.partial(gather_kernel, nz),
        out_shape=jax.ShapeDtypeStruct((count,) + x_t.shape, x_t.dtype),
        in_specs=[pl.BlockSpec(memory_space=pl.ANY)],
        out_specs=pl.BlockSpec(memory_space=pl.ANY),
        scratch_shapes=[pltpu.SemaphoreType.DMA, sems, sems, sems, sems],
        compiler_params=pltpu.CompilerParams(collective_id=0, has_side_effects=True),
        cost_estimate=pl.CostEstimate(flops=10**11, bytes_accessed=3 * 10**8, transcendentals=0),
        name="gather_tokens",
    )(x_t)


def scatter_kernel(
    nz, y_hbm, out_ref, held, beside_in, below_in, above_in,
    load_sem, side_sem, side_recv, up_sem, up_recv, down_sem, down_recv,
):
    ny = 2
    me = lax.axis_index("expert")
    z, y = me // ny, lax.rem(me, ny)
    beside = z * ny + (1 - y)

    def load(target):
        return pltpu.make_async_copy(y_hbm.at[target * ny + y], held.at[target], load_sem.at[target])

    def side(target):
        return pltpu.make_async_remote_copy(
            src_ref=y_hbm.at[target * ny + (1 - y)], dst_ref=beside_in.at[target],
            send_sem=side_sem.at[target], recv_sem=side_recv.at[target],
            device_id={"expert": beside},
        )

    def up(target):
        return pltpu.make_async_remote_copy(
            src_ref=held.at[target], dst_ref=below_in.at[target], send_sem=up_sem.at[target],
            recv_sem=up_recv.at[target], device_id={"expert": me + ny},
        )

    def down(target):
        return pltpu.make_async_remote_copy(
            src_ref=held.at[target], dst_ref=above_in.at[target], send_sem=down_sem.at[target],
            recv_sem=down_recv.at[target], device_id={"expert": me - ny},
        )

    def add(target, ref):
        step = 512

        def body(i, carry):
            rows = pl.ds(pl.multiple_of(i * step, step), step)
            total = held[target, rows, :].astype(F32) + ref[target, rows, :].astype(F32)
            held[target, rows, :] = total.astype(BF16)
            return carry

        lax.fori_loop(0, D // step, body, 0)

    greet(z, y, nz, ny)
    for k in range(nz - 1, -1, -1):
        @pl.when(z + k < nz)
        def _():
            side(z + k).start()

        if k > 0:
            @pl.when(z - k >= 0)
            def _():
                side(z - k).start()

    for target in range(nz):
        load(target).start()
    for target in range(nz):
        load(target).wait()
    for k in range(nz - 1, 0, -1):
        target = z + k

        @pl.when(z + k < nz)
        def _():
            side(target).wait_recv()
            add(target, beside_in)

            @pl.when(z > 0)
            def _():
                up(target).wait_recv()
                add(target, below_in)

            up(target).start()

        lower = z - k

        @pl.when(z - k >= 0)
        def _():
            side(lower).wait_recv()
            add(lower, beside_in)

            @pl.when(z < nz - 1)
            def _():
                down(lower).wait_recv()
                add(lower, above_in)

            down(lower).start()

    side(z).wait_recv()
    add(z, beside_in)

    @pl.when(z > 0)
    def _():
        up(z).wait_recv()
        add(z, below_in)

    @pl.when(z < nz - 1)
    def _():
        down(z).wait_recv()
        add(z, above_in)

    out_ref[...] = held[z]
    for target in range(nz):
        side(target).wait_send()

        @pl.when(target > z)
        def _():
            up(target).wait_send()

        @pl.when(target < z)
        def _():
            down(target).wait_send()


def scatter_sums(sums):
    count = lax.axis_size("expert")
    nz, ny = grid_of(count)
    if ny != 2:
        return lax.psum_scatter(sums, "expert", scatter_dimension=0, tiled=False)
    block = pltpu.VMEM((nz,) + sums.shape[1:], sums.dtype)
    sems = pltpu.SemaphoreType.DMA((nz,))
    return pl.pallas_call(
        functools.partial(scatter_kernel, nz),
        out_shape=jax.ShapeDtypeStruct(sums.shape[1:], sums.dtype),
        in_specs=[pl.BlockSpec(memory_space=pl.ANY)],
        out_specs=pl.BlockSpec(memory_space=pltpu.VMEM),
        scratch_shapes=[block] * 4 + [sems] * 7,
        compiler_params=pltpu.CompilerParams(
            collective_id=1, has_side_effects=True, vmem_limit_bytes=40 * 2**20
        ),
        cost_estimate=pl.CostEstimate(flops=10**11, bytes_accessed=3 * 10**8, transcendentals=0),
        name="scatter_sums",
    )(sums)


ROWS = D + 16
CAP = 48
CHUNK = 512
CHUNKS = D // CHUNK
SPANS = ((0, 1024), (1024, 1024), (2048, 1024), (3072, ROWS - 3072))
BITS = ((0, 8), (8, 8), (16, 8), (24, 4), (28, 4))
LEGS = ((1, *BITS[0]), (2, *BITS[0]), (0, 0, 16), (3, 0, 16)) + tuple((w, *b) for b in BITS[1:] for w in (1, 2))


def dot(a, b):
    return jnp.dot(a, b, preferred_element_type=F32)


def dot_turned(w, x):
    return lax.dot_general(w, x, (((0,), (0,)), ((), ())), preferred_element_type=F32)


def gelu(hidden):
    return ((0.5 * hidden) * (1.0 + lax.erf(hidden * (0.5**0.5)))).astype(BF16)


def aligned(start, step):
    return pl.ds(pl.multiple_of(start, step), step)


def apart(upper, lower):
    top, bottom = [], []
    for a, b in zip(upper, lower):
        top += [a, jnp.zeros_like(a)]
        bottom += [jnp.zeros_like(b), b]
    return jnp.concatenate([jnp.concatenate(top, axis=1), jnp.concatenate(bottom, axis=1)], axis=0)


def strided(ref, tiles, start):
    return [ref[i, pl.ds(start, NB, stride=NB), :].astype(BF16) for i in range(tiles)]


def up(tiles, load, w1, z_ref):
    def some(i, carry):
        for q in range(4):
            p = i * 4 + q
            parts = load(aligned(p * 2 * DB, 2 * DB))
            value = dot(w1[p], apart([x[:DB] for x in parts], [x[DB:] for x in parts]))
            for t in range(tiles):
                for side in range(2):
                    at = 2 * t + side
                    z_ref[t, aligned((2 * p + side) * DB, DB), :] = value[:, at * T : (at + 1) * T]
        return carry

    lax.fori_loop(0, NB // 8, some, 0)


def middle(tiles, w2, w3, z_ref, u_ref, first, count):
    batch = 8 if tiles == 1 else 4

    def some(i, carry):
        blocks = [first + i * batch + q for q in range(batch)]
        hidden = []
        for j in blocks:
            parts = strided(z_ref, tiles, j)
            rows = parts[0] if tiles == 1 else jnp.concatenate(parts, axis=1)
            hidden.append(gelu(dot_turned(w2[j], rows)))
        for j, h in zip(blocks, hidden):
            value = dot(w3[j], h)
            for t in range(tiles):
                u_ref[t, aligned(j * NB, NB), :] = value[:, t * T : (t + 1) * T]
        return carry

    lax.fori_loop(0, count // batch, some, 0)


def down(tiles, w4, u_ref, store, first, count):
    def some(i, carry):
        for q in range(4):
            p = first + i * 4 + q
            value = dot(w4[p], apart(strided(u_ref, tiles, 2 * p), strided(u_ref, tiles, 2 * p + 1)))
            for side in range(2):
                parts = [value[:, (2 * t + side) * T : (2 * t + side + 1) * T] for t in range(tiles)]
                store(aligned((2 * p + side) * DB, DB), parts)
        return carry

    lax.fori_loop(0, count // 4, some, 0)


def pack_pairs(src, dst, first, count):
    def some(i, carry):
        for q in range(4):
            p = i * 4 + q
            both = jnp.concatenate([src[2 * p], src[2 * p + 1]], axis=0)
            dst[first + p] = both.T
        return carry

    lax.fori_loop(0, count // 4, some, 0)


def layer_kernel(
    tok, ids, codes, r1, r2, r3, r4, s1, s2, s3, s4, out_ref,
    x_all, a1, a2, a3, a4, b1, b2, b3, b4, c1, c2, c3, c4,
    slots, z_ref, u_ref, hot, hot_t, share, shared_out, core_in, y_in, z_in,
    tok_in, r1_in, r4_in, s1_in, s4_in,
    local_sem, x_send, x_recv, b_send, b_recv, c_send, c_recv, sum_send, sum_recv,
):
    e, d = lax.axis_index("expert"), lax.axis_index("dp")
    z, y, x, c = e // 2, lax.rem(e, 2), d // 2, lax.rem(d, 2)
    near_z = e + 2 - 4 * lax.rem(z, 2)
    on_far = {"expert": lax.rem(e + 4, 8), "dp": d}
    on_near = {"expert": near_z, "dp": d}
    on_y = {"expert": e + 1 - 2 * y, "dp": d}
    on_core = {"expert": e, "dp": d + 1 - 2 * c}
    on_x = {"expert": e, "dp": lax.rem(d + 2, 4)}
    own_a, own_b, own_s = (a1, a2, a3, a4), (b1, b2, b3, b4), (c1, c2, c3, c4)

    def remote(src, dst, send, recv, target):
        return pltpu.make_async_remote_copy(
            src_ref=src, dst_ref=dst, send_sem=send, recv_sem=recv, device_id=target
        )

    def x_copy(number, source, slot, rows, target):
        return remote(
            x_all.at[source, rows], x_all.at[slot, rows], x_send.at[number], x_recv.at[number], target
        )

    whole = pl.ds(0, ROWS)
    spans = [pl.ds(*s) for s in SPANS]
    x_core = x_copy(0, 0, 1, whole, on_core)
    x_y = x_copy(1, 0, 2, whole, on_y)
    x_far = [x_copy(2 + i, 0, 4, rows, on_far) for i, rows in enumerate(spans)]
    x_y_core = x_copy(6, 2, 3, whole, on_core)
    x_far_core = [x_copy(7 + i, 4, 5, rows, on_core) for i, rows in enumerate(spans)]
    x_far_y = [x_copy(11 + i, 4, 6, rows, on_y) for i, rows in enumerate(spans)]
    x_last = [x_copy(15 + i, 6, 7, rows, on_core) for i, rows in enumerate(spans)]

    def leg(number, half, first):
        w, start, size = LEGS[number]
        rows = pl.ds(half * (16 if w in (0, 3) else 32) + start, size)
        src = (a1, r2.at[c], r3.at[c], a4)[w] if first else own_b[w]
        at = number if first else number + len(LEGS)
        return remote(
            src.at[rows], own_b[w].at[rows], b_send.at[at], b_recv.at[at], on_near if first else on_x
        )

    b_near = [leg(n, x, True) for n in range(len(LEGS))]
    b_x = [leg(n, x, False) for n in range(len(LEGS))]
    b_there = [leg(n, 1 - x, False) for n in range(len(LEGS))]

    def quarter(w, at, number, target, src=None):
        size = 8 if w in (0, 3) else 16
        rows = pl.ds(at * size, size)
        src = own_s[w].at[rows] if src is None else src
        return remote(src, own_s[w].at[rows], c_send.at[number], c_recv.at[number], target)

    sources = (None, s2, s3, None)
    c_core = [quarter(w, d, w, on_core, sources[w]) for w in range(4)]
    c_x = [quarter(w, d, 4 + w, on_x, sources[w]) for w in range(4)]
    c_fwd = [quarter(w, lax.rem(d + 2, 4), 8 + w, on_core) for w in range(4)]

    def local(number, src, dst):
        return pltpu.make_async_copy(src, dst, local_sem.at[number])

    here_s = pl.ds(d * 16, 16)
    tok_load = local(0, tok, tok_in)
    r1_load = local(1, r1.at[c], r1_in)
    r4_load = local(2, r4.at[c], r4_in)
    r_loads = [local(3, r2.at[c], a2), local(4, r3.at[c], a3)]
    s_packs = [local(5, s1, s1_in), local(6, s4, s4_in)]
    s_loads = [local(7, s2, c2.at[here_s]), local(8, s3, c3.at[here_s])]
    for copy in [tok_load, r1_load, r4_load] + s_packs:
        copy.start()

    barrier = pltpu.get_barrier_semaphore()
    for target in (on_far, on_near, on_y, on_core, on_x):
        pl.semaphore_signal(barrier, inc=1, device_id=target)
    pl.semaphore_wait(barrier, 5)

    b_near[0].start()
    b_near[1].start()
    c_x[1].start()
    c_x[2].start()
    numbers = [ref[...].astype(F32) for ref in (ids, codes)]
    extra = jnp.concatenate(numbers + [jnp.zeros((ROWS - D - 4, T), F32)], axis=0)
    x_all[0, D:ROWS, :] = extra.astype(BF16)
    tok_load.wait()
    for i in range(4):
        for at in range(i * 1024, i * 1024 + 1024, 256):
            x_all[0, at : at + 256, :] = tok_in[:, at : at + 256].T
        x_far[i].start()
    x_y.start()
    x_core.start()
    r1_load.wait()
    pack_pairs(r1_in, a1, 0, 32)
    b_near[2].start()
    r4_load.wait()
    pack_pairs(r4_in, a4, 0, 32)
    for copy in b_near[3:]:
        copy.start()
    for copy in s_packs:
        copy.wait()
    pack_pairs(s1_in, c1, d * 8, 8)
    pack_pairs(s4_in, c4, d * 8, 8)
    c_x[0].start()
    c_x[3].start()
    for copy in c_core + r_loads + s_loads:
        copy.start()

    ids_a = (2 * e + c).astype(F32)
    ids_b = (2 * near_z + c).astype(F32)

    def prepare(q):
        extra = jnp.concatenate(
            [x_all[2 * q, D:ROWS, :].astype(F32), x_all[2 * q + 1, D:ROWS, :].astype(F32)], axis=1
        )
        id0, id1, code0, code1 = (extra[i : i + 1] for i in range(4))
        lane = lax.broadcasted_iota(jnp.int32, (1, 2 * T), 1)
        before = lax.broadcasted_iota(jnp.int32, (2 * T, 2 * T), 0)
        after = lax.broadcasted_iota(jnp.int32, (2 * T, 2 * T), 1)
        tri = jnp.logical_and(before < after, (before < T) == (after < T))
        tri = tri.astype(F32).astype(BF16)
        row8 = lax.broadcasted_iota(jnp.int32, (8, 2 * T), 0)
        picks = [jnp.logical_or(id0 == n, id1 == n) for n in (ids_a, ids_b)]
        names = [jnp.where(p, 1.0, 0.0) for p in picks]
        codes = [jnp.where(id0 == n, code0, code1) for n in (ids_a, ids_b)]
        stacked = jnp.where(row8 == 0, names[0], jnp.where(row8 == 1, names[1], 0.0))
        ranks = dot(stacked.astype(BF16), tri)
        base = jnp.where(lane < T, 2 * q * CAP, (2 * q + 1) * CAP).astype(F32)
        places = [
            jnp.where(picks[n], ranks[n : n + 1] + base, -1000.0).astype(jnp.int32) for n in range(2)
        ]
        for tile, half in ((q, 0), (q - 1, 1)):
            if not 0 <= tile < 3:
                continue
            wanted = lax.broadcasted_iota(jnp.int32, (T, 2 * T), 0) + tile * T
            for n in range(2):
                own = (wanted == places[n]).astype(F32).astype(BF16)
                hot[q, half * 2 * T + n * T : half * 2 * T + (n + 1) * T, :] = own
                hot_t[tile, half * 2 * T : (half + 1) * 2 * T, n * T : (n + 1) * T] = own.T
                values = jnp.where(
                    row8 == 0, codes[n], jnp.where(row8 == 1, code0, jnp.where(row8 == 2, code1, 0.0))
                )
                got = lax.dot_general(
                    values.astype(BF16), own, (((1,), (1,)), ((), ())), preferred_element_type=F32
                )
                if half == 0:
                    share[n, tile] = got
                else:
                    share[n, tile] += got

    def pick(tile):
        def some(i, carry):
            rows = aligned(i * 256, 256)
            blocks = [x_all[2 * tile + n, rows, :] for n in range(4)]
            total = dot(jnp.concatenate(blocks, axis=1), hot_t[tile])
            total = total.astype(BF16)
            slots[0, tile, rows, :] = total[:, :T]
            slots[1, tile, rows, :] = total[:, T:]
            return carry

        lax.fori_loop(0, D // 256, some, 0)

    def slot_loader(n, first, count):
        return lambda rows: [slots[n, first + i, rows, :] for i in range(count)]

    def slot_storer(n, first, count):
        gates = []
        for i in range(count):
            got = share[n, first + i]
            under = got[1:2] + got[2:3]
            gates.append(jnp.where(under > 0.0, got[0:1] / jnp.maximum(under, 1.0), 0.0))
        gates = [jnp.broadcast_to(g, (DB, T)) for g in gates]

        def store(rows, parts):
            for i in range(count):
                slots[n, first + i, rows, :] = (parts[i] * gates[i]).astype(BF16)

        return store

    def forward(i):
        x_far[i].wait_recv()
        x_far_y[i].start()
        x_far_core[i].start()

    def relay(*numbers):
        for n in numbers:
            b_near[n].wait_recv()
            b_x[n].start()

    def last_hop(i):
        x_far_y[i].wait_recv()
        x_last[i].start()

    x_core.wait_recv()
    prepare(0)
    x_y.wait_recv()
    x_y_core.start()
    relay(0, 1)
    forward(0)
    x_y_core.wait_recv()
    prepare(1)
    pick(0)
    for copy in r_loads:
        copy.wait()
    up(1, slot_loader(0, 0, 1), a1, z_ref)
    forward(1)
    middle(1, a2, a3, z_ref, u_ref, 0, NB)
    for copy in c_x:
        copy.wait_recv()
    for copy in c_fwd:
        copy.start()
    forward(2)
    down(1, a4, u_ref, slot_storer(0, 0, 1), 0, NB // 2)
    last_hop(0)
    for copy in s_loads:
        copy.wait()
    for copy in c_core + c_fwd:
        copy.wait_recv()

    def keep_shared(rows, parts):
        shared_out[rows, :] = parts[0].astype(BF16)

    up(1, lambda rows: [x_all[0, rows, :]], c1, z_ref)
    forward(3)
    last_hop(1)
    middle(1, c2, c3, z_ref, u_ref, 0, NB)
    relay(2, 3)
    last_hop(2)
    down(1, c4, u_ref, keep_shared, 0, NB // 2)
    last_hop(3)
    for copy in x_far_core:
        copy.wait_recv()
    prepare(2)
    for copy in x_last:
        copy.wait_recv()
    prepare(3)
    pick(1)
    pick(2)
    relay(4, 5)
    up(2, slot_loader(0, 1, 2), a1, z_ref)
    middle(2, a2, a3, z_ref, u_ref, 0, NB)
    relay(6, 7)
    down(2, a4, u_ref, slot_storer(0, 1, 2), 0, NB // 2)
    b_there[2].wait_recv()
    up(3, slot_loader(1, 0, 3), b1, z_ref)
    relay(8, 9)
    here, there = x * 32, 32 - x * 32
    order = ((0, 0), (0, 1), (1, 0), (1, 1), (2, 0), (3, 0), (2, 1), (4, 0), (3, 1), (4, 1))
    for bit, side in order:
        start, size = BITS[bit]
        legs = (0, 1) if bit == 0 else (2 + 2 * bit, 3 + 2 * bit)
        if side == 1:
            for n in legs:
                b_there[n].wait_recv()
        if (bit, side) == (4, 0):
            relay(10, 11)
        middle(3, b2, b3, z_ref, u_ref, (there if side else here) + start, size)
    b_there[3].wait_recv()

    for copy in [x_core, x_y, x_y_core] + x_far + x_far_core + x_far_y + x_last:
        copy.wait_send()

    def sum_copy(number, src, dst, i, target):
        rows = aligned(i * CHUNK, CHUNK)
        at = number * CHUNKS + i
        return remote(src.at[rows], dst.at[rows], sum_send.at[at], sum_recv.at[at], target)

    def to_core(q, i):
        return sum_copy(q, x_all.at[2 * q + 1], core_in.at[q], i, on_core)

    def to_y(q, i):
        return sum_copy(4 + q // 2, x_all.at[2 * q], y_in.at[q // 2], i, on_y)

    def to_far(i):
        return sum_copy(6, x_all.at[4], z_in, i, on_far)

    def combine(q, i):
        where = [(tile, half) for tile, half in ((q, 0), (q - 1, 1)) if 0 <= tile < 3]
        first, last = where[0][1] * 2 * T, (where[-1][1] + 1) * 2 * T
        for j in range(CHUNK // 256):
            rows = aligned(i * CHUNK + j * 256, 256)
            both = jnp.concatenate([slots[n, tile, rows, :] for tile, _ in where for n in range(2)], axis=1)
            total = dot(both, hot[q, first:last, :]).astype(BF16)
            x_all[2 * q, rows, :] = total[:, :T]
            x_all[2 * q + 1, rows, :] = total[:, T:]
        to_core(q, i).start()

    def summed(q, refs, rows):
        total = x_all[2 * q, rows, :].astype(F32)
        for ref in refs:
            total += ref[rows, :].astype(F32)
        return total

    def add(q, refs, i):
        for j in range(CHUNK // 256):
            rows = aligned(i * CHUNK + j * 256, 256)
            x_all[2 * q, rows, :] = summed(q, refs, rows).astype(BF16)

    def over_y(q, i):
        to_core(q, i).wait_recv()
        add(q, [core_in.at[q]], i)
        to_y(q, i).start()

    def over_z(i):
        to_core(2, i).wait_recv()
        to_y(3, i).wait_recv()
        add(2, [core_in.at[2], y_in.at[1]], i)
        to_far(i).start()

    store_b = slot_storer(1, 0, 3)

    def begin(i, ahead, lag):
        down(3, b4, u_ref, store_b, 4 * i, 4)
        combine(3, i)
        combine(2, i)
        if ahead:
            over_y(3, i - 1)
        if lag:
            over_z(i - 4)

    def loop(first, last, body):
        lax.fori_loop(first, last, lambda i, carry: (body(i), carry)[1], 0)

    begin(0, False, False)
    loop(1, 4, lambda i: begin(i, True, False))
    loop(4, CHUNKS, lambda i: begin(i, True, True))
    over_y(3, CHUNKS - 1)

    def further(i):
        combine(1, 2 * i)
        combine(1, 2 * i + 1)
        over_z(i + CHUNKS - 4)
        over_y(1, 2 * i)
        over_y(1, 2 * i + 1)

    loop(0, CHUNKS // 2, further)
    loop(0, CHUNKS, lambda i: combine(0, i))

    def finish(i):
        to_core(0, i).wait_recv()
        to_y(1, i).wait_recv()
        to_far(i).wait_recv()
        for j in range(CHUNK // 256):
            rows = aligned(i * CHUNK + j * 256, 256)
            total = summed(0, [core_in.at[0], y_in.at[0], shared_out, z_in], rows)
            out_ref[rows, :] = total.astype(BF16)

    loop(0, CHUNKS, finish)

    for copy in b_near + b_x + c_core + c_x + c_fwd:
        copy.wait_send()

    def drain(i):
        for q in range(4):
            to_core(q, i).wait_send()
        to_y(1, i).wait_send()
        to_y(3, i).wait_send()
        to_far(i).wait_send()

    loop(0, CHUNKS, drain)


def layer_call(tokens, expert_ids, gate_codes, shared, routed):
    hbm = pl.BlockSpec(memory_space=pl.ANY)
    vmem = pl.BlockSpec(memory_space=pltpu.VMEM)
    weights = [
        pltpu.VMEM((NB // 2, NB, 2 * DB), BF16), pltpu.VMEM((NB, NB, HB), BF16),
        pltpu.VMEM((NB, NB, HB), BF16), pltpu.VMEM((NB // 2, DB, 2 * NB), BF16),
    ]
    sems = pltpu.SemaphoreType.DMA
    block = pltpu.VMEM((D, T), BF16)
    legs = 2 * len(LEGS)
    routed = (routed[0], routed[1], jnp.swapaxes(routed[2], -1, -2), routed[3])
    shared = (shared[0], shared[1], jnp.swapaxes(shared[2], -1, -2), shared[3])
    return pl.pallas_call(
        layer_kernel,
        out_shape=jax.ShapeDtypeStruct((D, T), BF16),
        in_specs=[hbm, vmem, vmem] + [hbm] * 8,
        out_specs=vmem,
        scratch_shapes=[pltpu.VMEM((8, ROWS, T), BF16)]
        + weights * 3
        + [
            pltpu.VMEM((2, 3, D, T), BF16),
            pltpu.VMEM((3, D, T), F32),
            pltpu.VMEM((3, D, T), F32),
            pltpu.VMEM((4, 4 * T, 2 * T), BF16),
            pltpu.VMEM((3, 4 * T, 2 * T), BF16),
            pltpu.VMEM((2, 3, 8, T), F32),
            block,
            pltpu.VMEM((4, D, T), BF16),
            pltpu.VMEM((2, D, T), BF16),
            block,
            pltpu.VMEM((T, D), BF16),
            pltpu.VMEM((NB, DB, NB), BF16),
            pltpu.VMEM((NB, NB, DB), BF16),
            pltpu.VMEM((NB // 4, DB, NB), BF16),
            pltpu.VMEM((NB // 4, NB, DB), BF16),
            sems((10,)), sems((19,)), sems((19,)), sems((legs,)), sems((legs,)),
            sems((12,)), sems((12,)), sems((7 * CHUNKS,)), sems((7 * CHUNKS,)),
        ],
        compiler_params=pltpu.CompilerParams(
            collective_id=2, has_side_effects=True, vmem_limit_bytes=63 * 2**20
        ),
        cost_estimate=pl.CostEstimate(flops=10**11, bytes_accessed=3 * 10**8, transcendentals=0),
        name="layer",
    )(tokens, expert_ids.T, gate_codes.T, *routed, *shared).T


def running(ones, width):
    groups = ones.reshape(ones.shape[0], -1, width).astype(F32)
    inside = jnp.einsum("rgt,tu->rgu", groups, jnp.triu(jnp.ones((width, width), F32)))
    count = groups.shape[1]
    earlier = jnp.triu(jnp.ones((count, count), F32), 1)
    before = jnp.einsum("rg,gh->rh", inside[:, :, -1], earlier, precision=lax.Precision.HIGHEST)
    return (inside + before[:, :, None]).reshape(ones.shape).astype(jnp.int32)


def shards(tokens, expert_ids, gate_codes, *factors):
    shared, routed = factors[:4], factors[4:]
    residents = routed[0].shape[0]
    sources = lax.axis_size("expert")
    tok_rows = tokens.shape[0]
    if sources == 8 and lax.axis_size("dp") == 4 and residents == 2:
        return layer_call(tokens, expert_ids, gate_codes, shared, routed)
    experts_all = residents * sources
    capacity = max(2, 6 * tok_rows // experts_all)
    tiles = -(-sources * capacity // (2 * T))
    depth = tiles * 2 * T
    window = min(depth, -(-(T - 1 + 2 * capacity) // T) * T)

    extra = jnp.concatenate([expert_ids, gate_codes], axis=1).T.astype(BF16)
    extra = jnp.pad(extra, ((0, 16 - extra.shape[0]), (0, 0)))
    x_t = jnp.concatenate([tokens.T, extra], axis=0)
    x_all = gather_tokens(x_t)
    ids_all = x_all[:, D : D + 2].astype(jnp.int32)
    codes = x_all[:, D + 2 : D + 4].astype(F32)
    gates_all = codes / jnp.sum(codes, axis=1, keepdims=True)
    mine = lax.axis_index("expert") * residents + jnp.arange(residents, dtype=jnp.int32)
    match = ids_all[None] == mine[:, None, None, None]
    picked = jnp.any(match, axis=2).reshape(residents, sources * tok_rows)
    gate = jnp.sum(jnp.where(match, gates_all[None], 0.0), axis=2).reshape(residents, sources * tok_rows)
    ones = picked.astype(jnp.int32)
    ranks = running(ones, tok_rows)
    counts = ranks[:, -1]
    starts = (ranks - ones).reshape(residents, sources // 2, 2 * T)[:, :, 0]
    starts = jnp.minimum(starts, depth - window) // T
    pos = jnp.where(picked, ranks - 1, -1)
    slots = jnp.arange(depth, dtype=jnp.int32)
    slot_gates = jnp.sum(
        jnp.where(pos[:, None, :] == slots[None, :, None], gate[:, None, :], 0.0), axis=2
    ).reshape(residents, tiles, 1, 2 * T)
    pos = pos.reshape(residents, sources // 2, 1, 2 * T)

    outs = routed_call(counts, pos, slot_gates, x_all, turned(routed), tiles)
    y = combine_call(starts, pos, outs, sources, depth, window)
    sums = scatter_sums(y)
    whole = tuple(lax.all_gather(w, "dp", axis=0, tiled=True)[None] for w in turned(shared))
    shared_t = shared_call(x_t, whole)
    total = shared_t.astype(F32) + sums.astype(F32)
    return total.astype(BF16).T


def solution(mesh):
    in_specs = (
        P(("expert", "dp"), None),
        P(("expert", "dp"), None),
        P(("expert", "dp"), None),
        P("dp", None, None),
        P("dp", None, None),
        P("dp", None, None),
        P("dp", None, None),
        P("expert", None, None, None),
        P("expert", None, None, None),
        P("expert", None, None, None),
        P("expert", None, None, None),
    )
    out_specs = P(("expert", "dp"), None)
    return jax.shard_map(shards, mesh=mesh, in_specs=in_specs, out_specs=out_specs, check_vma=False)
```

```python
import functools
import math

import jax
import jax.numpy as jnp
from jax import lax
from jax.experimental import pallas as pl
from jax.experimental.pallas import tpu as pltpu
from jax.sharding import PartitionSpec as P

D = 4096
NB = 64
DB = 64
HB = 256
T = 128
F32 = jnp.float32
BF16 = jnp.bfloat16


def tile_monarch(x_ref, lanes, w1_ref, w2_ref, w3_ref, w4_ref, z_refs, u_refs, store):
    def spread(refs, rows, value):
        for i in range(lanes):
            refs[i][rows, :] = value[:, i * T : (i + 1) * T]

    def strided(refs, start):
        parts = [refs[i][pl.ds(start, NB, stride=NB), :] for i in range(lanes)]
        return jnp.concatenate(parts, axis=1).astype(BF16)

    def up(a, carry):
        rows = pl.ds(pl.multiple_of(a * DB, DB), DB)
        x = x_ref[rows, : lanes * T]
        spread(z_refs, rows, jnp.dot(w1_ref[0, a], x, preferred_element_type=F32))
        return carry

    lax.fori_loop(0, NB, up, 0, unroll=8)

    def middle(j, carry):
        hidden = jnp.dot(w2_ref[0, j], strided(z_refs, j), preferred_element_type=F32)
        hidden = (0.5 * hidden) * (1.0 + lax.erf(hidden * (0.5**0.5)))
        u = jnp.dot(w3_ref[0, j], hidden.astype(BF16), preferred_element_type=F32)
        spread(u_refs, pl.ds(pl.multiple_of(j * NB, NB), NB), u)
        return carry

    lax.fori_loop(0, NB, middle, 0, unroll=4)

    def down(k, carry):
        rows = pl.ds(pl.multiple_of(k * DB, DB), DB)
        store(rows, jnp.dot(w4_ref[0, k], strided(u_refs, k), preferred_element_type=F32))
        return carry

    lax.fori_loop(0, NB, down, 0, unroll=8)


def shared_kernel(x_ref, w1_ref, w2_ref, w3_ref, w4_ref, o_ref, z_ref, u_ref):
    def store(rows, value):
        o_ref[rows, :] = value.astype(BF16)

    tile_monarch(x_ref, 1, w1_ref, w2_ref, w3_ref, w4_ref, (z_ref,), (u_ref,), store)


def routed_kernel(
    counts_ref, pos_ref, gate_ref, x_ref, w1_ref, w2_ref, w3_ref, w4_ref,
    o_ref, x_scr, z0_ref, z1_ref, u0_ref, u1_ref,
):
    expert, tile = pl.program_id(0), pl.program_id(1)
    left = counts_ref[expert] - tile * 2 * T
    sources = x_ref.shape[0]

    @pl.when(left <= T)
    def _():
        o_ref[...] = jnp.zeros_like(o_ref)

    def serve(lanes):
        width = lanes * T
        wanted = lax.broadcasted_iota(jnp.int32, (width, 2 * T), 0) + tile * 2 * T
        step = D // 8

        for part in range(8):
            rows = pl.ds(part * step, step)

            def pick(pair, total):
                both = jnp.concatenate([x_ref[2 * pair, rows, :], x_ref[2 * pair + 1, rows, :]], axis=1)
                onehot = (wanted == pos_ref[0, pair, :, :]).astype(F32).astype(BF16)
                return total + lax.dot_general(
                    both, onehot, (((1,), (1,)), ((), ())), preferred_element_type=F32
                )

            total = lax.fori_loop(0, sources // 2, pick, jnp.zeros((step, width), F32))
            x_scr[rows, :width] = total.astype(BF16)

        gate = gate_ref[0, 0][:, :width]

        def store(rows, value):
            o_ref[rows, :width] = (value * gate).astype(BF16)

        tile_monarch(
            x_scr, lanes, w1_ref, w2_ref, w3_ref, w4_ref, (z0_ref, z1_ref), (u0_ref, u1_ref), store
        )

    @pl.when(left > T)
    def _():
        serve(2)

    @pl.when(jnp.logical_and(left > 0, left <= T))
    def _():
        serve(1)


def weight_specs(index_map, buffers=2):
    shapes = ((NB, DB), (HB, NB), (NB, HB), (DB, NB))
    mode = pl.Buffered(buffers)
    return [pl.BlockSpec((1, NB) + shape, index_map, pipeline_mode=mode) for shape in shapes]


def turned(factors):
    return tuple(jnp.swapaxes(w, -1, -2) for w in factors)


def shared_call(x_t, factors):
    return pl.pallas_call(
        shared_kernel,
        out_shape=jax.ShapeDtypeStruct((D, T), BF16),
        grid=(1,),
        in_specs=[pl.BlockSpec((D, T), lambda i: (0, 0))] + weight_specs(lambda i: (0, 0, 0, 0)),
        out_specs=pl.BlockSpec((D, T), lambda i: (0, 0)),
        scratch_shapes=[pltpu.VMEM((D, T), F32), pltpu.VMEM((D, T), F32)],
        compiler_params=pltpu.CompilerParams(vmem_limit_bytes=56 * 2**20),
        cost_estimate=pl.CostEstimate(flops=10**10, bytes_accessed=10**7, transcendentals=0),
        name="shared_expert",
    )(x_t, *factors)


def routed_call(counts, pos, slot_gates, x_all, factors, tiles):
    residents = pos.shape[0]
    sources = x_all.shape[0]
    grid_spec = pltpu.PrefetchScalarGridSpec(
        num_scalar_prefetch=1,
        grid=(residents, tiles),
        in_specs=[
            pl.BlockSpec((1, sources // 2, 1, 2 * T), lambda e, i, c: (e, 0, 0, 0)),
            pl.BlockSpec((1, 1, 1, 2 * T), lambda e, i, c: (e, i, 0, 0)),
            pl.BlockSpec((sources, x_all.shape[1], T), lambda e, i, c: (0, 0, 0), pipeline_mode=pl.Buffered(1)),
        ]
        + weight_specs(lambda e, i, c: (e, 0, 0, 0), 2 if sources <= 8 else 1),
        out_specs=pl.BlockSpec((D, 2 * T), lambda e, i, c: (0, e * tiles + i)),
        scratch_shapes=[pltpu.VMEM((D, 2 * T), BF16)] + [pltpu.VMEM((D, T), F32)] * 4,
    )
    return pl.pallas_call(
        routed_kernel,
        out_shape=jax.ShapeDtypeStruct((D, residents * tiles * 2 * T), BF16),
        grid_spec=grid_spec,
        compiler_params=pltpu.CompilerParams(vmem_limit_bytes=62 * 2**20),
        cost_estimate=pl.CostEstimate(flops=4 * 10**10, bytes_accessed=2 * 10**7, transcendentals=0),
        name="routed_experts",
    )(counts, pos, slot_gates, x_all, *factors)


def combine_kernel(depth, window, starts_ref, pos_ref, o_ref, y_ref):
    residents = starts_ref.shape[0]
    pair = pl.program_id(0)
    wanted = lax.broadcasted_iota(jnp.int32, (window, 2 * T), 0)
    begins = [pl.multiple_of(starts_ref[e, pair] * T, T) for e in range(residents)]
    hots = [
        (wanted + begins[e] == pos_ref[e, 0, :, :]).astype(F32).astype(BF16) for e in range(residents)
    ]
    hot = jnp.concatenate(hots, axis=0)
    step = 512

    def part(i, carry):
        rows = pl.ds(pl.multiple_of(i * step, step), step)
        near = [
            o_ref[rows, pl.ds(pl.multiple_of(begins[e] + e * depth, T), window)] for e in range(residents)
        ]
        total = jnp.dot(jnp.concatenate(near, axis=1), hot, preferred_element_type=F32).astype(BF16)
        y_ref[0, rows, :] = total[:, :T]
        y_ref[1, rows, :] = total[:, T:]
        return carry

    lax.fori_loop(0, D // step, part, 0)


def combine_call(starts, pos, outs, sources, depth, window):
    residents = pos.shape[0]
    grid_spec = pltpu.PrefetchScalarGridSpec(
        num_scalar_prefetch=1,
        grid=(sources // 2,),
        in_specs=[
            pl.BlockSpec((residents, 1, 1, 2 * T), lambda s, c: (0, s, 0, 0)),
            pl.BlockSpec((D, residents * depth), lambda s, c: (0, 0), pipeline_mode=pl.Buffered(1)),
        ],
        out_specs=pl.BlockSpec((2, D, T), lambda s, c: (s, 0, 0)),
    )
    return pl.pallas_call(
        functools.partial(combine_kernel, depth, window),
        out_shape=jax.ShapeDtypeStruct((sources, D, T), BF16),
        grid_spec=grid_spec,
        compiler_params=pltpu.CompilerParams(vmem_limit_bytes=48 * 2**20),
        name="combine",
    )(starts, pos, outs)


def grid_of(count):
    side = math.isqrt(count // 2)
    return count // side, side


def greet(z, y, nz, ny):
    barrier = pltpu.get_barrier_semaphore()
    for other in range(1, ny):
        pl.semaphore_signal(barrier, inc=1, device_id={"expert": z * ny + lax.rem(y + other, ny)})

    @pl.when(z > 0)
    def _():
        pl.semaphore_signal(barrier, inc=1, device_id={"expert": (z - 1) * ny + y})

    @pl.when(z < nz - 1)
    def _():
        pl.semaphore_signal(barrier, inc=1, device_id={"expert": (z + 1) * ny + y})

    peers = ny - 1 + jnp.where(z > 0, 1, 0) + jnp.where(z < nz - 1, 1, 0)
    pl.semaphore_wait(barrier, peers)


def gather_kernel(nz, x_ref, out_ref, own_sem, up_sem, down_sem, side_sem, recv_sem):
    ny = 2
    me = lax.axis_index("expert")
    z, y = me // ny, lax.rem(me, ny)
    beside = z * ny + (1 - y)

    def send(block, src, sem, target):
        return pltpu.make_async_remote_copy(
            src_ref=src, dst_ref=out_ref.at[block], send_sem=sem.at[block],
            recv_sem=recv_sem.at[block], device_id={"expert": target},
        )

    def arrived(block):
        send(block, out_ref.at[block], side_sem, beside).wait_recv()

    greet(z, y, nz, ny)
    own = pltpu.make_async_copy(x_ref, out_ref.at[me], own_sem)
    own.start()

    @pl.when(z < nz - 1)
    def _():
        send(me, x_ref, up_sem, me + ny).start()

    @pl.when(z > 0)
    def _():
        send(me, x_ref, down_sem, me - ny).start()

    send(me, x_ref, side_sem, beside).start()

    for k in range(1, nz):
        block = me - k * ny

        @pl.when(z >= k)
        def _():
            arrived(block)

            @pl.when(z < nz - 1)
            def _():
                send(block, out_ref.at[block], up_sem, me + ny).start()

            send(block, out_ref.at[block], side_sem, beside).start()

        later = me + k * ny

        @pl.when(z + k < nz)
        def _():
            arrived(later)

            @pl.when(z > 0)
            def _():
                send(later, out_ref.at[later], down_sem, me - ny).start()

            send(later, out_ref.at[later], side_sem, beside).start()

    for other in range(nz):
        arrived(other * ny + (1 - y))
    own.wait()
    for other in range(nz):
        block = other * ny + y
        send(block, out_ref.at[block], side_sem, beside).wait_send()

        @pl.when(jnp.logical_and(other <= z, z < nz - 1))
        def _():
            send(block, out_ref.at[block], up_sem, me + ny).wait_send()

        @pl.when(jnp.logical_and(other >= z, z > 0))
        def _():
            send(block, out_ref.at[block], down_sem, me - ny).wait_send()


def gather_tokens(x_t):
    count = lax.axis_size("expert")
    nz, ny = grid_of(count)
    if ny != 2:
        return lax.all_gather(x_t, "expert", axis=0, tiled=False)
    sems = pltpu.SemaphoreType.DMA((count,))
    return pl.pallas_call(
        functools.partial(gather_kernel, nz),
        out_shape=jax.ShapeDtypeStruct((count,) + x_t.shape, x_t.dtype),
        in_specs=[pl.BlockSpec(memory_space=pl.ANY)],
        out_specs=pl.BlockSpec(memory_space=pl.ANY),
        scratch_shapes=[pltpu.SemaphoreType.DMA, sems, sems, sems, sems],
        compiler_params=pltpu.CompilerParams(collective_id=0, has_side_effects=True),
        cost_estimate=pl.CostEstimate(flops=10**11, bytes_accessed=3 * 10**8, transcendentals=0),
        name="gather_tokens",
    )(x_t)


def scatter_kernel(
    nz, y_hbm, out_ref, held, beside_in, below_in, above_in,
    load_sem, side_sem, side_recv, up_sem, up_recv, down_sem, down_recv,
):
    ny = 2
    me = lax.axis_index("expert")
    z, y = me // ny, lax.rem(me, ny)
    beside = z * ny + (1 - y)

    def load(target):
        return pltpu.make_async_copy(y_hbm.at[target * ny + y], held.at[target], load_sem.at[target])

    def side(target):
        return pltpu.make_async_remote_copy(
            src_ref=y_hbm.at[target * ny + (1 - y)], dst_ref=beside_in.at[target],
            send_sem=side_sem.at[target], recv_sem=side_recv.at[target],
            device_id={"expert": beside},
        )

    def up(target):
        return pltpu.make_async_remote_copy(
            src_ref=held.at[target], dst_ref=below_in.at[target], send_sem=up_sem.at[target],
            recv_sem=up_recv.at[target], device_id={"expert": me + ny},
        )

    def down(target):
        return pltpu.make_async_remote_copy(
            src_ref=held.at[target], dst_ref=above_in.at[target], send_sem=down_sem.at[target],
            recv_sem=down_recv.at[target], device_id={"expert": me - ny},
        )

    def add(target, ref):
        step = 512

        def body(i, carry):
            rows = pl.ds(pl.multiple_of(i * step, step), step)
            total = held[target, rows, :].astype(F32) + ref[target, rows, :].astype(F32)
            held[target, rows, :] = total.astype(BF16)
            return carry

        lax.fori_loop(0, D // step, body, 0)

    greet(z, y, nz, ny)
    for k in range(nz - 1, -1, -1):
        @pl.when(z + k < nz)
        def _():
            side(z + k).start()

        if k > 0:
            @pl.when(z - k >= 0)
            def _():
                side(z - k).start()

    for target in range(nz):
        load(target).start()
    for target in range(nz):
        load(target).wait()
    for k in range(nz - 1, 0, -1):
        target = z + k

        @pl.when(z + k < nz)
        def _():
            side(target).wait_recv()
            add(target, beside_in)

            @pl.when(z > 0)
            def _():
                up(target).wait_recv()
                add(target, below_in)

            up(target).start()

        lower = z - k

        @pl.when(z - k >= 0)
        def _():
            side(lower).wait_recv()
            add(lower, beside_in)

            @pl.when(z < nz - 1)
            def _():
                down(lower).wait_recv()
                add(lower, above_in)

            down(lower).start()

    side(z).wait_recv()
    add(z, beside_in)

    @pl.when(z > 0)
    def _():
        up(z).wait_recv()
        add(z, below_in)

    @pl.when(z < nz - 1)
    def _():
        down(z).wait_recv()
        add(z, above_in)

    out_ref[...] = held[z]
    for target in range(nz):
        side(target).wait_send()

        @pl.when(target > z)
        def _():
            up(target).wait_send()

        @pl.when(target < z)
        def _():
            down(target).wait_send()


def scatter_sums(sums):
    count = lax.axis_size("expert")
    nz, ny = grid_of(count)
    if ny != 2:
        return lax.psum_scatter(sums, "expert", scatter_dimension=0, tiled=False)
    block = pltpu.VMEM((nz,) + sums.shape[1:], sums.dtype)
    sems = pltpu.SemaphoreType.DMA((nz,))
    return pl.pallas_call(
        functools.partial(scatter_kernel, nz),
        out_shape=jax.ShapeDtypeStruct(sums.shape[1:], sums.dtype),
        in_specs=[pl.BlockSpec(memory_space=pl.ANY)],
        out_specs=pl.BlockSpec(memory_space=pltpu.VMEM),
        scratch_shapes=[block] * 4 + [sems] * 7,
        compiler_params=pltpu.CompilerParams(
            collective_id=1, has_side_effects=True, vmem_limit_bytes=40 * 2**20
        ),
        cost_estimate=pl.CostEstimate(flops=10**11, bytes_accessed=3 * 10**8, transcendentals=0),
        name="scatter_sums",
    )(sums)


ROWS = D + 16
CAP = 48
CHUNK = 256
CHUNKS = D // CHUNK
LAG = 6
SPANS = ((0, 1024), (1024, 1024), (2048, 1280), (3328, ROWS - 3328))
BITS = ((0, 8), (8, 4), (12, 4), (16, 4), (20, 4), (24, 4), (28, 2), (30, 2))
LEGS = ((1, *BITS[0]), (2, *BITS[0]), (0, 0, 16), (3, 0, 16)) + tuple((w, *b) for b in BITS[1:] for w in (1, 2))
RELAYED = len(LEGS) - 2


def dot(a, b):
    return jnp.dot(a, b, preferred_element_type=F32)


def dot_turned(w, x):
    return lax.dot_general(w, x, (((0,), (0,)), ((), ())), preferred_element_type=F32)


def gelu(hidden):
    return ((0.5 * hidden) * (1.0 + lax.erf(hidden * (0.5**0.5)))).astype(BF16)


def aligned(start, step):
    return pl.ds(pl.multiple_of(start, step), step)


def apart(upper, lower):
    top, bottom = [], []
    for a, b in zip(upper, lower):
        top += [a, jnp.zeros_like(a)]
        bottom += [jnp.zeros_like(b), b]
    return jnp.concatenate([jnp.concatenate(top, axis=1), jnp.concatenate(bottom, axis=1)], axis=0)


def strided(ref, tiles, start):
    return [ref[i, pl.ds(start, NB, stride=NB), :].astype(BF16) for i in range(tiles)]


def up(tiles, load, w1, z_ref):
    def some(i, carry):
        for q in range(4):
            p = i * 4 + q
            parts = load(aligned(p * 2 * DB, 2 * DB))
            value = dot(w1[p], apart([x[:DB] for x in parts], [x[DB:] for x in parts]))
            for t in range(tiles):
                for side in range(2):
                    at = 2 * t + side
                    z_ref[t, aligned((2 * p + side) * DB, DB), :] = value[:, at * T : (at + 1) * T]
        return carry

    lax.fori_loop(0, NB // 8, some, 0)


def middle(tiles, w2, w3, z_ref, u_ref, first, count):
    batch = min(count, 8 if tiles == 1 else 4)

    def some(i, carry):
        blocks = [first + i * batch + q for q in range(batch)]
        hidden = []
        for j in blocks:
            parts = strided(z_ref, tiles, j)
            rows = parts[0] if tiles == 1 else jnp.concatenate(parts, axis=1)
            hidden.append(gelu(dot_turned(w2[j], rows)))
        for j, h in zip(blocks, hidden):
            value = dot(w3[j], h)
            for t in range(tiles):
                u_ref[t, aligned(j * NB, NB), :] = value[:, t * T : (t + 1) * T]
        return carry

    lax.fori_loop(0, count // batch, some, 0)


def down(tiles, w4, u_ref, store, first, count):
    batch = min(count, 4)

    def some(i, carry):
        for q in range(batch):
            p = first + i * batch + q
            value = dot(w4[p], apart(strided(u_ref, tiles, 2 * p), strided(u_ref, tiles, 2 * p + 1)))
            for side in range(2):
                parts = [value[:, (2 * t + side) * T : (2 * t + side + 1) * T] for t in range(tiles)]
                store(aligned((2 * p + side) * DB, DB), parts)
        return carry

    lax.fori_loop(0, count // batch, some, 0)


def pack_pairs(src, dst, first, count):
    def some(i, carry):
        for q in range(4):
            p = i * 4 + q
            both = jnp.concatenate([src[2 * p], src[2 * p + 1]], axis=0)
            dst[first + p] = both.T
        return carry

    lax.fori_loop(0, count // 4, some, 0)


def layer_kernel(
    tok, ids, codes, r1, r2, r3, r4, s1, s2, s3, s4, out_ref,
    x_all, a1, a2, a3, a4, b1, b2, b3, b4, c1, c2, c3, c4,
    slots, z_ref, u_ref, hot, hot_t, share, shared_out, out_v, core_in, y_in, z_in,
    tok_in, r1_in, r4_in, s1_in, s4_in,
    local_sem, x_send, x_recv, b_send, b_recv, c_send, c_recv, sum_send, sum_recv,
):
    e, d = lax.axis_index("expert"), lax.axis_index("dp")
    z, y, x, c = e // 2, lax.rem(e, 2), d // 2, lax.rem(d, 2)
    near_z = e + 2 - 4 * lax.rem(z, 2)
    on_far = {"expert": lax.rem(e + 4, 8), "dp": d}
    on_near = {"expert": near_z, "dp": d}
    on_y = {"expert": e + 1 - 2 * y, "dp": d}
    on_core = {"expert": e, "dp": d + 1 - 2 * c}
    on_x = {"expert": e, "dp": lax.rem(d + 2, 4)}
    own_a, own_b, own_s = (a1, a2, a3, a4), (b1, b2, b3, b4), (c1, c2, c3, c4)

    def remote(src, dst, send, recv, target):
        return pltpu.make_async_remote_copy(
            src_ref=src, dst_ref=dst, send_sem=send, recv_sem=recv, device_id=target
        )

    def x_copy(number, source, slot, rows, target):
        return remote(
            x_all.at[source, rows], x_all.at[slot, rows], x_send.at[number], x_recv.at[number], target
        )

    whole = pl.ds(0, ROWS)
    spans = [pl.ds(*s) for s in SPANS]
    x_core = x_copy(0, 0, 1, whole, on_core)
    x_y = x_copy(1, 0, 2, whole, on_y)
    x_far = [x_copy(2 + i, 0, 4, rows, on_far) for i, rows in enumerate(spans)]
    x_y_core = x_copy(6, 2, 3, whole, on_core)
    x_far_core = [x_copy(7 + i, 4, 5, rows, on_core) for i, rows in enumerate(spans)]
    x_far_y = [x_copy(11 + i, 4, 6, rows, on_y) for i, rows in enumerate(spans)]
    x_last = [x_copy(15 + i, 6, 7, rows, on_core) for i, rows in enumerate(spans)]

    def leg(number, half, first, spare=0):
        w, start, size = LEGS[number]
        rows = pl.ds(half * (16 if w in (0, 3) else 32) + start, size)
        src = (a1, r2.at[c], r3.at[c], a4)[w] if first else own_b[w]
        at = number + spare if first else number + len(LEGS) + 2
        return remote(
            src.at[rows], own_b[w].at[rows], b_send.at[at], b_recv.at[at], on_near if first else on_x
        )

    b_near = [leg(n, x, True) for n in range(len(LEGS))]
    b_near += [leg(n, 1 - x, True, 2) for n in range(RELAYED, len(LEGS))]
    b_x = [leg(n, x, False) for n in range(RELAYED)]
    b_there = [leg(n, 1 - x, False) for n in range(RELAYED)]

    def quarter(w, at, number, target, src=None):
        size = 8 if w in (0, 3) else 16
        rows = pl.ds(at * size, size)
        src = own_s[w].at[rows] if src is None else src
        return remote(src, own_s[w].at[rows], c_send.at[number], c_recv.at[number], target)

    sources = (None, s2, s3, None)
    c_core = [quarter(w, d, w, on_core, sources[w]) for w in range(4)]
    c_x = [quarter(w, d, 4 + w, on_x, sources[w]) for w in range(4)]
    c_fwd = [quarter(w, lax.rem(d + 2, 4), 8 + w, on_core) for w in range(4)]

    def local(number, src, dst):
        return pltpu.make_async_copy(src, dst, local_sem.at[number])

    here_s = pl.ds(d * 16, 16)
    tok_load = local(0, tok, tok_in)
    r1_load = local(1, r1.at[c], r1_in)
    r4_load = local(2, r4.at[c], r4_in)
    r_loads = [local(3, r2.at[c], a2), local(4, r3.at[c], a3)]
    s_packs = [local(5, s1, s1_in), local(6, s4, s4_in)]
    s_loads = [local(7, s2, c2.at[here_s]), local(8, s3, c3.at[here_s])]
    for copy in [tok_load, r1_load, r4_load] + s_packs:
        copy.start()

    barrier = pltpu.get_barrier_semaphore()
    for target in (on_far, on_near, on_y, on_core, on_x):
        pl.semaphore_signal(barrier, inc=1, device_id=target)
    pl.semaphore_wait(barrier, 5)

    b_near[0].start()
    b_near[1].start()
    c_x[1].start()
    c_x[2].start()
    numbers = [ref[...].astype(F32) for ref in (ids, codes)]
    extra = jnp.concatenate(numbers + [jnp.zeros((ROWS - D - 4, T), F32)], axis=0)
    x_all[0, D:ROWS, :] = extra.astype(BF16)
    tok_load.wait()
    for i in range(4):
        for at in range(SPANS[i][0], min(D, sum(SPANS[i])), 256):
            x_all[0, at : at + 256, :] = tok_in[:, at : at + 256].T
        x_far[i].start()
    x_y.start()
    x_core.start()
    r1_load.wait()
    pack_pairs(r1_in, a1, 0, 32)
    b_near[2].start()
    r4_load.wait()
    pack_pairs(r4_in, a4, 0, 32)
    for copy in b_near[3:]:
        copy.start()
    for copy in s_packs:
        copy.wait()
    pack_pairs(s1_in, c1, d * 8, 8)
    pack_pairs(s4_in, c4, d * 8, 8)
    c_x[0].start()
    c_x[3].start()
    for copy in c_core + r_loads + s_loads:
        copy.start()

    ids_a = (2 * e + c).astype(F32)
    ids_b = (2 * near_z + c).astype(F32)

    def prepare(q):
        extra = jnp.concatenate(
            [x_all[2 * q, D:ROWS, :].astype(F32), x_all[2 * q + 1, D:ROWS, :].astype(F32)], axis=1
        )
        id0, id1, code0, code1 = (extra[i : i + 1] for i in range(4))
        lane = lax.broadcasted_iota(jnp.int32, (1, 2 * T), 1)
        before = lax.broadcasted_iota(jnp.int32, (2 * T, 2 * T), 0)
        after = lax.broadcasted_iota(jnp.int32, (2 * T, 2 * T), 1)
        tri = jnp.logical_and(before < after, (before < T) == (after < T))
        tri = tri.astype(F32).astype(BF16)
        row8 = lax.broadcasted_iota(jnp.int32, (8, 2 * T), 0)
        picks = [jnp.logical_or(id0 == n, id1 == n) for n in (ids_a, ids_b)]
        names = [jnp.where(p, 1.0, 0.0) for p in picks]
        codes = [jnp.where(id0 == n, code0, code1) for n in (ids_a, ids_b)]
        stacked = jnp.where(row8 == 0, names[0], jnp.where(row8 == 1, names[1], 0.0))
        ranks = dot(stacked.astype(BF16), tri)
        base = jnp.where(lane < T, 2 * q * CAP, (2 * q + 1) * CAP).astype(F32)
        places = [
            jnp.where(picks[n], ranks[n : n + 1] + base, -1000.0).astype(jnp.int32) for n in range(2)
        ]
        for tile, half in ((q, 0), (q - 1, 1)):
            if not 0 <= tile < 3:
                continue
            wanted = lax.broadcasted_iota(jnp.int32, (T, 2 * T), 0) + tile * T
            for n in range(2):
                own = (wanted == places[n]).astype(F32).astype(BF16)
                hot[q, half * 2 * T + n * T : half * 2 * T + (n + 1) * T, :] = own
                hot_t[tile, half * 2 * T : (half + 1) * 2 * T, n * T : (n + 1) * T] = own.T
                values = jnp.where(
                    row8 == 0, codes[n], jnp.where(row8 == 1, code0, jnp.where(row8 == 2, code1, 0.0))
                )
                got = lax.dot_general(
                    values.astype(BF16), own, (((1,), (1,)), ((), ())), preferred_element_type=F32
                )
                if half == 0:
                    share[n, tile] = got
                else:
                    share[n, tile] += got

    def pick(tile):
        def some(i, carry):
            rows = aligned(i * 512, 512)
            blocks = [x_all[2 * tile + n, rows, :] for n in range(4)]
            total = dot(jnp.concatenate(blocks, axis=1), hot_t[tile])
            total = total.astype(BF16)
            slots[0, tile, rows, :] = total[:, :T]
            slots[1, tile, rows, :] = total[:, T:]
            return carry

        lax.fori_loop(0, D // 512, some, 0)

    def slot_loader(n, first, count):
        return lambda rows: [slots[n, first + i, rows, :] for i in range(count)]

    def slot_storer(n, first, count):
        gates = []
        for i in range(count):
            got = share[n, first + i]
            under = got[1:2] + got[2:3]
            gates.append(jnp.where(under > 0.0, got[0:1] / jnp.maximum(under, 1.0), 0.0))
        gates = [jnp.broadcast_to(g, (DB, T)) for g in gates]

        def store(rows, parts):
            for i in range(count):
                slots[n, first + i, rows, :] = (parts[i] * gates[i]).astype(BF16)

        return store

    def forward(i):
        x_far[i].wait_recv()
        x_far_y[i].start()
        x_far_core[i].start()

    def relay(*numbers):
        for n in numbers:
            b_near[n].wait_recv()
            b_x[n].start()

    def last_hop(i):
        x_far_y[i].wait_recv()
        x_last[i].start()

    x_core.wait_recv()
    prepare(0)
    relay(0, 1)
    x_y.wait_recv()
    x_y_core.start()
    forward(0)
    x_y_core.wait_recv()
    prepare(1)
    pick(0)
    for copy in r_loads:
        copy.wait()
    up(1, slot_loader(0, 0, 1), a1, z_ref)
    for copy in c_x:
        copy.wait_recv()
    for copy in c_fwd:
        copy.start()
    middle(1, a2, a3, z_ref, u_ref, 0, NB)
    relay(2)
    forward(1)
    down(1, a4, u_ref, slot_storer(0, 0, 1), 0, NB // 2)
    last_hop(0)
    for copy in s_loads:
        copy.wait()
    for copy in c_core + c_fwd:
        copy.wait_recv()

    def keep_shared(rows, parts):
        shared_out[rows, :] = parts[0].astype(BF16)

    up(1, lambda rows: [x_all[0, rows, :]], c1, z_ref)
    middle(1, c2, c3, z_ref, u_ref, 0, NB // 2)
    forward(2)
    middle(1, c2, c3, z_ref, u_ref, NB // 2, NB // 2)
    last_hop(1)
    relay(3)
    down(1, c4, u_ref, keep_shared, 0, NB // 2)
    forward(3)
    for copy in x_far_core:
        copy.wait_recv()
    prepare(2)
    pick(1)
    relay(4, 5)
    up(1, slot_loader(0, 1, 1), a1, z_ref)
    last_hop(2)
    middle(1, a2, a3, z_ref, u_ref, 0, NB // 2)
    last_hop(3)
    relay(6, 7)
    middle(1, a2, a3, z_ref, u_ref, NB // 2, NB // 2)
    for copy in x_last:
        copy.wait_recv()
    prepare(3)
    pick(2)
    down(1, a4, u_ref, slot_storer(0, 1, 1), 0, NB // 2)
    up(1, slot_loader(0, 2, 1), a1, z_ref)
    relay(8, 9)
    middle(1, a2, a3, z_ref, u_ref, 0, NB)
    relay(10, 11)
    down(1, a4, u_ref, slot_storer(0, 2, 1), 0, NB // 2)
    b_there[2].wait_recv()
    up(3, slot_loader(1, 0, 3), b1, z_ref)
    here, there = x * 32, 32 - x * 32
    order = (
        (0, 0), (0, 1), (1, 0), (1, 1), (2, 0), (3, 0), (2, 1), (4, 0), (3, 1), (5, 0), (4, 1), (6, 0),
        (7, 0), (7, 1), (5, 1), (6, 1),
    )
    turns = {(0, 0): (12, 13), (2, 0): (14, 15)}
    for bit, side in order:
        start, size = BITS[bit]
        legs = (0, 1) if bit == 0 else (2 + 2 * bit, 3 + 2 * bit)
        if bit == 7:
            for n in legs:
                b_near[n + 2 * side].wait_recv()
        elif side == 1:
            for n in legs:
                b_there[n].wait_recv()
        middle(3, b2, b3, z_ref, u_ref, (there if side else here) + start, size)
        relay(*turns.get((bit, side), ()))
    b_there[3].wait_recv()

    for copy in [x_core, x_y, x_y_core] + x_far + x_far_core + x_far_y + x_last:
        copy.wait_send()

    def sum_copy(number, src, dst, i, target):
        rows = aligned(i * CHUNK, CHUNK)
        at = number * CHUNKS + i
        return remote(src.at[rows], dst.at[rows], sum_send.at[at], sum_recv.at[at], target)

    def to_core(q, i):
        return sum_copy(q, x_all.at[2 * q + 1], core_in.at[q], i, on_core)

    def to_y(q, i):
        return sum_copy(4 + q // 2, x_all.at[2 * q], y_in.at[q // 2], i, on_y)

    def to_far(i):
        return sum_copy(6, x_all.at[4], z_in, i, on_far)

    def combine(q, i):
        where = [(tile, half) for tile, half in ((q, 0), (q - 1, 1)) if 0 <= tile < 3]
        first, last = where[0][1] * 2 * T, (where[-1][1] + 1) * 2 * T
        for j in range(CHUNK // 256):
            rows = aligned(i * CHUNK + j * 256, 256)
            both = jnp.concatenate([slots[n, tile, rows, :] for tile, _ in where for n in range(2)], axis=1)
            total = dot(both, hot[q, first:last, :]).astype(BF16)
            x_all[2 * q, rows, :] = total[:, :T]
            x_all[2 * q + 1, rows, :] = total[:, T:]
        to_core(q, i).start()

    def summed(q, refs, rows):
        total = x_all[2 * q, rows, :].astype(F32)
        for ref in refs:
            total += ref[rows, :].astype(F32)
        return total

    def add(q, refs, i):
        for j in range(CHUNK // 256):
            rows = aligned(i * CHUNK + j * 256, 256)
            x_all[2 * q, rows, :] = summed(q, refs, rows).astype(BF16)

    def over_y(q, i):
        to_core(q, i).wait_recv()
        add(q, [core_in.at[q]], i)
        to_y(q, i).start()

    def over_z(i):
        to_core(2, i).wait_recv()
        to_y(3, i).wait_recv()
        add(2, [core_in.at[2], y_in.at[1]], i)
        to_far(i).start()

    store_b = slot_storer(1, 0, 3)

    def begin(i, ahead, lag):
        down(3, b4, u_ref, store_b, CHUNK // 128 * i, CHUNK // 128)
        combine(3, i)
        combine(2, i)
        if ahead:
            over_y(3, i - 1)
        if lag:
            over_z(i - LAG)

    def loop(first, last, body):
        lax.fori_loop(first, last, lambda i, carry: (body(i), carry)[1], 0)

    begin(0, False, False)
    loop(1, LAG, lambda i: begin(i, True, False))
    loop(LAG, CHUNKS, lambda i: begin(i, True, True))
    over_y(3, CHUNKS - 1)

    def further(i):
        over_z(i + CHUNKS - LAG)
        combine(1, i)

    loop(0, LAG, further)
    loop(LAG, CHUNKS, lambda i: combine(1, i))
    loop(0, CHUNKS, lambda i: over_y(1, i))
    loop(0, CHUNKS, lambda i: combine(0, i))

    def to_out(i):
        rows = aligned(i * CHUNK, CHUNK)
        return local(9 + i, out_v.at[rows], out_ref.at[rows])

    def finish(i):
        to_core(0, i).wait_recv()
        to_y(1, i).wait_recv()
        to_far(i).wait_recv()
        for j in range(CHUNK // 256):
            rows = aligned(i * CHUNK + j * 256, 256)
            total = summed(0, [core_in.at[0], y_in.at[0], shared_out, z_in], rows)
            out_v[rows, :] = total.astype(BF16)
        to_out(i).start()

    loop(0, CHUNKS, finish)

    for copy in b_near + b_x + c_core + c_x + c_fwd:
        copy.wait_send()

    def drain(i):
        for q in range(4):
            to_core(q, i).wait_send()
        to_y(1, i).wait_send()
        to_y(3, i).wait_send()
        to_far(i).wait_send()
        to_out(i).wait()

    loop(0, CHUNKS, drain)


def layer_call(tokens, expert_ids, gate_codes, shared, routed):
    hbm = pl.BlockSpec(memory_space=pl.ANY)
    vmem = pl.BlockSpec(memory_space=pltpu.VMEM)
    weights = [
        pltpu.VMEM((NB // 2, NB, 2 * DB), BF16), pltpu.VMEM((NB, NB, HB), BF16),
        pltpu.VMEM((NB, NB, HB), BF16), pltpu.VMEM((NB // 2, DB, 2 * NB), BF16),
    ]
    sems = pltpu.SemaphoreType.DMA
    block = pltpu.VMEM((D, T), BF16)
    legs = len(LEGS) + 2 + RELAYED
    routed = (routed[0], routed[1], jnp.swapaxes(routed[2], -1, -2), routed[3])
    shared = (shared[0], shared[1], jnp.swapaxes(shared[2], -1, -2), shared[3])
    return pl.pallas_call(
        layer_kernel,
        out_shape=jax.ShapeDtypeStruct((D, T), BF16),
        in_specs=[hbm, vmem, vmem] + [hbm] * 8,
        out_specs=hbm,
        scratch_shapes=[pltpu.VMEM((8, ROWS, T), BF16)]
        + weights * 3
        + [
            pltpu.VMEM((2, 3, D, T), BF16),
            pltpu.VMEM((3, D, T), F32),
            pltpu.VMEM((3, D, T), F32),
            pltpu.VMEM((4, 4 * T, 2 * T), BF16),
            pltpu.VMEM((3, 4 * T, 2 * T), BF16),
            pltpu.VMEM((2, 3, 8, T), F32),
            block,
            block,
            pltpu.VMEM((4, D, T), BF16),
            pltpu.VMEM((2, D, T), BF16),
            block,
            pltpu.VMEM((T, D), BF16),
            pltpu.VMEM((NB, DB, NB), BF16),
            pltpu.VMEM((NB, NB, DB), BF16),
            pltpu.VMEM((NB // 4, DB, NB), BF16),
            pltpu.VMEM((NB // 4, NB, DB), BF16),
            sems((9 + CHUNKS,)), sems((19,)), sems((19,)), sems((legs,)), sems((legs,)),
            sems((12,)), sems((12,)), sems((7 * CHUNKS,)), sems((7 * CHUNKS,)),
        ],
        compiler_params=pltpu.CompilerParams(
            collective_id=2, has_side_effects=True, vmem_limit_bytes=63 * 2**20
        ),
        cost_estimate=pl.CostEstimate(flops=10**11, bytes_accessed=3 * 10**8, transcendentals=0),
        name="layer",
    )(tokens, expert_ids.T, gate_codes.T, *routed, *shared).T


def running(ones, width):
    groups = ones.reshape(ones.shape[0], -1, width).astype(F32)
    inside = jnp.einsum("rgt,tu->rgu", groups, jnp.triu(jnp.ones((width, width), F32)))
    count = groups.shape[1]
    earlier = jnp.triu(jnp.ones((count, count), F32), 1)
    before = jnp.einsum("rg,gh->rh", inside[:, :, -1], earlier, precision=lax.Precision.HIGHEST)
    return (inside + before[:, :, None]).reshape(ones.shape).astype(jnp.int32)


def shards(tokens, expert_ids, gate_codes, *factors):
    shared, routed = factors[:4], factors[4:]
    residents = routed[0].shape[0]
    sources = lax.axis_size("expert")
    tok_rows = tokens.shape[0]
    if sources == 8 and lax.axis_size("dp") == 4 and residents == 2:
        return layer_call(tokens, expert_ids, gate_codes, shared, routed)
    experts_all = residents * sources
    capacity = max(2, 6 * tok_rows // experts_all)
    tiles = -(-sources * capacity // (2 * T))
    depth = tiles * 2 * T
    window = min(depth, -(-(T - 1 + 2 * capacity) // T) * T)

    extra = jnp.concatenate([expert_ids, gate_codes], axis=1).T.astype(BF16)
    extra = jnp.pad(extra, ((0, 16 - extra.shape[0]), (0, 0)))
    x_t = jnp.concatenate([tokens.T, extra], axis=0)
    x_all = gather_tokens(x_t)
    ids_all = x_all[:, D : D + 2].astype(jnp.int32)
    codes = x_all[:, D + 2 : D + 4].astype(F32)
    gates_all = codes / jnp.sum(codes, axis=1, keepdims=True)
    mine = lax.axis_index("expert") * residents + jnp.arange(residents, dtype=jnp.int32)
    match = ids_all[None] == mine[:, None, None, None]
    picked = jnp.any(match, axis=2).reshape(residents, sources * tok_rows)
    gate = jnp.sum(jnp.where(match, gates_all[None], 0.0), axis=2).reshape(residents, sources * tok_rows)
    ones = picked.astype(jnp.int32)
    ranks = running(ones, tok_rows)
    counts = ranks[:, -1]
    starts = (ranks - ones).reshape(residents, sources // 2, 2 * T)[:, :, 0]
    starts = jnp.minimum(starts, depth - window) // T
    pos = jnp.where(picked, ranks - 1, -1)
    slots = jnp.arange(depth, dtype=jnp.int32)
    slot_gates = jnp.sum(
        jnp.where(pos[:, None, :] == slots[None, :, None], gate[:, None, :], 0.0), axis=2
    ).reshape(residents, tiles, 1, 2 * T)
    pos = pos.reshape(residents, sources // 2, 1, 2 * T)

    outs = routed_call(counts, pos, slot_gates, x_all, turned(routed), tiles)
    y = combine_call(starts, pos, outs, sources, depth, window)
    sums = scatter_sums(y)
    whole = tuple(lax.all_gather(w, "dp", axis=0, tiled=True)[None] for w in turned(shared))
    shared_t = shared_call(x_t, whole)
    total = shared_t.astype(F32) + sums.astype(F32)
    return total.astype(BF16).T


def solution(mesh):
    in_specs = (
        P(("expert", "dp"), None),
        P(("expert", "dp"), None),
        P(("expert", "dp"), None),
        P("dp", None, None),
        P("dp", None, None),
        P("dp", None, None),
        P("dp", None, None),
        P("expert", None, None, None),
        P("expert", None, None, None),
        P("expert", None, None, None),
        P("expert", None, None, None),
    )
    out_specs = P(("expert", "dp"), None)
    return jax.shard_map(shards, mesh=mesh, in_specs=in_specs, out_specs=out_specs, check_vma=False)
```

```python
import functools
import math

import jax
import jax.numpy as jnp
from jax import lax
from jax.experimental import pallas as pl
from jax.experimental.pallas import tpu as pltpu
from jax.sharding import PartitionSpec as P

D = 4096
NB = 64
DB = 64
HB = 256
T = 128
F32 = jnp.float32
BF16 = jnp.bfloat16


def tile_monarch(x_ref, lanes, w1_ref, w2_ref, w3_ref, w4_ref, z_refs, u_refs, store):
    def spread(refs, rows, value):
        for i in range(lanes):
            refs[i][rows, :] = value[:, i * T : (i + 1) * T]

    def strided(refs, start):
        parts = [refs[i][pl.ds(start, NB, stride=NB), :] for i in range(lanes)]
        return jnp.concatenate(parts, axis=1).astype(BF16)

    def up(a, carry):
        rows = pl.ds(pl.multiple_of(a * DB, DB), DB)
        x = x_ref[rows, : lanes * T]
        spread(z_refs, rows, jnp.dot(w1_ref[0, a], x, preferred_element_type=F32))
        return carry

    lax.fori_loop(0, NB, up, 0, unroll=8)

    def middle(j, carry):
        hidden = jnp.dot(w2_ref[0, j], strided(z_refs, j), preferred_element_type=F32)
        hidden = (0.5 * hidden) * (1.0 + lax.erf(hidden * (0.5**0.5)))
        u = jnp.dot(w3_ref[0, j], hidden.astype(BF16), preferred_element_type=F32)
        spread(u_refs, pl.ds(pl.multiple_of(j * NB, NB), NB), u)
        return carry

    lax.fori_loop(0, NB, middle, 0, unroll=4)

    def down(k, carry):
        rows = pl.ds(pl.multiple_of(k * DB, DB), DB)
        store(rows, jnp.dot(w4_ref[0, k], strided(u_refs, k), preferred_element_type=F32))
        return carry

    lax.fori_loop(0, NB, down, 0, unroll=8)


def shared_kernel(x_ref, w1_ref, w2_ref, w3_ref, w4_ref, o_ref, z_ref, u_ref):
    def store(rows, value):
        o_ref[rows, :] = value.astype(BF16)

    tile_monarch(x_ref, 1, w1_ref, w2_ref, w3_ref, w4_ref, (z_ref,), (u_ref,), store)


def routed_kernel(
    counts_ref, pos_ref, gate_ref, x_ref, w1_ref, w2_ref, w3_ref, w4_ref,
    o_ref, x_scr, z0_ref, z1_ref, u0_ref, u1_ref,
):
    expert, tile = pl.program_id(0), pl.program_id(1)
    left = counts_ref[expert] - tile * 2 * T
    sources = x_ref.shape[0]

    @pl.when(left <= T)
    def _():
        o_ref[...] = jnp.zeros_like(o_ref)

    def serve(lanes):
        width = lanes * T
        wanted = lax.broadcasted_iota(jnp.int32, (width, 2 * T), 0) + tile * 2 * T
        step = D // 8

        for part in range(8):
            rows = pl.ds(part * step, step)

            def pick(pair, total):
                both = jnp.concatenate([x_ref[2 * pair, rows, :], x_ref[2 * pair + 1, rows, :]], axis=1)
                onehot = (wanted == pos_ref[0, pair, :, :]).astype(F32).astype(BF16)
                return total + lax.dot_general(
                    both, onehot, (((1,), (1,)), ((), ())), preferred_element_type=F32
                )

            total = lax.fori_loop(0, sources // 2, pick, jnp.zeros((step, width), F32))
            x_scr[rows, :width] = total.astype(BF16)

        gate = gate_ref[0, 0][:, :width]

        def store(rows, value):
            o_ref[rows, :width] = (value * gate).astype(BF16)

        tile_monarch(
            x_scr, lanes, w1_ref, w2_ref, w3_ref, w4_ref, (z0_ref, z1_ref), (u0_ref, u1_ref), store
        )

    @pl.when(left > T)
    def _():
        serve(2)

    @pl.when(jnp.logical_and(left > 0, left <= T))
    def _():
        serve(1)


def weight_specs(index_map, buffers=2):
    shapes = ((NB, DB), (HB, NB), (NB, HB), (DB, NB))
    mode = pl.Buffered(buffers)
    return [pl.BlockSpec((1, NB) + shape, index_map, pipeline_mode=mode) for shape in shapes]


def turned(factors):
    return tuple(jnp.swapaxes(w, -1, -2) for w in factors)


def shared_call(x_t, factors):
    return pl.pallas_call(
        shared_kernel,
        out_shape=jax.ShapeDtypeStruct((D, T), BF16),
        grid=(1,),
        in_specs=[pl.BlockSpec((D, T), lambda i: (0, 0))] + weight_specs(lambda i: (0, 0, 0, 0)),
        out_specs=pl.BlockSpec((D, T), lambda i: (0, 0)),
        scratch_shapes=[pltpu.VMEM((D, T), F32), pltpu.VMEM((D, T), F32)],
        compiler_params=pltpu.CompilerParams(vmem_limit_bytes=56 * 2**20),
        cost_estimate=pl.CostEstimate(flops=10**10, bytes_accessed=10**7, transcendentals=0),
        name="shared_expert",
    )(x_t, *factors)


def routed_call(counts, pos, slot_gates, x_all, factors, tiles):
    residents = pos.shape[0]
    sources = x_all.shape[0]
    grid_spec = pltpu.PrefetchScalarGridSpec(
        num_scalar_prefetch=1,
        grid=(residents, tiles),
        in_specs=[
            pl.BlockSpec((1, sources // 2, 1, 2 * T), lambda e, i, c: (e, 0, 0, 0)),
            pl.BlockSpec((1, 1, 1, 2 * T), lambda e, i, c: (e, i, 0, 0)),
            pl.BlockSpec((sources, x_all.shape[1], T), lambda e, i, c: (0, 0, 0), pipeline_mode=pl.Buffered(1)),
        ]
        + weight_specs(lambda e, i, c: (e, 0, 0, 0), 2 if sources <= 8 else 1),
        out_specs=pl.BlockSpec((D, 2 * T), lambda e, i, c: (0, e * tiles + i)),
        scratch_shapes=[pltpu.VMEM((D, 2 * T), BF16)] + [pltpu.VMEM((D, T), F32)] * 4,
    )
    return pl.pallas_call(
        routed_kernel,
        out_shape=jax.ShapeDtypeStruct((D, residents * tiles * 2 * T), BF16),
        grid_spec=grid_spec,
        compiler_params=pltpu.CompilerParams(vmem_limit_bytes=62 * 2**20),
        cost_estimate=pl.CostEstimate(flops=4 * 10**10, bytes_accessed=2 * 10**7, transcendentals=0),
        name="routed_experts",
    )(counts, pos, slot_gates, x_all, *factors)


def combine_kernel(depth, window, starts_ref, pos_ref, o_ref, y_ref):
    residents = starts_ref.shape[0]
    pair = pl.program_id(0)
    wanted = lax.broadcasted_iota(jnp.int32, (window, 2 * T), 0)
    begins = [pl.multiple_of(starts_ref[e, pair] * T, T) for e in range(residents)]
    hots = [
        (wanted + begins[e] == pos_ref[e, 0, :, :]).astype(F32).astype(BF16) for e in range(residents)
    ]
    hot = jnp.concatenate(hots, axis=0)
    step = 512

    def part(i, carry):
        rows = pl.ds(pl.multiple_of(i * step, step), step)
        near = [
            o_ref[rows, pl.ds(pl.multiple_of(begins[e] + e * depth, T), window)] for e in range(residents)
        ]
        total = jnp.dot(jnp.concatenate(near, axis=1), hot, preferred_element_type=F32).astype(BF16)
        y_ref[0, rows, :] = total[:, :T]
        y_ref[1, rows, :] = total[:, T:]
        return carry

    lax.fori_loop(0, D // step, part, 0)


def combine_call(starts, pos, outs, sources, depth, window):
    residents = pos.shape[0]
    grid_spec = pltpu.PrefetchScalarGridSpec(
        num_scalar_prefetch=1,
        grid=(sources // 2,),
        in_specs=[
            pl.BlockSpec((residents, 1, 1, 2 * T), lambda s, c: (0, s, 0, 0)),
            pl.BlockSpec((D, residents * depth), lambda s, c: (0, 0), pipeline_mode=pl.Buffered(1)),
        ],
        out_specs=pl.BlockSpec((2, D, T), lambda s, c: (s, 0, 0)),
    )
    return pl.pallas_call(
        functools.partial(combine_kernel, depth, window),
        out_shape=jax.ShapeDtypeStruct((sources, D, T), BF16),
        grid_spec=grid_spec,
        compiler_params=pltpu.CompilerParams(vmem_limit_bytes=48 * 2**20),
        name="combine",
    )(starts, pos, outs)


def grid_of(count):
    side = math.isqrt(count // 2)
    return count // side, side


def greet(z, y, nz, ny):
    barrier = pltpu.get_barrier_semaphore()
    for other in range(1, ny):
        pl.semaphore_signal(barrier, inc=1, device_id={"expert": z * ny + lax.rem(y + other, ny)})

    @pl.when(z > 0)
    def _():
        pl.semaphore_signal(barrier, inc=1, device_id={"expert": (z - 1) * ny + y})

    @pl.when(z < nz - 1)
    def _():
        pl.semaphore_signal(barrier, inc=1, device_id={"expert": (z + 1) * ny + y})

    peers = ny - 1 + jnp.where(z > 0, 1, 0) + jnp.where(z < nz - 1, 1, 0)
    pl.semaphore_wait(barrier, peers)


def gather_kernel(nz, x_ref, out_ref, own_sem, up_sem, down_sem, side_sem, recv_sem):
    ny = 2
    me = lax.axis_index("expert")
    z, y = me // ny, lax.rem(me, ny)
    beside = z * ny + (1 - y)

    def send(block, src, sem, target):
        return pltpu.make_async_remote_copy(
            src_ref=src, dst_ref=out_ref.at[block], send_sem=sem.at[block],
            recv_sem=recv_sem.at[block], device_id={"expert": target},
        )

    def arrived(block):
        send(block, out_ref.at[block], side_sem, beside).wait_recv()

    greet(z, y, nz, ny)
    own = pltpu.make_async_copy(x_ref, out_ref.at[me], own_sem)
    own.start()

    @pl.when(z < nz - 1)
    def _():
        send(me, x_ref, up_sem, me + ny).start()

    @pl.when(z > 0)
    def _():
        send(me, x_ref, down_sem, me - ny).start()

    send(me, x_ref, side_sem, beside).start()

    for k in range(1, nz):
        block = me - k * ny

        @pl.when(z >= k)
        def _():
            arrived(block)

            @pl.when(z < nz - 1)
            def _():
                send(block, out_ref.at[block], up_sem, me + ny).start()

            send(block, out_ref.at[block], side_sem, beside).start()

        later = me + k * ny

        @pl.when(z + k < nz)
        def _():
            arrived(later)

            @pl.when(z > 0)
            def _():
                send(later, out_ref.at[later], down_sem, me - ny).start()

            send(later, out_ref.at[later], side_sem, beside).start()

    for other in range(nz):
        arrived(other * ny + (1 - y))
    own.wait()
    for other in range(nz):
        block = other * ny + y
        send(block, out_ref.at[block], side_sem, beside).wait_send()

        @pl.when(jnp.logical_and(other <= z, z < nz - 1))
        def _():
            send(block, out_ref.at[block], up_sem, me + ny).wait_send()

        @pl.when(jnp.logical_and(other >= z, z > 0))
        def _():
            send(block, out_ref.at[block], down_sem, me - ny).wait_send()


def gather_tokens(x_t):
    count = lax.axis_size("expert")
    nz, ny = grid_of(count)
    if ny != 2:
        return lax.all_gather(x_t, "expert", axis=0, tiled=False)
    sems = pltpu.SemaphoreType.DMA((count,))
    return pl.pallas_call(
        functools.partial(gather_kernel, nz),
        out_shape=jax.ShapeDtypeStruct((count,) + x_t.shape, x_t.dtype),
        in_specs=[pl.BlockSpec(memory_space=pl.ANY)],
        out_specs=pl.BlockSpec(memory_space=pl.ANY),
        scratch_shapes=[pltpu.SemaphoreType.DMA, sems, sems, sems, sems],
        compiler_params=pltpu.CompilerParams(collective_id=0, has_side_effects=True),
        cost_estimate=pl.CostEstimate(flops=10**11, bytes_accessed=3 * 10**8, transcendentals=0),
        name="gather_tokens",
    )(x_t)


def scatter_kernel(
    nz, y_hbm, out_ref, held, beside_in, below_in, above_in,
    load_sem, side_sem, side_recv, up_sem, up_recv, down_sem, down_recv,
):
    ny = 2
    me = lax.axis_index("expert")
    z, y = me // ny, lax.rem(me, ny)
    beside = z * ny + (1 - y)

    def load(target):
        return pltpu.make_async_copy(y_hbm.at[target * ny + y], held.at[target], load_sem.at[target])

    def side(target):
        return pltpu.make_async_remote_copy(
            src_ref=y_hbm.at[target * ny + (1 - y)], dst_ref=beside_in.at[target],
            send_sem=side_sem.at[target], recv_sem=side_recv.at[target],
            device_id={"expert": beside},
        )

    def up(target):
        return pltpu.make_async_remote_copy(
            src_ref=held.at[target], dst_ref=below_in.at[target], send_sem=up_sem.at[target],
            recv_sem=up_recv.at[target], device_id={"expert": me + ny},
        )

    def down(target):
        return pltpu.make_async_remote_copy(
            src_ref=held.at[target], dst_ref=above_in.at[target], send_sem=down_sem.at[target],
            recv_sem=down_recv.at[target], device_id={"expert": me - ny},
        )

    def add(target, ref):
        step = 512

        def body(i, carry):
            rows = pl.ds(pl.multiple_of(i * step, step), step)
            total = held[target, rows, :].astype(F32) + ref[target, rows, :].astype(F32)
            held[target, rows, :] = total.astype(BF16)
            return carry

        lax.fori_loop(0, D // step, body, 0)

    greet(z, y, nz, ny)
    for k in range(nz - 1, -1, -1):
        @pl.when(z + k < nz)
        def _():
            side(z + k).start()

        if k > 0:
            @pl.when(z - k >= 0)
            def _():
                side(z - k).start()

    for target in range(nz):
        load(target).start()
    for target in range(nz):
        load(target).wait()
    for k in range(nz - 1, 0, -1):
        target = z + k

        @pl.when(z + k < nz)
        def _():
            side(target).wait_recv()
            add(target, beside_in)

            @pl.when(z > 0)
            def _():
                up(target).wait_recv()
                add(target, below_in)

            up(target).start()

        lower = z - k

        @pl.when(z - k >= 0)
        def _():
            side(lower).wait_recv()
            add(lower, beside_in)

            @pl.when(z < nz - 1)
            def _():
                down(lower).wait_recv()
                add(lower, above_in)

            down(lower).start()

    side(z).wait_recv()
    add(z, beside_in)

    @pl.when(z > 0)
    def _():
        up(z).wait_recv()
        add(z, below_in)

    @pl.when(z < nz - 1)
    def _():
        down(z).wait_recv()
        add(z, above_in)

    out_ref[...] = held[z]
    for target in range(nz):
        side(target).wait_send()

        @pl.when(target > z)
        def _():
            up(target).wait_send()

        @pl.when(target < z)
        def _():
            down(target).wait_send()


def scatter_sums(sums):
    count = lax.axis_size("expert")
    nz, ny = grid_of(count)
    if ny != 2:
        return lax.psum_scatter(sums, "expert", scatter_dimension=0, tiled=False)
    block = pltpu.VMEM((nz,) + sums.shape[1:], sums.dtype)
    sems = pltpu.SemaphoreType.DMA((nz,))
    return pl.pallas_call(
        functools.partial(scatter_kernel, nz),
        out_shape=jax.ShapeDtypeStruct(sums.shape[1:], sums.dtype),
        in_specs=[pl.BlockSpec(memory_space=pl.ANY)],
        out_specs=pl.BlockSpec(memory_space=pltpu.VMEM),
        scratch_shapes=[block] * 4 + [sems] * 7,
        compiler_params=pltpu.CompilerParams(
            collective_id=1, has_side_effects=True, vmem_limit_bytes=40 * 2**20
        ),
        cost_estimate=pl.CostEstimate(flops=10**11, bytes_accessed=3 * 10**8, transcendentals=0),
        name="scatter_sums",
    )(sums)


ROWS = D + 16
CAP = 48
CHUNK = 256
CHUNKS = D // CHUNK
LAG = 6
SPANS = ((0, 1024), (1024, 1024), (2048, 1280), (3328, ROWS - 3328))
BITS = ((0, 8), (8, 4), (12, 4), (16, 4), (20, 4), (24, 4), (28, 1), (29, 3))
LEGS = ((1, *BITS[0]), (2, *BITS[0]), (0, 0, 16), (3, 0, 16)) + tuple((w, *b) for b in BITS[1:] for w in (1, 2))
RELAYED = len(LEGS) - 2


def dot(a, b):
    return jnp.dot(a, b, preferred_element_type=F32)


def dot_turned(w, x):
    return lax.dot_general(w, x, (((0,), (0,)), ((), ())), preferred_element_type=F32)


def gelu(hidden):
    return ((0.5 * hidden) * (1.0 + lax.erf(hidden * (0.5**0.5)))).astype(BF16)


def aligned(start, step):
    return pl.ds(pl.multiple_of(start, step), step)


def apart(upper, lower):
    top, bottom = [], []
    for a, b in zip(upper, lower):
        top += [a, jnp.zeros_like(a)]
        bottom += [jnp.zeros_like(b), b]
    return jnp.concatenate([jnp.concatenate(top, axis=1), jnp.concatenate(bottom, axis=1)], axis=0)


def strided(ref, tiles, start):
    return [ref[i, pl.ds(start, NB, stride=NB), :].astype(BF16) for i in range(tiles)]


def up(tiles, load, w1, z_ref):
    def some(i, carry):
        for q in range(4):
            p = i * 4 + q
            parts = load(aligned(p * 2 * DB, 2 * DB))
            value = dot(w1[p], apart([x[:DB] for x in parts], [x[DB:] for x in parts]))
            for t in range(tiles):
                for side in range(2):
                    at = 2 * t + side
                    z_ref[t, aligned((2 * p + side) * DB, DB), :] = value[:, at * T : (at + 1) * T]
        return carry

    lax.fori_loop(0, NB // 8, some, 0)


def middle(tiles, w2, w3, z_ref, u_ref, first, count):
    batch = min(count, 8 if tiles == 1 else 4)

    def some(i, carry):
        blocks = [first + i * batch + q for q in range(batch)]
        hidden = []
        for j in blocks:
            parts = strided(z_ref, tiles, j)
            rows = parts[0] if tiles == 1 else jnp.concatenate(parts, axis=1)
            hidden.append(gelu(dot_turned(w2[j], rows)))
        for j, h in zip(blocks, hidden):
            value = dot(w3[j], h)
            for t in range(tiles):
                u_ref[t, aligned(j * NB, NB), :] = value[:, t * T : (t + 1) * T]
        return carry

    lax.fori_loop(0, count // batch, some, 0)


def down(tiles, w4, u_ref, store, first, count):
    batch = min(count, 4)

    def some(i, carry):
        for q in range(batch):
            p = first + i * batch + q
            value = dot(w4[p], apart(strided(u_ref, tiles, 2 * p), strided(u_ref, tiles, 2 * p + 1)))
            for side in range(2):
                parts = [value[:, (2 * t + side) * T : (2 * t + side + 1) * T] for t in range(tiles)]
                store(aligned((2 * p + side) * DB, DB), parts)
        return carry

    lax.fori_loop(0, count // batch, some, 0)


def pack_pairs(src, dst, first, count):
    def some(i, carry):
        for q in range(4):
            p = i * 4 + q
            both = jnp.concatenate([src[2 * p], src[2 * p + 1]], axis=0)
            dst[first + p] = both.T
        return carry

    lax.fori_loop(0, count // 4, some, 0)


def layer_kernel(
    tok, ids, codes, r1, r2, r3, r4, s1, s2, s3, s4, out_ref,
    x_all, a1, a2, a3, a4, b1, b2, b3, b4, c1, c2, c3, c4,
    slots, z_ref, u_ref, hot, hot_t, share, shared_out, out_v, core_in, y_in, z_in,
    tok_in, r1_in, r4_in, s1_in, s4_in,
    local_sem, x_send, x_recv, b_send, b_recv, c_send, c_recv, sum_recv,
):
    e, d = lax.axis_index("expert"), lax.axis_index("dp")
    z, y, x, c = e // 2, lax.rem(e, 2), d // 2, lax.rem(d, 2)
    near_z = e + 2 - 4 * lax.rem(z, 2)
    on_far = {"expert": lax.rem(e + 4, 8), "dp": d}
    on_near = {"expert": near_z, "dp": d}
    on_y = {"expert": e + 1 - 2 * y, "dp": d}
    on_core = {"expert": e, "dp": d + 1 - 2 * c}
    on_x = {"expert": e, "dp": lax.rem(d + 2, 4)}
    own_a, own_b, own_s = (a1, a2, a3, a4), (b1, b2, b3, b4), (c1, c2, c3, c4)

    def remote(src, dst, send, recv, target):
        return pltpu.make_async_remote_copy(
            src_ref=src, dst_ref=dst, send_sem=send, recv_sem=recv, device_id=target
        )

    def x_copy(number, source, slot, rows, target):
        return remote(
            x_all.at[source, rows], x_all.at[slot, rows], x_send.at[number], x_recv.at[number], target
        )

    whole = pl.ds(0, ROWS)
    spans = [pl.ds(*s) for s in SPANS]
    x_core = x_copy(0, 0, 1, whole, on_core)
    x_y = x_copy(1, 0, 2, whole, on_y)
    x_far = [x_copy(2 + i, 0, 4, rows, on_far) for i, rows in enumerate(spans)]
    x_y_core = x_copy(6, 2, 3, whole, on_core)
    x_far_core = [x_copy(7 + i, 4, 5, rows, on_core) for i, rows in enumerate(spans)]
    x_far_y = [x_copy(11 + i, 4, 6, rows, on_y) for i, rows in enumerate(spans)]
    x_last = [x_copy(15 + i, 6, 7, rows, on_core) for i, rows in enumerate(spans)]

    def leg(number, half, first, spare=0):
        w, start, size = LEGS[number]
        rows = pl.ds(half * (16 if w in (0, 3) else 32) + start, size)
        src = (a1, r2.at[c], r3.at[c], a4)[w] if first else own_b[w]
        at = number + spare if first else number + len(LEGS) + 2
        return remote(
            src.at[rows], own_b[w].at[rows], b_send.at[at], b_recv.at[at], on_near if first else on_x
        )

    b_near = [leg(n, x, True) for n in range(len(LEGS))]
    b_near += [leg(n, 1 - x, True, 2) for n in range(RELAYED, len(LEGS))]
    b_x = [leg(n, x, False) for n in range(RELAYED)]
    b_there = [leg(n, 1 - x, False) for n in range(RELAYED)]

    def quarter(w, at, number, target, src=None):
        size = 8 if w in (0, 3) else 16
        rows = pl.ds(at * size, size)
        src = own_s[w].at[rows] if src is None else src
        return remote(src, own_s[w].at[rows], c_send.at[number], c_recv.at[number], target)

    sources = (None, s2, s3, None)
    c_core = [quarter(w, d, w, on_core, sources[w]) for w in range(4)]
    c_x = [quarter(w, d, 4 + w, on_x, sources[w]) for w in range(4)]
    c_fwd = [quarter(w, lax.rem(d + 2, 4), 8 + w, on_core) for w in range(4)]

    def local(number, src, dst):
        return pltpu.make_async_copy(src, dst, local_sem.at[number])

    here_s = pl.ds(d * 16, 16)
    tok_load = local(0, tok, tok_in)
    r1_load = local(1, r1.at[c], r1_in)
    r4_load = local(2, r4.at[c], r4_in)
    r_loads = [local(3, r2.at[c], a2), local(4, r3.at[c], a3)]
    s_packs = [local(5, s1, s1_in), local(6, s4, s4_in)]
    s_loads = [local(7, s2, c2.at[here_s]), local(8, s3, c3.at[here_s])]
    for copy in [tok_load, r1_load, r4_load] + s_packs:
        copy.start()

    barrier = pltpu.get_barrier_semaphore()
    for target in (on_far, on_near, on_y, on_core, on_x):
        pl.semaphore_signal(barrier, inc=1, device_id=target)
    pl.semaphore_wait(barrier, 5)

    b_near[0].start()
    b_near[1].start()
    for copy in s_packs:
        copy.wait()
    pack_pairs(s1_in, c1, d * 8, 8)
    for w in range(3):
        c_x[w].start()
    numbers = [ref[...].astype(F32) for ref in (ids, codes)]
    extra = jnp.concatenate(numbers + [jnp.zeros((ROWS - D - 4, T), F32)], axis=0)
    x_all[0, D:ROWS, :] = extra.astype(BF16)
    tok_load.wait()
    for i in range(4):
        for at in range(SPANS[i][0], min(D, sum(SPANS[i])), 256):
            x_all[0, at : at + 256, :] = tok_in[:, at : at + 256].T
        x_far[i].start()
    x_y.start()
    x_core.start()
    r1_load.wait()
    pack_pairs(r1_in, a1, 0, 32)
    b_near[2].start()
    r4_load.wait()
    pack_pairs(r4_in, a4, 0, 32)
    for copy in b_near[3:]:
        copy.start()
    pack_pairs(s4_in, c4, d * 8, 8)
    c_x[3].start()
    for copy in c_core + r_loads + s_loads:
        copy.start()

    ids_a = (2 * e + c).astype(F32)
    ids_b = (2 * near_z + c).astype(F32)

    def prepare(q):
        extra = jnp.concatenate(
            [x_all[2 * q, D:ROWS, :].astype(F32), x_all[2 * q + 1, D:ROWS, :].astype(F32)], axis=1
        )
        id0, id1, code0, code1 = (extra[i : i + 1] for i in range(4))
        lane = lax.broadcasted_iota(jnp.int32, (1, 2 * T), 1)
        before = lax.broadcasted_iota(jnp.int32, (2 * T, 2 * T), 0)
        after = lax.broadcasted_iota(jnp.int32, (2 * T, 2 * T), 1)
        tri = jnp.logical_and(before < after, (before < T) == (after < T))
        tri = tri.astype(F32).astype(BF16)
        row8 = lax.broadcasted_iota(jnp.int32, (8, 2 * T), 0)
        picks = [jnp.logical_or(id0 == n, id1 == n) for n in (ids_a, ids_b)]
        names = [jnp.where(p, 1.0, 0.0) for p in picks]
        codes = [jnp.where(id0 == n, code0, code1) for n in (ids_a, ids_b)]
        stacked = jnp.where(row8 == 0, names[0], jnp.where(row8 == 1, names[1], 0.0))
        ranks = dot(stacked.astype(BF16), tri)
        base = jnp.where(lane < T, 2 * q * CAP, (2 * q + 1) * CAP).astype(F32)
        places = [
            jnp.where(picks[n], ranks[n : n + 1] + base, -1000.0).astype(jnp.int32) for n in range(2)
        ]
        for tile, half in ((q, 0), (q - 1, 1)):
            if not 0 <= tile < 3:
                continue
            wanted = lax.broadcasted_iota(jnp.int32, (T, 2 * T), 0) + tile * T
            for n in range(2):
                own = (wanted == places[n]).astype(F32).astype(BF16)
                hot[q, half * 2 * T + n * T : half * 2 * T + (n + 1) * T, :] = own
                hot_t[tile, half * 2 * T : (half + 1) * 2 * T, n * T : (n + 1) * T] = own.T
                values = jnp.where(
                    row8 == 0, codes[n], jnp.where(row8 == 1, code0, jnp.where(row8 == 2, code1, 0.0))
                )
                got = lax.dot_general(
                    values.astype(BF16), own, (((1,), (1,)), ((), ())), preferred_element_type=F32
                )
                if half == 0:
                    share[n, tile] = got
                else:
                    share[n, tile] += got

    def pick(tile):
        def some(i, carry):
            rows = aligned(i * 512, 512)
            blocks = [x_all[2 * tile + n, rows, :] for n in range(4)]
            total = dot(jnp.concatenate(blocks, axis=1), hot_t[tile])
            total = total.astype(BF16)
            slots[0, tile, rows, :] = total[:, :T]
            slots[1, tile, rows, :] = total[:, T:]
            return carry

        lax.fori_loop(0, D // 512, some, 0)

    def slot_loader(n, first, count):
        return lambda rows: [slots[n, first + i, rows, :] for i in range(count)]

    def slot_storer(n, first, count):
        gates = []
        for i in range(count):
            got = share[n, first + i]
            under = got[1:2] + got[2:3]
            gates.append(jnp.where(under > 0.0, got[0:1] / jnp.maximum(under, 1.0), 0.0))
        gates = [jnp.broadcast_to(g, (DB, T)) for g in gates]

        def store(rows, parts):
            for i in range(count):
                slots[n, first + i, rows, :] = (parts[i] * gates[i]).astype(BF16)

        return store

    def forward(i):
        x_far[i].wait_recv()
        x_far_y[i].start()
        x_far_core[i].start()

    def relay(*numbers):
        for n in numbers:
            b_near[n].wait_recv()
            b_x[n].start()

    def last_hop(i):
        x_far_y[i].wait_recv()
        x_last[i].start()

    here, there = x * 32, 32 - x * 32
    z_s, u_s = z_ref.at[pl.ds(1, 1)], u_ref.at[pl.ds(1, 1)]
    x_core.wait_recv()
    prepare(0)
    for copy in s_loads:
        copy.wait()
    for copy in c_core:
        copy.wait_recv()
    c_x[0].wait_recv()
    c_fwd[0].start()
    c_fwd[0].wait_recv()
    up(1, lambda rows: [x_all[0, rows, :]], c1, z_s)
    middle(1, c2, c3, z_s, u_s, here, NB // 2)
    relay(0, 1)
    x_y.wait_recv()
    x_y_core.start()
    forward(0)
    x_y_core.wait_recv()
    prepare(1)
    pick(0)
    for copy in r_loads:
        copy.wait()
    up(1, slot_loader(0, 0, 1), a1, z_ref)
    for copy in c_x[1:]:
        copy.wait_recv()
    for copy in c_fwd[1:]:
        copy.start()
    middle(1, a2, a3, z_ref, u_ref, 0, NB)
    relay(2)
    forward(1)
    down(1, a4, u_ref, slot_storer(0, 0, 1), 0, NB // 2)
    last_hop(0)
    for copy in c_fwd[1:]:
        copy.wait_recv()

    def keep_shared(rows, parts):
        shared_out[rows, :] = parts[0].astype(BF16)

    middle(1, c2, c3, z_s, u_s, there, NB // 2)
    forward(2)
    down(1, c4, u_s, keep_shared, 0, NB // 2)
    last_hop(1)
    relay(3)
    forward(3)
    for copy in x_far_core:
        copy.wait_recv()
    prepare(2)
    pick(1)
    up(1, slot_loader(0, 1, 1), a1, z_ref)
    middle(1, a2, a3, z_ref, u_ref, 0, NB // 2)
    relay(4, 5)
    last_hop(2)
    middle(1, a2, a3, z_ref, u_ref, NB // 2, NB // 2)
    last_hop(3)
    down(1, a4, u_ref, slot_storer(0, 1, 1), 0, NB // 2)
    relay(6, 7)
    for copy in x_last:
        copy.wait_recv()
    prepare(3)
    pick(2)
    up(1, slot_loader(0, 2, 1), a1, z_ref)
    middle(1, a2, a3, z_ref, u_ref, 0, NB // 2)
    relay(8, 9)
    middle(1, a2, a3, z_ref, u_ref, NB // 2, NB // 2)
    down(1, a4, u_ref, slot_storer(0, 2, 1), 0, NB // 2)
    relay(10, 11)
    b_there[2].wait_recv()
    up(3, slot_loader(1, 0, 3), b1, z_ref)
    z_two, u_two = z_ref.at[pl.ds(1, 2)], u_ref.at[pl.ds(1, 2)]

    def blocks_of(bit, side):
        start, size = BITS[bit]
        return (there if side else here) + start, size

    def feed(tiles, bit, side):
        for n in (0, 1) if bit == 0 else (2 + 2 * bit, 3 + 2 * bit):
            if bit == len(BITS) - 1:
                b_near[n + 2 * side].wait_recv()
            elif side == 1:
                b_there[n].wait_recv()
        z_own, u_own = (z_ref, u_ref) if tiles == 3 else (z_two, u_two)
        middle(tiles, b2, b3, z_own, u_own, *blocks_of(bit, side))

    feed(3, 0, 0)
    feed(3, 0, 1)
    relay(12, 13)
    feed(3, 1, 0)
    feed(3, 1, 1)
    feed(3, 2, 0)
    relay(14, 15)
    feed(3, 2, 1)
    feed(3, 3, 0)
    feed(3, 3, 1)
    feed(3, 4, 0)
    feed(3, 4, 1)
    feed(2, 5, 0)
    feed(2, 6, 0)
    feed(2, 7, 0)
    feed(2, 7, 1)
    feed(2, 5, 1)
    feed(2, 6, 1)
    b_there[3].wait_recv()

    for copy in [x_core, x_y, x_y_core] + x_far + x_far_core + x_far_y + x_last:
        copy.wait_send()

    for copy in b_near + b_x + c_core + c_x + c_fwd:
        copy.wait_send()

    def sum_copy(at, src, dst, i, size, target):
        rows = aligned(i * size, size)
        return remote(src.at[rows], dst.at[rows], b_send.at[at], sum_recv.at[at], target)

    def to_core(q, i):
        at = i + (8 + CHUNKS * (q - 2) if q > 1 else 4 * q)
        return sum_copy(at, x_all.at[2 * q + 1], core_in.at[q], i, CHUNK if q > 1 else 1024, on_core)

    def to_y(q, i):
        at = 8 + 2 * CHUNKS + i + (4 if q > 1 else 0)
        return sum_copy(at, x_all.at[2 * q], y_in.at[q // 2], i, CHUNK if q > 1 else 1024, on_y)

    def to_far(i):
        return sum_copy(12 + 3 * CHUNKS + i, x_all.at[4], z_in, i, CHUNK, on_far)

    def combine(q, i):
        where = [(tile, half) for tile, half in ((q, 0), (q - 1, 1)) if 0 <= tile < 3]
        first, last = where[0][1] * 2 * T, (where[-1][1] + 1) * 2 * T
        size = CHUNK if q > 1 else 1024
        for j in range(size // 256):
            rows = aligned(i * size + j * 256, 256)
            both = jnp.concatenate([slots[n, tile, rows, :] for tile, _ in where for n in range(2)], axis=1)
            total = dot(both, hot[q, first:last, :]).astype(BF16)
            x_all[2 * q, rows, :] = total[:, :T]
            x_all[2 * q + 1, rows, :] = total[:, T:]
        to_core(q, i).start()

    def summed(q, refs, rows):
        total = x_all[2 * q, rows, :].astype(F32)
        for ref in refs:
            total += ref[rows, :].astype(F32)
        return total

    def add(q, refs, i):
        size = CHUNK if q > 1 else 1024
        for j in range(size // 256):
            rows = aligned(i * size + j * 256, 256)
            x_all[2 * q, rows, :] = summed(q, refs, rows).astype(BF16)

    def over_y(q, i):
        to_core(q, i).wait_recv()
        add(q, [core_in.at[q]], i)
        to_y(q, i).start()

    def over_z(i):
        to_core(2, i).wait_recv()
        to_y(3, i).wait_recv()
        add(2, [core_in.at[2], y_in.at[1]], i)
        to_far(i).start()

    store_b = slot_storer(1, 1, 2)

    def begin(i, ahead, lag):
        down(2, b4, u_two, store_b, CHUNK // 128 * i, CHUNK // 128)
        combine(3, i)
        if ahead:
            over_y(3, i - 1)
        combine(2, i)
        if lag:
            over_z(i - LAG)

    def loop(first, last, body):
        lax.fori_loop(first, last, lambda i, carry: (body(i), carry)[1], 0)

    begin(0, False, False)
    loop(1, LAG, lambda i: begin(i, True, False))
    loop(LAG, CHUNKS, lambda i: begin(i, True, True))
    over_y(3, CHUNKS - 1)
    z_one, u_one = z_ref.at[pl.ds(0, 1)], u_ref.at[pl.ds(0, 1)]
    for half in (here, there):
        middle(1, b2, b3, z_one, u_one, half + BITS[5][0], 32 - BITS[5][0])
    down(1, b4, u_one, slot_storer(1, 0, 1), 0, NB // 2)
    over_z(CHUNKS - LAG)
    loop(0, 4, lambda i: combine(1, i))
    over_z(CHUNKS - LAG + 1)
    loop(0, 4, lambda i: over_y(1, i))
    loop(CHUNKS - LAG + 2, CHUNKS, over_z)
    loop(0, 4, lambda i: combine(0, i))
    for i in range(4):
        to_core(0, i).wait_recv()
        to_y(1, i).wait_recv()

    def to_out(i):
        rows = aligned(i * CHUNK, CHUNK)
        return pltpu.make_async_copy(out_v.at[rows], out_ref.at[rows], x_send.at[i])

    def finish(i):
        to_far(i).wait_recv()
        for j in range(CHUNK // 256):
            rows = aligned(i * CHUNK + j * 256, 256)
            total = summed(0, [core_in.at[0], y_in.at[0], shared_out, z_in], rows)
            out_v[rows, :] = total.astype(BF16)
        to_out(i).start()

    loop(0, CHUNKS, finish)

    def drain(i):
        to_core(2, i).wait_send()
        to_core(3, i).wait_send()
        to_y(3, i).wait_send()
        to_far(i).wait_send()
        to_out(i).wait()

    for i in range(4):
        to_core(0, i).wait_send()
        to_core(1, i).wait_send()
        to_y(1, i).wait_send()
    loop(0, CHUNKS, drain)


def layer_call(tokens, expert_ids, gate_codes, shared, routed):
    hbm = pl.BlockSpec(memory_space=pl.ANY)
    vmem = pl.BlockSpec(memory_space=pltpu.VMEM)
    weights = [
        pltpu.VMEM((NB // 2, NB, 2 * DB), BF16), pltpu.VMEM((NB, NB, HB), BF16),
        pltpu.VMEM((NB, NB, HB), BF16), pltpu.VMEM((NB // 2, DB, 2 * NB), BF16),
    ]
    sems = pltpu.SemaphoreType.DMA
    block = pltpu.VMEM((D, T), BF16)
    legs, sums = len(LEGS) + 2 + RELAYED, 12 + 4 * CHUNKS
    routed = (routed[0], routed[1], jnp.swapaxes(routed[2], -1, -2), routed[3])
    shared = (shared[0], shared[1], jnp.swapaxes(shared[2], -1, -2), shared[3])
    return pl.pallas_call(
        layer_kernel,
        out_shape=jax.ShapeDtypeStruct((D, T), BF16),
        in_specs=[hbm, vmem, vmem] + [hbm] * 8,
        out_specs=hbm,
        scratch_shapes=[pltpu.VMEM((8, ROWS, T), BF16)]
        + weights * 3
        + [
            pltpu.VMEM((2, 3, D, T), BF16),
            pltpu.VMEM((3, D, T), F32),
            pltpu.VMEM((3, D, T), F32),
            pltpu.VMEM((4, 4 * T, 2 * T), BF16),
            pltpu.VMEM((3, 4 * T, 2 * T), BF16),
            pltpu.VMEM((2, 3, 8, T), F32),
            block,
            block,
            pltpu.VMEM((4, D, T), BF16),
            pltpu.VMEM((2, D, T), BF16),
            block,
            pltpu.VMEM((T, D), BF16),
            pltpu.VMEM((NB, DB, NB), BF16),
            pltpu.VMEM((NB, NB, DB), BF16),
            pltpu.VMEM((NB // 4, DB, NB), BF16),
            pltpu.VMEM((NB // 4, NB, DB), BF16),
            sems((9,)), sems((19,)), sems((19,)), sems((max(legs, sums),)), sems((legs,)),
            sems((12,)), sems((12,)), sems((sums,)),
        ],
        compiler_params=pltpu.CompilerParams(
            collective_id=2, has_side_effects=True, vmem_limit_bytes=63 * 2**20
        ),
        cost_estimate=pl.CostEstimate(flops=10**11, bytes_accessed=3 * 10**8, transcendentals=0),
        name="layer",
    )(tokens, expert_ids.T, gate_codes.T, *routed, *shared).T


def running(ones, width):
    groups = ones.reshape(ones.shape[0], -1, width).astype(F32)
    inside = jnp.einsum("rgt,tu->rgu", groups, jnp.triu(jnp.ones((width, width), F32)))
    count = groups.shape[1]
    earlier = jnp.triu(jnp.ones((count, count), F32), 1)
    before = jnp.einsum("rg,gh->rh", inside[:, :, -1], earlier, precision=lax.Precision.HIGHEST)
    return (inside + before[:, :, None]).reshape(ones.shape).astype(jnp.int32)


def shards(tokens, expert_ids, gate_codes, *factors):
    shared, routed = factors[:4], factors[4:]
    residents = routed[0].shape[0]
    sources = lax.axis_size("expert")
    tok_rows = tokens.shape[0]
    if sources == 8 and lax.axis_size("dp") == 4 and residents == 2:
        return layer_call(tokens, expert_ids, gate_codes, shared, routed)
    experts_all = residents * sources
    capacity = max(2, 6 * tok_rows // experts_all)
    tiles = -(-sources * capacity // (2 * T))
    depth = tiles * 2 * T
    window = min(depth, -(-(T - 1 + 2 * capacity) // T) * T)

    extra = jnp.concatenate([expert_ids, gate_codes], axis=1).T.astype(BF16)
    extra = jnp.pad(extra, ((0, 16 - extra.shape[0]), (0, 0)))
    x_t = jnp.concatenate([tokens.T, extra], axis=0)
    x_all = gather_tokens(x_t)
    ids_all = x_all[:, D : D + 2].astype(jnp.int32)
    codes = x_all[:, D + 2 : D + 4].astype(F32)
    gates_all = codes / jnp.sum(codes, axis=1, keepdims=True)
    mine = lax.axis_index("expert") * residents + jnp.arange(residents, dtype=jnp.int32)
    match = ids_all[None] == mine[:, None, None, None]
    picked = jnp.any(match, axis=2).reshape(residents, sources * tok_rows)
    gate = jnp.sum(jnp.where(match, gates_all[None], 0.0), axis=2).reshape(residents, sources * tok_rows)
    ones = picked.astype(jnp.int32)
    ranks = running(ones, tok_rows)
    counts = ranks[:, -1]
    starts = (ranks - ones).reshape(residents, sources // 2, 2 * T)[:, :, 0]
    starts = jnp.minimum(starts, depth - window) // T
    pos = jnp.where(picked, ranks - 1, -1)
    slots = jnp.arange(depth, dtype=jnp.int32)
    slot_gates = jnp.sum(
        jnp.where(pos[:, None, :] == slots[None, :, None], gate[:, None, :], 0.0), axis=2
    ).reshape(residents, tiles, 1, 2 * T)
    pos = pos.reshape(residents, sources // 2, 1, 2 * T)

    outs = routed_call(counts, pos, slot_gates, x_all, turned(routed), tiles)
    y = combine_call(starts, pos, outs, sources, depth, window)
    sums = scatter_sums(y)
    whole = tuple(lax.all_gather(w, "dp", axis=0, tiled=True)[None] for w in turned(shared))
    shared_t = shared_call(x_t, whole)
    total = shared_t.astype(F32) + sums.astype(F32)
    return total.astype(BF16).T


def solution(mesh):
    in_specs = (
        P(("expert", "dp"), None),
        P(("expert", "dp"), None),
        P(("expert", "dp"), None),
        P("dp", None, None),
        P("dp", None, None),
        P("dp", None, None),
        P("dp", None, None),
        P("expert", None, None, None),
        P("expert", None, None, None),
        P("expert", None, None, None),
        P("expert", None, None, None),
    )
    out_specs = P(("expert", "dp"), None)
    return jax.shard_map(shards, mesh=mesh, in_specs=in_specs, out_specs=out_specs, check_vma=False)
```

```python
import functools
import math

import jax
import jax.numpy as jnp
from jax import lax
from jax.experimental import pallas as pl
from jax.experimental.pallas import tpu as pltpu
from jax.sharding import PartitionSpec as P

D = 4096
NB = 64
DB = 64
HB = 256
T = 128
F32 = jnp.float32
BF16 = jnp.bfloat16


def tile_monarch(x_ref, lanes, w1_ref, w2_ref, w3_ref, w4_ref, z_refs, u_refs, store):
    def spread(refs, rows, value):
        for i in range(lanes):
            refs[i][rows, :] = value[:, i * T : (i + 1) * T]

    def strided(refs, start):
        parts = [refs[i][pl.ds(start, NB, stride=NB), :] for i in range(lanes)]
        return jnp.concatenate(parts, axis=1).astype(BF16)

    def up(a, carry):
        rows = pl.ds(pl.multiple_of(a * DB, DB), DB)
        x = x_ref[rows, : lanes * T]
        spread(z_refs, rows, jnp.dot(w1_ref[0, a], x, preferred_element_type=F32))
        return carry

    lax.fori_loop(0, NB, up, 0, unroll=8)

    def middle(j, carry):
        hidden = jnp.dot(w2_ref[0, j], strided(z_refs, j), preferred_element_type=F32)
        hidden = (0.5 * hidden) * (1.0 + lax.erf(hidden * (0.5**0.5)))
        u = jnp.dot(w3_ref[0, j], hidden.astype(BF16), preferred_element_type=F32)
        spread(u_refs, pl.ds(pl.multiple_of(j * NB, NB), NB), u)
        return carry

    lax.fori_loop(0, NB, middle, 0, unroll=4)

    def down(k, carry):
        rows = pl.ds(pl.multiple_of(k * DB, DB), DB)
        store(rows, jnp.dot(w4_ref[0, k], strided(u_refs, k), preferred_element_type=F32))
        return carry

    lax.fori_loop(0, NB, down, 0, unroll=8)


def shared_kernel(x_ref, w1_ref, w2_ref, w3_ref, w4_ref, o_ref, z_ref, u_ref):
    def store(rows, value):
        o_ref[rows, :] = value.astype(BF16)

    tile_monarch(x_ref, 1, w1_ref, w2_ref, w3_ref, w4_ref, (z_ref,), (u_ref,), store)


def routed_kernel(
    counts_ref, pos_ref, gate_ref, x_ref, w1_ref, w2_ref, w3_ref, w4_ref,
    o_ref, x_scr, z0_ref, z1_ref, u0_ref, u1_ref,
):
    expert, tile = pl.program_id(0), pl.program_id(1)
    left = counts_ref[expert] - tile * 2 * T
    sources = x_ref.shape[0]

    @pl.when(left <= T)
    def _():
        o_ref[...] = jnp.zeros_like(o_ref)

    def serve(lanes):
        width = lanes * T
        wanted = lax.broadcasted_iota(jnp.int32, (width, 2 * T), 0) + tile * 2 * T
        step = D // 8

        for part in range(8):
            rows = pl.ds(part * step, step)

            def pick(pair, total):
                both = jnp.concatenate([x_ref[2 * pair, rows, :], x_ref[2 * pair + 1, rows, :]], axis=1)
                onehot = (wanted == pos_ref[0, pair, :, :]).astype(F32).astype(BF16)
                return total + lax.dot_general(
                    both, onehot, (((1,), (1,)), ((), ())), preferred_element_type=F32
                )

            total = lax.fori_loop(0, sources // 2, pick, jnp.zeros((step, width), F32))
            x_scr[rows, :width] = total.astype(BF16)

        gate = gate_ref[0, 0][:, :width]

        def store(rows, value):
            o_ref[rows, :width] = (value * gate).astype(BF16)

        tile_monarch(
            x_scr, lanes, w1_ref, w2_ref, w3_ref, w4_ref, (z0_ref, z1_ref), (u0_ref, u1_ref), store
        )

    @pl.when(left > T)
    def _():
        serve(2)

    @pl.when(jnp.logical_and(left > 0, left <= T))
    def _():
        serve(1)


def weight_specs(index_map, buffers=2):
    shapes = ((NB, DB), (HB, NB), (NB, HB), (DB, NB))
    mode = pl.Buffered(buffers)
    return [pl.BlockSpec((1, NB) + shape, index_map, pipeline_mode=mode) for shape in shapes]


def turned(factors):
    return tuple(jnp.swapaxes(w, -1, -2) for w in factors)


def shared_call(x_t, factors):
    return pl.pallas_call(
        shared_kernel,
        out_shape=jax.ShapeDtypeStruct((D, T), BF16),
        grid=(1,),
        in_specs=[pl.BlockSpec((D, T), lambda i: (0, 0))] + weight_specs(lambda i: (0, 0, 0, 0)),
        out_specs=pl.BlockSpec((D, T), lambda i: (0, 0)),
        scratch_shapes=[pltpu.VMEM((D, T), F32), pltpu.VMEM((D, T), F32)],
        compiler_params=pltpu.CompilerParams(vmem_limit_bytes=56 * 2**20),
        cost_estimate=pl.CostEstimate(flops=10**10, bytes_accessed=10**7, transcendentals=0),
        name="shared_expert",
    )(x_t, *factors)


def routed_call(counts, pos, slot_gates, x_all, factors, tiles):
    residents = pos.shape[0]
    sources = x_all.shape[0]
    grid_spec = pltpu.PrefetchScalarGridSpec(
        num_scalar_prefetch=1,
        grid=(residents, tiles),
        in_specs=[
            pl.BlockSpec((1, sources // 2, 1, 2 * T), lambda e, i, c: (e, 0, 0, 0)),
            pl.BlockSpec((1, 1, 1, 2 * T), lambda e, i, c: (e, i, 0, 0)),
            pl.BlockSpec((sources, x_all.shape[1], T), lambda e, i, c: (0, 0, 0), pipeline_mode=pl.Buffered(1)),
        ]
        + weight_specs(lambda e, i, c: (e, 0, 0, 0), 2 if sources <= 8 else 1),
        out_specs=pl.BlockSpec((D, 2 * T), lambda e, i, c: (0, e * tiles + i)),
        scratch_shapes=[pltpu.VMEM((D, 2 * T), BF16)] + [pltpu.VMEM((D, T), F32)] * 4,
    )
    return pl.pallas_call(
        routed_kernel,
        out_shape=jax.ShapeDtypeStruct((D, residents * tiles * 2 * T), BF16),
        grid_spec=grid_spec,
        compiler_params=pltpu.CompilerParams(vmem_limit_bytes=62 * 2**20),
        cost_estimate=pl.CostEstimate(flops=4 * 10**10, bytes_accessed=2 * 10**7, transcendentals=0),
        name="routed_experts",
    )(counts, pos, slot_gates, x_all, *factors)


def combine_kernel(depth, window, starts_ref, pos_ref, o_ref, y_ref):
    residents = starts_ref.shape[0]
    pair = pl.program_id(0)
    wanted = lax.broadcasted_iota(jnp.int32, (window, 2 * T), 0)
    begins = [pl.multiple_of(starts_ref[e, pair] * T, T) for e in range(residents)]
    hots = [
        (wanted + begins[e] == pos_ref[e, 0, :, :]).astype(F32).astype(BF16) for e in range(residents)
    ]
    hot = jnp.concatenate(hots, axis=0)
    step = 512

    def part(i, carry):
        rows = pl.ds(pl.multiple_of(i * step, step), step)
        near = [
            o_ref[rows, pl.ds(pl.multiple_of(begins[e] + e * depth, T), window)] for e in range(residents)
        ]
        total = jnp.dot(jnp.concatenate(near, axis=1), hot, preferred_element_type=F32).astype(BF16)
        y_ref[0, rows, :] = total[:, :T]
        y_ref[1, rows, :] = total[:, T:]
        return carry

    lax.fori_loop(0, D // step, part, 0)


def combine_call(starts, pos, outs, sources, depth, window):
    residents = pos.shape[0]
    grid_spec = pltpu.PrefetchScalarGridSpec(
        num_scalar_prefetch=1,
        grid=(sources // 2,),
        in_specs=[
            pl.BlockSpec((residents, 1, 1, 2 * T), lambda s, c: (0, s, 0, 0)),
            pl.BlockSpec((D, residents * depth), lambda s, c: (0, 0), pipeline_mode=pl.Buffered(1)),
        ],
        out_specs=pl.BlockSpec((2, D, T), lambda s, c: (s, 0, 0)),
    )
    return pl.pallas_call(
        functools.partial(combine_kernel, depth, window),
        out_shape=jax.ShapeDtypeStruct((sources, D, T), BF16),
        grid_spec=grid_spec,
        compiler_params=pltpu.CompilerParams(vmem_limit_bytes=48 * 2**20),
        name="combine",
    )(starts, pos, outs)


def grid_of(count):
    side = math.isqrt(count // 2)
    return count // side, side


def greet(z, y, nz, ny):
    barrier = pltpu.get_barrier_semaphore()
    for other in range(1, ny):
        pl.semaphore_signal(barrier, inc=1, device_id={"expert": z * ny + lax.rem(y + other, ny)})

    @pl.when(z > 0)
    def _():
        pl.semaphore_signal(barrier, inc=1, device_id={"expert": (z - 1) * ny + y})

    @pl.when(z < nz - 1)
    def _():
        pl.semaphore_signal(barrier, inc=1, device_id={"expert": (z + 1) * ny + y})

    peers = ny - 1 + jnp.where(z > 0, 1, 0) + jnp.where(z < nz - 1, 1, 0)
    pl.semaphore_wait(barrier, peers)


def gather_kernel(nz, x_ref, out_ref, own_sem, up_sem, down_sem, side_sem, recv_sem):
    ny = 2
    me = lax.axis_index("expert")
    z, y = me // ny, lax.rem(me, ny)
    beside = z * ny + (1 - y)

    def send(block, src, sem, target):
        return pltpu.make_async_remote_copy(
            src_ref=src, dst_ref=out_ref.at[block], send_sem=sem.at[block],
            recv_sem=recv_sem.at[block], device_id={"expert": target},
        )

    def arrived(block):
        send(block, out_ref.at[block], side_sem, beside).wait_recv()

    greet(z, y, nz, ny)
    own = pltpu.make_async_copy(x_ref, out_ref.at[me], own_sem)
    own.start()

    @pl.when(z < nz - 1)
    def _():
        send(me, x_ref, up_sem, me + ny).start()

    @pl.when(z > 0)
    def _():
        send(me, x_ref, down_sem, me - ny).start()

    send(me, x_ref, side_sem, beside).start()

    for k in range(1, nz):
        block = me - k * ny

        @pl.when(z >= k)
        def _():
            arrived(block)

            @pl.when(z < nz - 1)
            def _():
                send(block, out_ref.at[block], up_sem, me + ny).start()

            send(block, out_ref.at[block], side_sem, beside).start()

        later = me + k * ny

        @pl.when(z + k < nz)
        def _():
            arrived(later)

            @pl.when(z > 0)
            def _():
                send(later, out_ref.at[later], down_sem, me - ny).start()

            send(later, out_ref.at[later], side_sem, beside).start()

    for other in range(nz):
        arrived(other * ny + (1 - y))
    own.wait()
    for other in range(nz):
        block = other * ny + y
        send(block, out_ref.at[block], side_sem, beside).wait_send()

        @pl.when(jnp.logical_and(other <= z, z < nz - 1))
        def _():
            send(block, out_ref.at[block], up_sem, me + ny).wait_send()

        @pl.when(jnp.logical_and(other >= z, z > 0))
        def _():
            send(block, out_ref.at[block], down_sem, me - ny).wait_send()


def gather_tokens(x_t):
    count = lax.axis_size("expert")
    nz, ny = grid_of(count)
    if ny != 2:
        return lax.all_gather(x_t, "expert", axis=0, tiled=False)
    sems = pltpu.SemaphoreType.DMA((count,))
    return pl.pallas_call(
        functools.partial(gather_kernel, nz),
        out_shape=jax.ShapeDtypeStruct((count,) + x_t.shape, x_t.dtype),
        in_specs=[pl.BlockSpec(memory_space=pl.ANY)],
        out_specs=pl.BlockSpec(memory_space=pl.ANY),
        scratch_shapes=[pltpu.SemaphoreType.DMA, sems, sems, sems, sems],
        compiler_params=pltpu.CompilerParams(collective_id=0, has_side_effects=True),
        cost_estimate=pl.CostEstimate(flops=10**11, bytes_accessed=3 * 10**8, transcendentals=0),
        name="gather_tokens",
    )(x_t)


def scatter_kernel(
    nz, y_hbm, out_ref, held, beside_in, below_in, above_in,
    load_sem, side_sem, side_recv, up_sem, up_recv, down_sem, down_recv,
):
    ny = 2
    me = lax.axis_index("expert")
    z, y = me // ny, lax.rem(me, ny)
    beside = z * ny + (1 - y)

    def load(target):
        return pltpu.make_async_copy(y_hbm.at[target * ny + y], held.at[target], load_sem.at[target])

    def side(target):
        return pltpu.make_async_remote_copy(
            src_ref=y_hbm.at[target * ny + (1 - y)], dst_ref=beside_in.at[target],
            send_sem=side_sem.at[target], recv_sem=side_recv.at[target],
            device_id={"expert": beside},
        )

    def up(target):
        return pltpu.make_async_remote_copy(
            src_ref=held.at[target], dst_ref=below_in.at[target], send_sem=up_sem.at[target],
            recv_sem=up_recv.at[target], device_id={"expert": me + ny},
        )

    def down(target):
        return pltpu.make_async_remote_copy(
            src_ref=held.at[target], dst_ref=above_in.at[target], send_sem=down_sem.at[target],
            recv_sem=down_recv.at[target], device_id={"expert": me - ny},
        )

    def add(target, ref):
        step = 512

        def body(i, carry):
            rows = pl.ds(pl.multiple_of(i * step, step), step)
            total = held[target, rows, :].astype(F32) + ref[target, rows, :].astype(F32)
            held[target, rows, :] = total.astype(BF16)
            return carry

        lax.fori_loop(0, D // step, body, 0)

    greet(z, y, nz, ny)
    for k in range(nz - 1, -1, -1):
        @pl.when(z + k < nz)
        def _():
            side(z + k).start()

        if k > 0:
            @pl.when(z - k >= 0)
            def _():
                side(z - k).start()

    for target in range(nz):
        load(target).start()
    for target in range(nz):
        load(target).wait()
    for k in range(nz - 1, 0, -1):
        target = z + k

        @pl.when(z + k < nz)
        def _():
            side(target).wait_recv()
            add(target, beside_in)

            @pl.when(z > 0)
            def _():
                up(target).wait_recv()
                add(target, below_in)

            up(target).start()

        lower = z - k

        @pl.when(z - k >= 0)
        def _():
            side(lower).wait_recv()
            add(lower, beside_in)

            @pl.when(z < nz - 1)
            def _():
                down(lower).wait_recv()
                add(lower, above_in)

            down(lower).start()

    side(z).wait_recv()
    add(z, beside_in)

    @pl.when(z > 0)
    def _():
        up(z).wait_recv()
        add(z, below_in)

    @pl.when(z < nz - 1)
    def _():
        down(z).wait_recv()
        add(z, above_in)

    out_ref[...] = held[z]
    for target in range(nz):
        side(target).wait_send()

        @pl.when(target > z)
        def _():
            up(target).wait_send()

        @pl.when(target < z)
        def _():
            down(target).wait_send()


def scatter_sums(sums):
    count = lax.axis_size("expert")
    nz, ny = grid_of(count)
    if ny != 2:
        return lax.psum_scatter(sums, "expert", scatter_dimension=0, tiled=False)
    block = pltpu.VMEM((nz,) + sums.shape[1:], sums.dtype)
    sems = pltpu.SemaphoreType.DMA((nz,))
    return pl.pallas_call(
        functools.partial(scatter_kernel, nz),
        out_shape=jax.ShapeDtypeStruct(sums.shape[1:], sums.dtype),
        in_specs=[pl.BlockSpec(memory_space=pl.ANY)],
        out_specs=pl.BlockSpec(memory_space=pltpu.VMEM),
        scratch_shapes=[block] * 4 + [sems] * 7,
        compiler_params=pltpu.CompilerParams(
            collective_id=1, has_side_effects=True, vmem_limit_bytes=40 * 2**20
        ),
        cost_estimate=pl.CostEstimate(flops=10**11, bytes_accessed=3 * 10**8, transcendentals=0),
        name="scatter_sums",
    )(sums)


ROWS = D + 16
CAP = 48
CHUNK = 256
CHUNKS = D // CHUNK
LAG = 5
SPANS = ((0, 1024), (1024, 1024), (2048, 1280), (3328, ROWS - 3328))
EIGHTS = (0, 8, 16, 24)
KEPT = NB // 2
LEGS = ((1, 0, 8, 0), (0, 0, 16, 0), (1, 8, 8, 0), (1, 16, 8, 0), (1, 24, 8, 0), (3, 0, 16, 0)) + tuple(
    (2, start, 8, k) for k in (0, KEPT) for start in EIGHTS
)


def dot(a, b):
    return jnp.dot(a, b, preferred_element_type=F32)


def dot_turned(w, x):
    return lax.dot_general(w, x, (((0,), (0,)), ((), ())), preferred_element_type=F32)


def gelu(hidden):
    return ((0.5 * hidden) * (1.0 + lax.erf(hidden * (0.5**0.5)))).astype(BF16)


def aligned(start, step):
    return pl.ds(pl.multiple_of(start, step), step)


def apart(upper, lower):
    top, bottom = [], []
    for a, b in zip(upper, lower):
        top += [a, jnp.zeros_like(a)]
        bottom += [jnp.zeros_like(b), b]
    return jnp.concatenate([jnp.concatenate(top, axis=1), jnp.concatenate(bottom, axis=1)], axis=0)


def strided(ref, tiles, start):
    return [ref[i, pl.ds(start, NB, stride=NB), :].astype(BF16) for i in range(tiles)]


def up(tiles, load, w1, z_ref):
    def some(i, carry):
        for q in range(4):
            p = i * 4 + q
            parts = load(aligned(p * 2 * DB, 2 * DB))
            value = dot(w1[p], apart([x[:DB] for x in parts], [x[DB:] for x in parts]))
            for t in range(tiles):
                for side in range(2):
                    at = 2 * t + side
                    z_ref[t, aligned((2 * p + side) * DB, DB), :] = value[:, at * T : (at + 1) * T]
        return carry

    lax.fori_loop(0, NB // 8, some, 0)


def middle(tiles, w2, w3, z_ref, u_ref, first, count):
    batch = min(count, 8 if tiles == 1 else 4)

    def some(i, carry):
        blocks = [first + i * batch + q for q in range(batch)]
        hidden = []
        for j in blocks:
            parts = strided(z_ref, tiles, j)
            rows = parts[0] if tiles == 1 else jnp.concatenate(parts, axis=1)
            hidden.append(gelu(dot_turned(w2[j], rows)))
        for j, h in zip(blocks, hidden):
            value = dot(w3[j], h)
            for t in range(tiles):
                u_ref[t, aligned(j * NB, NB), :] = value[:, t * T : (t + 1) * T]
        return carry

    lax.fori_loop(0, count // batch, some, 0)


def expand(w2, z_ref, h_ref, first, count):
    def some(i, carry):
        blocks = [first + i * 4 + q for q in range(4)]
        hidden = [dot_turned(w2[j], jnp.concatenate(strided(z_ref, 2, j), axis=1)) for j in blocks]
        for j, h in zip(blocks, hidden):
            h_ref[j] = gelu(h)
        return carry

    lax.fori_loop(0, count // 4, some, 0)


def contract(w3, h_ref, u_ref, first, count, start):
    def some(i, carry):
        for q in range(4):
            j = first + i * 4 + q
            value = dot(w3[j, pl.ds(start, KEPT), :], h_ref[j])
            for t in range(2):
                u_ref[t, aligned(j * NB + start, KEPT), :] = value[:, t * T : (t + 1) * T]
        return carry

    lax.fori_loop(0, count // 4, some, 0)


def down(tiles, w4, u_ref, store, first, count):
    batch = min(count, 4)

    def some(i, carry):
        for q in range(batch):
            p = first + i * batch + q
            value = dot(w4[p], apart(strided(u_ref, tiles, 2 * p), strided(u_ref, tiles, 2 * p + 1)))
            for side in range(2):
                parts = [value[:, (2 * t + side) * T : (2 * t + side + 1) * T] for t in range(tiles)]
                store(aligned((2 * p + side) * DB, DB), parts)
        return carry

    lax.fori_loop(0, count // batch, some, 0)


def pack_pairs(src, dst, first, count):
    def some(i, carry):
        for q in range(4):
            p = i * 4 + q
            both = jnp.concatenate([src[2 * p], src[2 * p + 1]], axis=0)
            dst[first + p] = both.T
        return carry

    lax.fori_loop(0, count // 4, some, 0)


def layer_kernel(
    tok, ids, codes, r1, r2, r3, r4, s1, s2, s3, s4, out_ref,
    x_all, a1, a2, a3, a4, b1, b2, b3, b4, c1, c2, c3, c4,
    slots, z_ref, u_ref, hot, hot_t, share, shared_out, core_in, y_in, z_in,
    tok_in, r_in, s1_in, s4_in, h_ref,
    local_sem, x_send, x_recv, b_send, b_recv, c_send, c_recv, sum_send, sum_recv,
):
    e, d = lax.axis_index("expert"), lax.axis_index("dp")
    z, y, x, c = e // 2, lax.rem(e, 2), d // 2, lax.rem(d, 2)
    near_z = e + 2 - 4 * lax.rem(z, 2)
    on_far = {"expert": lax.rem(e + 4, 8), "dp": d}
    on_near = {"expert": near_z, "dp": d}
    on_y = {"expert": e + 1 - 2 * y, "dp": d}
    on_core = {"expert": e, "dp": d + 1 - 2 * c}
    on_x = {"expert": e, "dp": lax.rem(d + 2, 4)}
    own_a, own_b, own_s = (a1, a2, a3, a4), (b1, b2, b3, b4), (c1, c2, c3, c4)

    def remote(src, dst, send, recv, target):
        return pltpu.make_async_remote_copy(
            src_ref=src, dst_ref=dst, send_sem=send, recv_sem=recv, device_id=target
        )

    def x_copy(number, source, slot, rows, target):
        return remote(
            x_all.at[source, rows], x_all.at[slot, rows], x_send.at[number], x_recv.at[number], target
        )

    whole = pl.ds(0, ROWS)
    spans = [pl.ds(*s) for s in SPANS]
    x_core = x_copy(0, 0, 1, whole, on_core)
    x_y = x_copy(1, 0, 2, whole, on_y)
    x_far = [x_copy(2 + i, 0, 4, rows, on_far) for i, rows in enumerate(spans)]
    x_y_core = x_copy(6, 2, 3, whole, on_core)
    x_far_core = [x_copy(7 + i, 4, 5, rows, on_core) for i, rows in enumerate(spans)]
    x_far_y = [x_copy(11 + i, 4, 6, rows, on_y) for i, rows in enumerate(spans)]
    x_last = [x_copy(15 + i, 6, 7, rows, on_core) for i, rows in enumerate(spans)]

    def leg(number, half, first):
        w, start, size, k = LEGS[number]
        rows = pl.ds(half * (16 if w in (0, 3) else 32) + start, size)
        where = (rows, pl.ds(k, KEPT)) if w == 2 else rows
        src = (a1, r2.at[c], r3.at[c], a4)[w] if first else own_b[w]
        at = number if first else number + len(LEGS)
        return remote(
            src.at[where], own_b[w].at[where], b_send.at[at], b_recv.at[at], on_near if first else on_x
        )

    b_near = [leg(n, x, True) for n in range(len(LEGS))]
    b_x = [leg(n, x, False) for n in range(len(LEGS))]
    b_there = [leg(n, 1 - x, False) for n in range(len(LEGS))]

    def quarter(w, at, number, target, src=None):
        size = 8 if w in (0, 3) else 16
        rows = pl.ds(at * size, size)
        src = own_s[w].at[rows] if src is None else src
        return remote(src, own_s[w].at[rows], c_send.at[number], c_recv.at[number], target)

    sources = (None, s2, s3, None)
    c_core = [quarter(w, d, w, on_core, sources[w]) for w in range(4)]
    c_x = [quarter(w, d, 4 + w, on_x, sources[w]) for w in range(4)]
    c_fwd = [quarter(w, lax.rem(d + 2, 4), 8 + w, on_core) for w in range(4)]

    def local(number, src, dst):
        return pltpu.make_async_copy(src, dst, local_sem.at[number])

    here_s = pl.ds(d * 16, 16)
    tok_load = local(0, tok, tok_in)
    r1_load = local(1, r1.at[c], r_in)
    r4_load = local(2, r4.at[c], r_in)
    r_loads = [local(3, r2.at[c], a2), local(4, r3.at[c], a3)]
    s_packs = [local(5, s1, s1_in), local(6, s4, s4_in)]
    s_loads = [local(7, s2, c2.at[here_s]), local(8, s3, c3.at[here_s])]
    for copy in [tok_load, r1_load] + s_packs:
        copy.start()

    barrier = pltpu.get_barrier_semaphore()
    for target in (on_far, on_near, on_y, on_core, on_x):
        pl.semaphore_signal(barrier, inc=1, device_id=target)
    pl.semaphore_wait(barrier, 5)

    b_near[0].start()
    for copy in s_packs:
        copy.wait()
    pack_pairs(s1_in, c1, d * 8, 8)
    for w in range(3):
        c_x[w].start()
    numbers = [ref[...].astype(F32) for ref in (ids, codes)]
    extra = jnp.concatenate(numbers + [jnp.zeros((ROWS - D - 4, T), F32)], axis=0)
    x_all[0, D:ROWS, :] = extra.astype(BF16)
    tok_load.wait()
    for i in range(4):
        for at in range(SPANS[i][0], min(D, sum(SPANS[i])), 256):
            x_all[0, at : at + 256, :] = tok_in[:, at : at + 256].T
        x_far[i].start()
    x_y.start()
    x_core.start()
    r1_load.wait()
    pack_pairs(r_in, a1, 0, 32)
    r4_load.start()
    for n in (1, 2, 3, 4):
        b_near[n].start()
    pack_pairs(s4_in, c4, d * 8, 8)
    c_x[3].start()
    for copy in c_core + r_loads + s_loads:
        copy.start()
    r4_load.wait()
    pack_pairs(r_in, a4, 0, 32)
    for copy in b_near[5:]:
        copy.start()

    ids_a = (2 * e + c).astype(F32)
    ids_b = (2 * near_z + c).astype(F32)

    def prepare(q):
        extra = jnp.concatenate(
            [x_all[2 * q, D:ROWS, :].astype(F32), x_all[2 * q + 1, D:ROWS, :].astype(F32)], axis=1
        )
        id0, id1, code0, code1 = (extra[i : i + 1] for i in range(4))
        lane = lax.broadcasted_iota(jnp.int32, (1, 2 * T), 1)
        before = lax.broadcasted_iota(jnp.int32, (2 * T, 2 * T), 0)
        after = lax.broadcasted_iota(jnp.int32, (2 * T, 2 * T), 1)
        tri = jnp.logical_and(before < after, (before < T) == (after < T))
        tri = tri.astype(F32).astype(BF16)
        row8 = lax.broadcasted_iota(jnp.int32, (8, 2 * T), 0)
        picks = [jnp.logical_or(id0 == n, id1 == n) for n in (ids_a, ids_b)]
        names = [jnp.where(p, 1.0, 0.0) for p in picks]
        codes = [jnp.where(id0 == n, code0, code1) for n in (ids_a, ids_b)]
        stacked = jnp.where(row8 == 0, names[0], jnp.where(row8 == 1, names[1], 0.0))
        ranks = dot(stacked.astype(BF16), tri)
        base = jnp.where(lane < T, 2 * q * CAP, (2 * q + 1) * CAP).astype(F32)
        places = [
            jnp.where(picks[n], ranks[n : n + 1] + base, -1000.0).astype(jnp.int32) for n in range(2)
        ]
        for tile, half in ((q, 0), (q - 1, 1)):
            if not 0 <= tile < 3:
                continue
            wanted = lax.broadcasted_iota(jnp.int32, (T, 2 * T), 0) + tile * T
            for n in range(2):
                own = (wanted == places[n]).astype(F32).astype(BF16)
                hot[q, half * 2 * T + n * T : half * 2 * T + (n + 1) * T, :] = own
                hot_t[tile, half * 2 * T : (half + 1) * 2 * T, n * T : (n + 1) * T] = own.T
                values = jnp.where(
                    row8 == 0, codes[n], jnp.where(row8 == 1, code0, jnp.where(row8 == 2, code1, 0.0))
                )
                got = lax.dot_general(
                    values.astype(BF16), own, (((1,), (1,)), ((), ())), preferred_element_type=F32
                )
                if half == 0:
                    share[n, tile] = got
                else:
                    share[n, tile] += got

    def pick(tile):
        def some(i, carry):
            rows = aligned(i * 512, 512)
            blocks = [x_all[2 * tile + n, rows, :] for n in range(4)]
            total = dot(jnp.concatenate(blocks, axis=1), hot_t[tile])
            total = total.astype(BF16)
            slots[0, tile, rows, :] = total[:, :T]
            slots[1, tile, rows, :] = total[:, T:]
            return carry

        lax.fori_loop(0, D // 512, some, 0)

    def slot_loader(n, first, count):
        return lambda rows: [slots[n, first + i, rows, :] for i in range(count)]

    def slot_storer(n, first, count):
        gates = []
        for i in range(count):
            got = share[n, first + i]
            under = got[1:2] + got[2:3]
            gates.append(jnp.where(under > 0.0, got[0:1] / jnp.maximum(under, 1.0), 0.0))
        gates = [jnp.broadcast_to(g, (DB, T)) for g in gates]

        def store(rows, parts):
            for i in range(count):
                slots[n, first + i, rows, :] = (parts[i] * gates[i]).astype(BF16)

        return store

    def forward(i):
        x_far[i].wait_recv()
        x_far_y[i].start()
        x_far_core[i].start()

    def relay(*numbers):
        for n in numbers:
            b_near[n].wait_recv()
            b_x[n].start()

    def last_hop(i):
        x_far_y[i].wait_recv()
        x_last[i].start()

    here, there = x * 32, 32 - x * 32
    z_s, u_s = z_ref.at[pl.ds(1, 1)], u_ref.at[pl.ds(1, 1)]
    x_core.wait_recv()
    prepare(0)
    for copy in s_loads:
        copy.wait()
    for copy in c_core:
        copy.wait_recv()
    c_x[0].wait_recv()
    c_fwd[0].start()
    c_fwd[0].wait_recv()
    up(1, lambda rows: [x_all[0, rows, :]], c1, z_s)
    middle(1, c2, c3, z_s, u_s, here, NB // 2)
    relay(0)
    x_y.wait_recv()
    x_y_core.start()
    x_y_core.wait_recv()
    prepare(1)
    pick(0)
    forward(0)
    for copy in r_loads:
        copy.wait()
    up(1, slot_loader(0, 0, 1), a1, z_ref)
    for copy in c_x[1:]:
        copy.wait_recv()
    for copy in c_fwd[1:]:
        copy.start()
    middle(1, a2, a3, z_ref, u_ref, 0, NB)
    relay(1)
    forward(1)
    down(1, a4, u_ref, slot_storer(0, 0, 1), 0, NB // 2)
    last_hop(0)
    for copy in c_fwd[1:]:
        copy.wait_recv()

    def keep_shared(rows, parts):
        shared_out[rows, :] = parts[0].astype(BF16)

    relay(2)
    middle(1, c2, c3, z_s, u_s, there, NB // 2)
    forward(2)
    down(1, c4, u_s, keep_shared, 0, NB // 2)
    last_hop(1)
    forward(3)
    relay(3)
    for copy in x_far_core:
        copy.wait_recv()
    prepare(2)
    pick(1)
    up(1, slot_loader(0, 1, 1), a1, z_ref)
    middle(1, a2, a3, z_ref, u_ref, 0, NB // 2)
    relay(4)
    last_hop(2)
    middle(1, a2, a3, z_ref, u_ref, NB // 2, NB // 2)
    last_hop(3)
    down(1, a4, u_ref, slot_storer(0, 1, 1), 0, NB // 2)
    relay(5)
    for copy in x_last:
        copy.wait_recv()
    prepare(3)
    pick(2)
    up(1, slot_loader(0, 2, 1), a1, z_ref)
    middle(1, a2, a3, z_ref, u_ref, 0, NB // 2)
    relay(6, 7)
    middle(1, a2, a3, z_ref, u_ref, NB // 2, NB // 2)
    down(1, a4, u_ref, slot_storer(0, 2, 1), 0, NB // 2)
    relay(8)
    b_there[1].wait_recv()
    z_two, u_two = z_ref.at[pl.ds(1, 2)], u_ref.at[pl.ds(1, 2)]
    up(2, slot_loader(1, 1, 2), b1, z_two)
    relay(9)
    expand(b2, z_two, h_ref, here, 32)
    for n in (0, 2, 3, 4):
        b_there[n].wait_recv()
    expand(b2, z_two, h_ref, there, 16)
    relay(10)
    expand(b2, z_two, h_ref, there + 16, 16)
    contract(b3, h_ref, u_two, here, 32, 0)
    relay(11)
    b_there[6].wait_recv()
    b_there[7].wait_recv()
    contract(b3, h_ref, u_two, there, 16, 0)
    b_there[8].wait_recv()
    b_there[9].wait_recv()
    contract(b3, h_ref, u_two, there + 16, 16, 0)
    b_there[5].wait_recv()

    for copy in [x_core, x_y, x_y_core] + x_far + x_far_core + x_far_y + x_last:
        copy.wait_send()

    def sum_copy(at, src, dst, i, size, target):
        rows = aligned(i * size, size)
        return remote(src.at[rows], dst.at[rows], sum_send.at[at], sum_recv.at[at], target)

    def to_core(q, i):
        at = i + (8 + CHUNKS * (q - 2) if q > 1 else 4 * q)
        return sum_copy(at, x_all.at[2 * q + 1], core_in.at[q], i, CHUNK if q > 1 else 1024, on_core)

    def to_y(q, i):
        at = 8 + 2 * CHUNKS + i + (4 if q > 1 else 0)
        return sum_copy(at, x_all.at[2 * q], y_in.at[q // 2], i, CHUNK if q > 1 else 1024, on_y)

    def to_far(i):
        return sum_copy(12 + 3 * CHUNKS + i, x_all.at[4], z_in, i, CHUNK, on_far)

    def combine(q, i):
        where = [(tile, half) for tile, half in ((q, 0), (q - 1, 1)) if 0 <= tile < 3]
        first, last = where[0][1] * 2 * T, (where[-1][1] + 1) * 2 * T
        size = CHUNK if q > 1 else 1024
        for j in range(size // 256):
            rows = aligned(i * size + j * 256, 256)
            both = jnp.concatenate([slots[n, tile, rows, :] for tile, _ in where for n in range(2)], axis=1)
            total = dot(both, hot[q, first:last, :]).astype(BF16)
            x_all[2 * q, rows, :] = total[:, :T]
            x_all[2 * q + 1, rows, :] = total[:, T:]
        to_core(q, i).start()

    def summed(q, refs, rows):
        total = x_all[2 * q, rows, :].astype(F32)
        for ref in refs:
            total += ref[rows, :].astype(F32)
        return total

    def add(q, refs, i):
        size = CHUNK if q > 1 else 1024
        for j in range(size // 256):
            rows = aligned(i * size + j * 256, 256)
            x_all[2 * q, rows, :] = summed(q, refs, rows).astype(BF16)

    def over_y(q, i):
        to_core(q, i).wait_recv()
        add(q, [core_in.at[q]], i)
        to_y(q, i).start()

    def over_z(i):
        to_core(2, i).wait_recv()
        to_y(3, i).wait_recv()
        add(2, [core_in.at[2], y_in.at[1]], i)
        to_far(i).start()

    store_b = slot_storer(1, 1, 2)

    def begin(i, ahead, lag):
        down(2, b4, u_two, store_b, CHUNK // 128 * i, CHUNK // 128)
        combine(3, i)
        if ahead:
            over_y(3, i - 1)
        combine(2, i)
        if lag:
            over_z(i - LAG)

    def loop(first, last, body):
        lax.fori_loop(first, last, lambda i, carry: (body(i), carry)[1], 0)

    relay(12)
    begin(0, False, False)
    loop(1, 3, lambda i: begin(i, True, False))
    relay(13)
    loop(3, LAG, lambda i: begin(i, True, False))
    loop(LAG, CHUNKS // 2, lambda i: begin(i, True, True))
    over_y(3, CHUNKS // 2 - 1)
    contract(b3, h_ref, u_two, here, 32, KEPT)
    for n in (10, 11, 12, 13):
        b_there[n].wait_recv()
    contract(b3, h_ref, u_two, there, 32, KEPT)
    begin(CHUNKS // 2, False, True)
    loop(CHUNKS // 2 + 1, CHUNKS, lambda i: begin(i, True, True))
    over_y(3, CHUNKS - 1)
    z_one, u_one = z_ref.at[pl.ds(0, 1)], u_ref.at[pl.ds(0, 1)]
    up(1, slot_loader(1, 0, 1), b1, z_one)
    middle(1, b2, b3, z_one, u_one, 0, NB)
    store_one = slot_storer(1, 0, 1)
    for i in range(4):
        down(1, b4, u_one, store_one, 8 * i, 8)
        combine(1, i)
        if i > 0:
            over_y(1, i - 1)
    over_y(1, 3)
    loop(CHUNKS - LAG, CHUNKS, over_z)
    loop(0, 4, lambda i: combine(0, i))
    for i in range(4):
        to_core(0, i).wait_recv()
        to_y(1, i).wait_recv()

    def to_out(i):
        rows = aligned(i * CHUNK, CHUNK)
        return pltpu.make_async_copy(shared_out.at[rows], out_ref.at[rows], x_send.at[i])

    def finish(i):
        to_far(i).wait_recv()
        for j in range(CHUNK // 256):
            rows = aligned(i * CHUNK + j * 256, 256)
            total = summed(0, [core_in.at[0], y_in.at[0], shared_out, z_in], rows)
            shared_out[rows, :] = total.astype(BF16)
        to_out(i).start()

    loop(0, CHUNKS, finish)

    def drain(i):
        to_core(2, i).wait_send()
        to_core(3, i).wait_send()
        to_y(3, i).wait_send()
        to_far(i).wait_send()
        to_out(i).wait()

    for copy in b_near + b_x + c_core + c_x + c_fwd:
        copy.wait_send()
    for i in range(4):
        to_core(0, i).wait_send()
        to_core(1, i).wait_send()
        to_y(1, i).wait_send()
    loop(0, CHUNKS, drain)


def layer_call(tokens, expert_ids, gate_codes, shared, routed):
    hbm = pl.BlockSpec(memory_space=pl.ANY)
    vmem = pl.BlockSpec(memory_space=pltpu.VMEM)
    weights = [
        pltpu.VMEM((NB // 2, NB, 2 * DB), BF16), pltpu.VMEM((NB, NB, HB), BF16),
        pltpu.VMEM((NB, NB, HB), BF16), pltpu.VMEM((NB // 2, DB, 2 * NB), BF16),
    ]
    sems = pltpu.SemaphoreType.DMA
    block = pltpu.VMEM((D, T), BF16)
    legs, sums = 2 * len(LEGS), 12 + 4 * CHUNKS
    routed = (routed[0], routed[1], jnp.swapaxes(routed[2], -1, -2), routed[3])
    shared = (shared[0], shared[1], jnp.swapaxes(shared[2], -1, -2), shared[3])
    return pl.pallas_call(
        layer_kernel,
        out_shape=jax.ShapeDtypeStruct((D, T), BF16),
        in_specs=[hbm, vmem, vmem] + [hbm] * 8,
        out_specs=hbm,
        scratch_shapes=[pltpu.VMEM((8, ROWS, T), BF16)]
        + weights * 3
        + [
            pltpu.VMEM((2, 3, D, T), BF16),
            pltpu.VMEM((3, D, T), F32),
            pltpu.VMEM((3, D, T), F32),
            pltpu.VMEM((4, 4 * T, 2 * T), BF16),
            pltpu.VMEM((3, 4 * T, 2 * T), BF16),
            pltpu.VMEM((2, 3, 8, T), F32),
            block,
            pltpu.VMEM((4, D, T), BF16),
            pltpu.VMEM((2, D, T), BF16),
            block,
            pltpu.VMEM((T, D), BF16),
            pltpu.VMEM((NB, DB, NB), BF16),
            pltpu.VMEM((NB // 4, DB, NB), BF16),
            pltpu.VMEM((NB // 4, NB, DB), BF16),
            pltpu.VMEM((NB, HB, 2 * T), BF16),
            sems((9,)), sems((19,)), sems((19,)), sems((legs,)), sems((legs,)),
            sems((12,)), sems((12,)), sems((sums,)), sems((sums,)),
        ],
        compiler_params=pltpu.CompilerParams(
            collective_id=2, has_side_effects=True, vmem_limit_bytes=63 * 2**20
        ),
        cost_estimate=pl.CostEstimate(flops=10**11, bytes_accessed=3 * 10**8, transcendentals=0),
        name="layer",
    )(tokens, expert_ids.T, gate_codes.T, *routed, *shared).T


def running(ones, width):
    groups = ones.reshape(ones.shape[0], -1, width).astype(F32)
    inside = jnp.einsum("rgt,tu->rgu", groups, jnp.triu(jnp.ones((width, width), F32)))
    count = groups.shape[1]
    earlier = jnp.triu(jnp.ones((count, count), F32), 1)
    before = jnp.einsum("rg,gh->rh", inside[:, :, -1], earlier, precision=lax.Precision.HIGHEST)
    return (inside + before[:, :, None]).reshape(ones.shape).astype(jnp.int32)


def shards(tokens, expert_ids, gate_codes, *factors):
    shared, routed = factors[:4], factors[4:]
    residents = routed[0].shape[0]
    sources = lax.axis_size("expert")
    tok_rows = tokens.shape[0]
    if sources == 8 and lax.axis_size("dp") == 4 and residents == 2:
        return layer_call(tokens, expert_ids, gate_codes, shared, routed)
    experts_all = residents * sources
    capacity = max(2, 6 * tok_rows // experts_all)
    tiles = -(-sources * capacity // (2 * T))
    depth = tiles * 2 * T
    window = min(depth, -(-(T - 1 + 2 * capacity) // T) * T)

    extra = jnp.concatenate([expert_ids, gate_codes], axis=1).T.astype(BF16)
    extra = jnp.pad(extra, ((0, 16 - extra.shape[0]), (0, 0)))
    x_t = jnp.concatenate([tokens.T, extra], axis=0)
    x_all = gather_tokens(x_t)
    ids_all = x_all[:, D : D + 2].astype(jnp.int32)
    codes = x_all[:, D + 2 : D + 4].astype(F32)
    gates_all = codes / jnp.sum(codes, axis=1, keepdims=True)
    mine = lax.axis_index("expert") * residents + jnp.arange(residents, dtype=jnp.int32)
    match = ids_all[None] == mine[:, None, None, None]
    picked = jnp.any(match, axis=2).reshape(residents, sources * tok_rows)
    gate = jnp.sum(jnp.where(match, gates_all[None], 0.0), axis=2).reshape(residents, sources * tok_rows)
    ones = picked.astype(jnp.int32)
    ranks = running(ones, tok_rows)
    counts = ranks[:, -1]
    starts = (ranks - ones).reshape(residents, sources // 2, 2 * T)[:, :, 0]
    starts = jnp.minimum(starts, depth - window) // T
    pos = jnp.where(picked, ranks - 1, -1)
    slots = jnp.arange(depth, dtype=jnp.int32)
    slot_gates = jnp.sum(
        jnp.where(pos[:, None, :] == slots[None, :, None], gate[:, None, :], 0.0), axis=2
    ).reshape(residents, tiles, 1, 2 * T)
    pos = pos.reshape(residents, sources // 2, 1, 2 * T)

    outs = routed_call(counts, pos, slot_gates, x_all, turned(routed), tiles)
    y = combine_call(starts, pos, outs, sources, depth, window)
    sums = scatter_sums(y)
    whole = tuple(lax.all_gather(w, "dp", axis=0, tiled=True)[None] for w in turned(shared))
    shared_t = shared_call(x_t, whole)
    total = shared_t.astype(F32) + sums.astype(F32)
    return total.astype(BF16).T


def solution(mesh):
    in_specs = (
        P(("expert", "dp"), None),
        P(("expert", "dp"), None),
        P(("expert", "dp"), None),
        P("dp", None, None),
        P("dp", None, None),
        P("dp", None, None),
        P("dp", None, None),
        P("expert", None, None, None),
        P("expert", None, None, None),
        P("expert", None, None, None),
        P("expert", None, None, None),
    )
    out_specs = P(("expert", "dp"), None)
    return jax.shard_map(shards, mesh=mesh, in_specs=in_specs, out_specs=out_specs, check_vma=False)
```

```python
import functools
import math

import jax
import jax.numpy as jnp
from jax import lax
from jax.experimental import pallas as pl
from jax.experimental.pallas import tpu as pltpu
from jax.sharding import PartitionSpec as P

D = 4096
NB = 64
DB = 64
HB = 256
T = 128
F32 = jnp.float32
BF16 = jnp.bfloat16


def tile_monarch(x_ref, lanes, w1_ref, w2_ref, w3_ref, w4_ref, z_refs, u_refs, store):
    def spread(refs, rows, value):
        for i in range(lanes):
            refs[i][rows, :] = value[:, i * T : (i + 1) * T]

    def strided(refs, start):
        parts = [refs[i][pl.ds(start, NB, stride=NB), :] for i in range(lanes)]
        return jnp.concatenate(parts, axis=1).astype(BF16)

    def up(a, carry):
        rows = pl.ds(pl.multiple_of(a * DB, DB), DB)
        x = x_ref[rows, : lanes * T]
        spread(z_refs, rows, jnp.dot(w1_ref[0, a], x, preferred_element_type=F32))
        return carry

    lax.fori_loop(0, NB, up, 0, unroll=8)

    def middle(j, carry):
        hidden = jnp.dot(w2_ref[0, j], strided(z_refs, j), preferred_element_type=F32)
        hidden = (0.5 * hidden) * (1.0 + lax.erf(hidden * (0.5**0.5)))
        u = jnp.dot(w3_ref[0, j], hidden.astype(BF16), preferred_element_type=F32)
        spread(u_refs, pl.ds(pl.multiple_of(j * NB, NB), NB), u)
        return carry

    lax.fori_loop(0, NB, middle, 0, unroll=4)

    def down(k, carry):
        rows = pl.ds(pl.multiple_of(k * DB, DB), DB)
        store(rows, jnp.dot(w4_ref[0, k], strided(u_refs, k), preferred_element_type=F32))
        return carry

    lax.fori_loop(0, NB, down, 0, unroll=8)


def shared_kernel(x_ref, w1_ref, w2_ref, w3_ref, w4_ref, o_ref, z_ref, u_ref):
    def store(rows, value):
        o_ref[rows, :] = value.astype(BF16)

    tile_monarch(x_ref, 1, w1_ref, w2_ref, w3_ref, w4_ref, (z_ref,), (u_ref,), store)


def routed_kernel(
    counts_ref, pos_ref, gate_ref, x_ref, w1_ref, w2_ref, w3_ref, w4_ref,
    o_ref, x_scr, z0_ref, z1_ref, u0_ref, u1_ref,
):
    expert, tile = pl.program_id(0), pl.program_id(1)
    left = counts_ref[expert] - tile * 2 * T
    sources = x_ref.shape[0]

    @pl.when(left <= T)
    def _():
        o_ref[...] = jnp.zeros_like(o_ref)

    def serve(lanes):
        width = lanes * T
        wanted = lax.broadcasted_iota(jnp.int32, (width, 2 * T), 0) + tile * 2 * T
        step = D // 8

        for part in range(8):
            rows = pl.ds(part * step, step)

            def pick(pair, total):
                both = jnp.concatenate([x_ref[2 * pair, rows, :], x_ref[2 * pair + 1, rows, :]], axis=1)
                onehot = (wanted == pos_ref[0, pair, :, :]).astype(F32).astype(BF16)
                return total + lax.dot_general(
                    both, onehot, (((1,), (1,)), ((), ())), preferred_element_type=F32
                )

            total = lax.fori_loop(0, sources // 2, pick, jnp.zeros((step, width), F32))
            x_scr[rows, :width] = total.astype(BF16)

        gate = gate_ref[0, 0][:, :width]

        def store(rows, value):
            o_ref[rows, :width] = (value * gate).astype(BF16)

        tile_monarch(
            x_scr, lanes, w1_ref, w2_ref, w3_ref, w4_ref, (z0_ref, z1_ref), (u0_ref, u1_ref), store
        )

    @pl.when(left > T)
    def _():
        serve(2)

    @pl.when(jnp.logical_and(left > 0, left <= T))
    def _():
        serve(1)


def weight_specs(index_map, buffers=2):
    shapes = ((NB, DB), (HB, NB), (NB, HB), (DB, NB))
    mode = pl.Buffered(buffers)
    return [pl.BlockSpec((1, NB) + shape, index_map, pipeline_mode=mode) for shape in shapes]


def turned(factors):
    return tuple(jnp.swapaxes(w, -1, -2) for w in factors)


def shared_call(x_t, factors):
    return pl.pallas_call(
        shared_kernel,
        out_shape=jax.ShapeDtypeStruct((D, T), BF16),
        grid=(1,),
        in_specs=[pl.BlockSpec((D, T), lambda i: (0, 0))] + weight_specs(lambda i: (0, 0, 0, 0)),
        out_specs=pl.BlockSpec((D, T), lambda i: (0, 0)),
        scratch_shapes=[pltpu.VMEM((D, T), F32), pltpu.VMEM((D, T), F32)],
        compiler_params=pltpu.CompilerParams(vmem_limit_bytes=56 * 2**20),
        cost_estimate=pl.CostEstimate(flops=10**10, bytes_accessed=10**7, transcendentals=0),
        name="shared_expert",
    )(x_t, *factors)


def routed_call(counts, pos, slot_gates, x_all, factors, tiles):
    residents = pos.shape[0]
    sources = x_all.shape[0]
    grid_spec = pltpu.PrefetchScalarGridSpec(
        num_scalar_prefetch=1,
        grid=(residents, tiles),
        in_specs=[
            pl.BlockSpec((1, sources // 2, 1, 2 * T), lambda e, i, c: (e, 0, 0, 0)),
            pl.BlockSpec((1, 1, 1, 2 * T), lambda e, i, c: (e, i, 0, 0)),
            pl.BlockSpec((sources, x_all.shape[1], T), lambda e, i, c: (0, 0, 0), pipeline_mode=pl.Buffered(1)),
        ]
        + weight_specs(lambda e, i, c: (e, 0, 0, 0), 2 if sources <= 8 else 1),
        out_specs=pl.BlockSpec((D, 2 * T), lambda e, i, c: (0, e * tiles + i)),
        scratch_shapes=[pltpu.VMEM((D, 2 * T), BF16)] + [pltpu.VMEM((D, T), F32)] * 4,
    )
    return pl.pallas_call(
        routed_kernel,
        out_shape=jax.ShapeDtypeStruct((D, residents * tiles * 2 * T), BF16),
        grid_spec=grid_spec,
        compiler_params=pltpu.CompilerParams(vmem_limit_bytes=62 * 2**20),
        cost_estimate=pl.CostEstimate(flops=4 * 10**10, bytes_accessed=2 * 10**7, transcendentals=0),
        name="routed_experts",
    )(counts, pos, slot_gates, x_all, *factors)


def combine_kernel(depth, window, starts_ref, pos_ref, o_ref, y_ref):
    residents = starts_ref.shape[0]
    pair = pl.program_id(0)
    wanted = lax.broadcasted_iota(jnp.int32, (window, 2 * T), 0)
    begins = [pl.multiple_of(starts_ref[e, pair] * T, T) for e in range(residents)]
    hots = [
        (wanted + begins[e] == pos_ref[e, 0, :, :]).astype(F32).astype(BF16) for e in range(residents)
    ]
    hot = jnp.concatenate(hots, axis=0)
    step = 512

    def part(i, carry):
        rows = pl.ds(pl.multiple_of(i * step, step), step)
        near = [
            o_ref[rows, pl.ds(pl.multiple_of(begins[e] + e * depth, T), window)] for e in range(residents)
        ]
        total = jnp.dot(jnp.concatenate(near, axis=1), hot, preferred_element_type=F32).astype(BF16)
        y_ref[0, rows, :] = total[:, :T]
        y_ref[1, rows, :] = total[:, T:]
        return carry

    lax.fori_loop(0, D // step, part, 0)


def combine_call(starts, pos, outs, sources, depth, window):
    residents = pos.shape[0]
    grid_spec = pltpu.PrefetchScalarGridSpec(
        num_scalar_prefetch=1,
        grid=(sources // 2,),
        in_specs=[
            pl.BlockSpec((residents, 1, 1, 2 * T), lambda s, c: (0, s, 0, 0)),
            pl.BlockSpec((D, residents * depth), lambda s, c: (0, 0), pipeline_mode=pl.Buffered(1)),
        ],
        out_specs=pl.BlockSpec((2, D, T), lambda s, c: (s, 0, 0)),
    )
    return pl.pallas_call(
        functools.partial(combine_kernel, depth, window),
        out_shape=jax.ShapeDtypeStruct((sources, D, T), BF16),
        grid_spec=grid_spec,
        compiler_params=pltpu.CompilerParams(vmem_limit_bytes=48 * 2**20),
        name="combine",
    )(starts, pos, outs)


def grid_of(count):
    side = math.isqrt(count // 2)
    return count // side, side


def greet(z, y, nz, ny):
    barrier = pltpu.get_barrier_semaphore()
    for other in range(1, ny):
        pl.semaphore_signal(barrier, inc=1, device_id={"expert": z * ny + lax.rem(y + other, ny)})

    @pl.when(z > 0)
    def _():
        pl.semaphore_signal(barrier, inc=1, device_id={"expert": (z - 1) * ny + y})

    @pl.when(z < nz - 1)
    def _():
        pl.semaphore_signal(barrier, inc=1, device_id={"expert": (z + 1) * ny + y})

    peers = ny - 1 + jnp.where(z > 0, 1, 0) + jnp.where(z < nz - 1, 1, 0)
    pl.semaphore_wait(barrier, peers)


def gather_kernel(nz, x_ref, out_ref, own_sem, up_sem, down_sem, side_sem, recv_sem):
    ny = 2
    me = lax.axis_index("expert")
    z, y = me // ny, lax.rem(me, ny)
    beside = z * ny + (1 - y)

    def send(block, src, sem, target):
        return pltpu.make_async_remote_copy(
            src_ref=src, dst_ref=out_ref.at[block], send_sem=sem.at[block],
            recv_sem=recv_sem.at[block], device_id={"expert": target},
        )

    def arrived(block):
        send(block, out_ref.at[block], side_sem, beside).wait_recv()

    greet(z, y, nz, ny)
    own = pltpu.make_async_copy(x_ref, out_ref.at[me], own_sem)
    own.start()

    @pl.when(z < nz - 1)
    def _():
        send(me, x_ref, up_sem, me + ny).start()

    @pl.when(z > 0)
    def _():
        send(me, x_ref, down_sem, me - ny).start()

    send(me, x_ref, side_sem, beside).start()

    for k in range(1, nz):
        block = me - k * ny

        @pl.when(z >= k)
        def _():
            arrived(block)

            @pl.when(z < nz - 1)
            def _():
                send(block, out_ref.at[block], up_sem, me + ny).start()

            send(block, out_ref.at[block], side_sem, beside).start()

        later = me + k * ny

        @pl.when(z + k < nz)
        def _():
            arrived(later)

            @pl.when(z > 0)
            def _():
                send(later, out_ref.at[later], down_sem, me - ny).start()

            send(later, out_ref.at[later], side_sem, beside).start()

    for other in range(nz):
        arrived(other * ny + (1 - y))
    own.wait()
    for other in range(nz):
        block = other * ny + y
        send(block, out_ref.at[block], side_sem, beside).wait_send()

        @pl.when(jnp.logical_and(other <= z, z < nz - 1))
        def _():
            send(block, out_ref.at[block], up_sem, me + ny).wait_send()

        @pl.when(jnp.logical_and(other >= z, z > 0))
        def _():
            send(block, out_ref.at[block], down_sem, me - ny).wait_send()


def gather_tokens(x_t):
    count = lax.axis_size("expert")
    nz, ny = grid_of(count)
    if ny != 2:
        return lax.all_gather(x_t, "expert", axis=0, tiled=False)
    sems = pltpu.SemaphoreType.DMA((count,))
    return pl.pallas_call(
        functools.partial(gather_kernel, nz),
        out_shape=jax.ShapeDtypeStruct((count,) + x_t.shape, x_t.dtype),
        in_specs=[pl.BlockSpec(memory_space=pl.ANY)],
        out_specs=pl.BlockSpec(memory_space=pl.ANY),
        scratch_shapes=[pltpu.SemaphoreType.DMA, sems, sems, sems, sems],
        compiler_params=pltpu.CompilerParams(collective_id=0, has_side_effects=True),
        cost_estimate=pl.CostEstimate(flops=10**11, bytes_accessed=3 * 10**8, transcendentals=0),
        name="gather_tokens",
    )(x_t)


def scatter_kernel(
    nz, y_hbm, out_ref, held, beside_in, below_in, above_in,
    load_sem, side_sem, side_recv, up_sem, up_recv, down_sem, down_recv,
):
    ny = 2
    me = lax.axis_index("expert")
    z, y = me // ny, lax.rem(me, ny)
    beside = z * ny + (1 - y)

    def load(target):
        return pltpu.make_async_copy(y_hbm.at[target * ny + y], held.at[target], load_sem.at[target])

    def side(target):
        return pltpu.make_async_remote_copy(
            src_ref=y_hbm.at[target * ny + (1 - y)], dst_ref=beside_in.at[target],
            send_sem=side_sem.at[target], recv_sem=side_recv.at[target],
            device_id={"expert": beside},
        )

    def up(target):
        return pltpu.make_async_remote_copy(
            src_ref=held.at[target], dst_ref=below_in.at[target], send_sem=up_sem.at[target],
            recv_sem=up_recv.at[target], device_id={"expert": me + ny},
        )

    def down(target):
        return pltpu.make_async_remote_copy(
            src_ref=held.at[target], dst_ref=above_in.at[target], send_sem=down_sem.at[target],
            recv_sem=down_recv.at[target], device_id={"expert": me - ny},
        )

    def add(target, ref):
        step = 512

        def body(i, carry):
            rows = pl.ds(pl.multiple_of(i * step, step), step)
            total = held[target, rows, :].astype(F32) + ref[target, rows, :].astype(F32)
            held[target, rows, :] = total.astype(BF16)
            return carry

        lax.fori_loop(0, D // step, body, 0)

    greet(z, y, nz, ny)
    for k in range(nz - 1, -1, -1):
        @pl.when(z + k < nz)
        def _():
            side(z + k).start()

        if k > 0:
            @pl.when(z - k >= 0)
            def _():
                side(z - k).start()

    for target in range(nz):
        load(target).start()
    for target in range(nz):
        load(target).wait()
    for k in range(nz - 1, 0, -1):
        target = z + k

        @pl.when(z + k < nz)
        def _():
            side(target).wait_recv()
            add(target, beside_in)

            @pl.when(z > 0)
            def _():
                up(target).wait_recv()
                add(target, below_in)

            up(target).start()

        lower = z - k

        @pl.when(z - k >= 0)
        def _():
            side(lower).wait_recv()
            add(lower, beside_in)

            @pl.when(z < nz - 1)
            def _():
                down(lower).wait_recv()
                add(lower, above_in)

            down(lower).start()

    side(z).wait_recv()
    add(z, beside_in)

    @pl.when(z > 0)
    def _():
        up(z).wait_recv()
        add(z, below_in)

    @pl.when(z < nz - 1)
    def _():
        down(z).wait_recv()
        add(z, above_in)

    out_ref[...] = held[z]
    for target in range(nz):
        side(target).wait_send()

        @pl.when(target > z)
        def _():
            up(target).wait_send()

        @pl.when(target < z)
        def _():
            down(target).wait_send()


def scatter_sums(sums):
    count = lax.axis_size("expert")
    nz, ny = grid_of(count)
    if ny != 2:
        return lax.psum_scatter(sums, "expert", scatter_dimension=0, tiled=False)
    block = pltpu.VMEM((nz,) + sums.shape[1:], sums.dtype)
    sems = pltpu.SemaphoreType.DMA((nz,))
    return pl.pallas_call(
        functools.partial(scatter_kernel, nz),
        out_shape=jax.ShapeDtypeStruct(sums.shape[1:], sums.dtype),
        in_specs=[pl.BlockSpec(memory_space=pl.ANY)],
        out_specs=pl.BlockSpec(memory_space=pltpu.VMEM),
        scratch_shapes=[block] * 4 + [sems] * 7,
        compiler_params=pltpu.CompilerParams(
            collective_id=1, has_side_effects=True, vmem_limit_bytes=40 * 2**20
        ),
        cost_estimate=pl.CostEstimate(flops=10**11, bytes_accessed=3 * 10**8, transcendentals=0),
        name="scatter_sums",
    )(sums)


ROWS = D + 16
CAP = 48
CHUNK = 256
CHUNKS = D // CHUNK
LAG = 5
SPANS = ((0, 1024), (1024, 1024), (2048, 1280), (3328, ROWS - 3328))
EIGHTS = (0, 8, 16, 24)
KEPT = NB // 2
LEGS = ((1, 0, 8, 0), (0, 0, 16, 0), (1, 8, 8, 0), (1, 16, 8, 0), (1, 24, 8, 0), (3, 0, 16, 0)) + tuple(
    (2, start, 8, k) for k in (0, KEPT) for start in EIGHTS
)


def dot(a, b):
    return jnp.dot(a, b, preferred_element_type=F32)


def dot_turned(w, x):
    return lax.dot_general(w, x, (((0,), (0,)), ((), ())), preferred_element_type=F32)


def gelu(hidden):
    return ((0.5 * hidden) * (1.0 + lax.erf(hidden * (0.5**0.5)))).astype(BF16)


def aligned(start, step):
    return pl.ds(pl.multiple_of(start, step), step)


def apart(upper, lower):
    top, bottom = [], []
    for a, b in zip(upper, lower):
        top += [a, jnp.zeros_like(a)]
        bottom += [jnp.zeros_like(b), b]
    return jnp.concatenate([jnp.concatenate(top, axis=1), jnp.concatenate(bottom, axis=1)], axis=0)


def strided(ref, tiles, start):
    return [ref[i, pl.ds(start, NB, stride=NB), :].astype(BF16) for i in range(tiles)]


def up(tiles, load, w1, z_ref):
    def some(i, carry):
        for q in range(4):
            p = i * 4 + q
            parts = load(aligned(p * 2 * DB, 2 * DB))
            value = dot(w1[p], apart([x[:DB] for x in parts], [x[DB:] for x in parts]))
            for t in range(tiles):
                for side in range(2):
                    at = 2 * t + side
                    z_ref[t, aligned((2 * p + side) * DB, DB), :] = value[:, at * T : (at + 1) * T]
        return carry

    lax.fori_loop(0, NB // 8, some, 0)


def middle(tiles, w2, w3, z_ref, u_ref, first, count):
    batch = min(count, 8 if tiles == 1 else 4)

    def some(i, carry):
        blocks = [first + i * batch + q for q in range(batch)]
        hidden = []
        for j in blocks:
            parts = strided(z_ref, tiles, j)
            rows = parts[0] if tiles == 1 else jnp.concatenate(parts, axis=1)
            hidden.append(gelu(dot_turned(w2[j], rows)))
        for j, h in zip(blocks, hidden):
            value = dot(w3[j], h)
            for t in range(tiles):
                u_ref[t, aligned(j * NB, NB), :] = value[:, t * T : (t + 1) * T]
        return carry

    lax.fori_loop(0, count // batch, some, 0)


def expand(w2, z_ref, h_ref, first, count):
    def some(i, carry):
        blocks = [first + i * 4 + q for q in range(4)]
        hidden = [dot_turned(w2[j], jnp.concatenate(strided(z_ref, 2, j), axis=1)) for j in blocks]
        for j, h in zip(blocks, hidden):
            h_ref[j] = gelu(h)
        return carry

    lax.fori_loop(0, count // 4, some, 0)


def contract(w3, h_ref, u_ref, first, count, start):
    def some(i, carry):
        for q in range(4):
            j = first + i * 4 + q
            value = dot(w3[j, pl.ds(start, KEPT), :], h_ref[j])
            for t in range(2):
                u_ref[t, aligned(j * NB + start, KEPT), :] = value[:, t * T : (t + 1) * T]
        return carry

    lax.fori_loop(0, count // 4, some, 0)


def down(tiles, w4, u_ref, store, first, count):
    batch = min(count, 4)

    def some(i, carry):
        for q in range(batch):
            p = first + i * batch + q
            value = dot(w4[p], apart(strided(u_ref, tiles, 2 * p), strided(u_ref, tiles, 2 * p + 1)))
            for side in range(2):
                parts = [value[:, (2 * t + side) * T : (2 * t + side + 1) * T] for t in range(tiles)]
                store(aligned((2 * p + side) * DB, DB), parts)
        return carry

    lax.fori_loop(0, count // batch, some, 0)


def pack_pairs(src, dst, first, count):
    def some(i, carry):
        for q in range(4):
            p = i * 4 + q
            both = jnp.concatenate([src[2 * p], src[2 * p + 1]], axis=0)
            dst[first + p] = both.T
        return carry

    lax.fori_loop(0, count // 4, some, 0)


def layer_kernel(
    tok, ids, codes, r1, r2, r3, r4, s1, s2, s3, s4, out_ref,
    x_all, a1, a2, a3, a4, b1, b2, b3, b4, c1, c2, c3, c4,
    slots, z_ref, u_ref, hot, hot_t, share, shared_out, core_in, y_in, z_in,
    tok_in, r_in, s1_in, s4_in, h_ref,
    local_sem, x_send, x_recv, b_send, b_recv, c_send, c_recv, sum_send, sum_recv,
):
    e, d = lax.axis_index("expert"), lax.axis_index("dp")
    z, y, x, c = e // 2, lax.rem(e, 2), d // 2, lax.rem(d, 2)
    near_z = e + 2 - 4 * lax.rem(z, 2)
    on_far = {"expert": lax.rem(e + 4, 8), "dp": d}
    on_near = {"expert": near_z, "dp": d}
    on_y = {"expert": e + 1 - 2 * y, "dp": d}
    on_core = {"expert": e, "dp": d + 1 - 2 * c}
    on_x = {"expert": e, "dp": lax.rem(d + 2, 4)}
    own_a, own_b, own_s = (a1, a2, a3, a4), (b1, b2, b3, b4), (c1, c2, c3, c4)

    def remote(src, dst, send, recv, target):
        return pltpu.make_async_remote_copy(
            src_ref=src, dst_ref=dst, send_sem=send, recv_sem=recv, device_id=target
        )

    def x_copy(number, source, slot, rows, target):
        return remote(
            x_all.at[source, rows], x_all.at[slot, rows], x_send.at[number], x_recv.at[number], target
        )

    whole = pl.ds(0, ROWS)
    spans = [pl.ds(*s) for s in SPANS]
    x_core = x_copy(0, 0, 1, whole, on_core)
    x_y = x_copy(1, 0, 2, whole, on_y)
    x_far = [x_copy(2 + i, 0, 4, rows, on_far) for i, rows in enumerate(spans)]
    x_y_core = x_copy(6, 2, 3, whole, on_core)
    x_far_core = [x_copy(7 + i, 4, 5, rows, on_core) for i, rows in enumerate(spans)]
    x_far_y = [x_copy(11 + i, 4, 6, rows, on_y) for i, rows in enumerate(spans)]
    x_last = [x_copy(15 + i, 6, 7, rows, on_core) for i, rows in enumerate(spans)]

    def leg(number, half, first):
        w, start, size, k = LEGS[number]
        rows = pl.ds(half * (16 if w in (0, 3) else 32) + start, size)
        where = (rows, pl.ds(k, KEPT)) if w == 2 else rows
        src = (a1, r2.at[c], r3.at[c], a4)[w] if first else own_b[w]
        at = number if first else number + len(LEGS)
        return remote(
            src.at[where], own_b[w].at[where], b_send.at[at], b_recv.at[at], on_near if first else on_x
        )

    b_near = [leg(n, x, True) for n in range(len(LEGS))]
    b_x = [leg(n, x, False) for n in range(len(LEGS))]
    b_there = [leg(n, 1 - x, False) for n in range(len(LEGS))]

    def quarter(w, at, number, target, src=None):
        size = 8 if w in (0, 3) else 16
        rows = pl.ds(at * size, size)
        src = own_s[w].at[rows] if src is None else src
        return remote(src, own_s[w].at[rows], c_send.at[number], c_recv.at[number], target)

    sources = (None, s2, s3, None)
    c_core = [quarter(w, d, w, on_core, sources[w]) for w in range(4)]
    c_x = [quarter(w, d, 4 + w, on_x, sources[w]) for w in range(4)]
    c_fwd = [quarter(w, lax.rem(d + 2, 4), 8 + w, on_core) for w in range(4)]

    def local(number, src, dst):
        return pltpu.make_async_copy(src, dst, local_sem.at[number])

    here_s = pl.ds(d * 16, 16)
    tok_load = local(0, tok, tok_in)
    r1_load = local(1, r1.at[c], r_in)
    r4_load = local(2, r4.at[c], r_in)
    r_loads = [local(3, r2.at[c], a2), local(4, r3.at[c], a3)]
    s_packs = [local(5, s1, s1_in), local(6, s4, s4_in)]
    s_loads = [local(7, s2, c2.at[here_s]), local(8, s3, c3.at[here_s])]
    for copy in [tok_load, r1_load] + s_packs:
        copy.start()

    barrier = pltpu.get_barrier_semaphore()
    for target in (on_far, on_near, on_y, on_core, on_x):
        pl.semaphore_signal(barrier, inc=1, device_id=target)
    pl.semaphore_wait(barrier, 5)

    b_near[0].start()
    for copy in s_packs:
        copy.wait()
    pack_pairs(s1_in, c1, d * 8, 8)
    for w in range(3):
        c_x[w].start()
    numbers = [ref[...].astype(F32) for ref in (ids, codes)]
    extra = jnp.concatenate(numbers + [jnp.zeros((ROWS - D - 4, T), F32)], axis=0)
    x_all[0, D:ROWS, :] = extra.astype(BF16)
    tok_load.wait()
    for i in range(4):
        for at in range(SPANS[i][0], min(D, sum(SPANS[i])), 256):
            x_all[0, at : at + 256, :] = tok_in[:, at : at + 256].T
        x_far[i].start()
    x_y.start()
    x_core.start()
    r1_load.wait()
    pack_pairs(r_in, a1, 0, 32)
    r4_load.start()
    for n in (1, 2, 3, 4):
        b_near[n].start()
    pack_pairs(s4_in, c4, d * 8, 8)
    c_x[3].start()
    for copy in c_core + r_loads + s_loads:
        copy.start()
    r4_load.wait()
    pack_pairs(r_in, a4, 0, 32)
    for copy in b_near[5:]:
        copy.start()

    ids_a = (2 * e + c).astype(F32)
    ids_b = (2 * near_z + c).astype(F32)

    def prepare(q):
        extra = jnp.concatenate(
            [x_all[2 * q, D:ROWS, :].astype(F32), x_all[2 * q + 1, D:ROWS, :].astype(F32)], axis=1
        )
        id0, id1, code0, code1 = (extra[i : i + 1] for i in range(4))
        lane = lax.broadcasted_iota(jnp.int32, (1, 2 * T), 1)
        before = lax.broadcasted_iota(jnp.int32, (2 * T, 2 * T), 0)
        after = lax.broadcasted_iota(jnp.int32, (2 * T, 2 * T), 1)
        tri = jnp.logical_and(before < after, (before < T) == (after < T))
        tri = tri.astype(F32).astype(BF16)
        row8 = lax.broadcasted_iota(jnp.int32, (8, 2 * T), 0)
        picks = [jnp.logical_or(id0 == n, id1 == n) for n in (ids_a, ids_b)]
        names = [jnp.where(p, 1.0, 0.0) for p in picks]
        codes = [jnp.where(id0 == n, code0, code1) for n in (ids_a, ids_b)]
        stacked = jnp.where(row8 == 0, names[0], jnp.where(row8 == 1, names[1], 0.0))
        ranks = dot(stacked.astype(BF16), tri)
        base = jnp.where(lane < T, 2 * q * CAP, (2 * q + 1) * CAP).astype(F32)
        places = [
            jnp.where(picks[n], ranks[n : n + 1] + base, -1000.0).astype(jnp.int32) for n in range(2)
        ]
        for tile, half in ((q, 0), (q - 1, 1)):
            if not 0 <= tile < 3:
                continue
            wanted = lax.broadcasted_iota(jnp.int32, (T, 2 * T), 0) + tile * T
            for n in range(2):
                own = (wanted == places[n]).astype(F32).astype(BF16)
                hot[q, half * 2 * T + n * T : half * 2 * T + (n + 1) * T, :] = own
                hot_t[tile, half * 2 * T : (half + 1) * 2 * T, n * T : (n + 1) * T] = own.T
                values = jnp.where(
                    row8 == 0, codes[n], jnp.where(row8 == 1, code0, jnp.where(row8 == 2, code1, 0.0))
                )
                got = lax.dot_general(
                    values.astype(BF16), own, (((1,), (1,)), ((), ())), preferred_element_type=F32
                )
                if half == 0:
                    share[n, tile] = got
                else:
                    share[n, tile] += got

    def pick(tile):
        def some(i, carry):
            rows = aligned(i * 512, 512)
            blocks = [x_all[2 * tile + n, rows, :] for n in range(4)]
            total = dot(jnp.concatenate(blocks, axis=1), hot_t[tile])
            total = total.astype(BF16)
            slots[0, tile, rows, :] = total[:, :T]
            slots[1, tile, rows, :] = total[:, T:]
            return carry

        lax.fori_loop(0, D // 512, some, 0)

    def slot_loader(n, first, count):
        return lambda rows: [slots[n, first + i, rows, :] for i in range(count)]

    def slot_storer(n, first, count):
        gates = []
        for i in range(count):
            got = share[n, first + i]
            under = got[1:2] + got[2:3]
            gates.append(jnp.where(under > 0.0, got[0:1] / jnp.maximum(under, 1.0), 0.0))
        gates = [jnp.broadcast_to(g, (DB, T)) for g in gates]

        def store(rows, parts):
            for i in range(count):
                slots[n, first + i, rows, :] = (parts[i] * gates[i]).astype(BF16)

        return store

    def forward(i):
        x_far[i].wait_recv()
        x_far_y[i].start()
        x_far_core[i].start()

    def relay(*numbers):
        for n in numbers:
            b_near[n].wait_recv()
            b_x[n].start()

    def last_hop(i):
        x_far_y[i].wait_recv()
        x_last[i].start()

    here, there = x * 32, 32 - x * 32
    z_s, u_s = z_ref.at[pl.ds(1, 1)], u_ref.at[pl.ds(1, 1)]
    z_one, u_one = z_ref.at[pl.ds(0, 1)], u_ref.at[pl.ds(0, 1)]
    x_core.wait_recv()
    prepare(0)
    for copy in s_loads:
        copy.wait()
    for copy in c_core:
        copy.wait_recv()
    c_x[0].wait_recv()
    c_fwd[0].start()
    c_fwd[0].wait_recv()
    up(1, lambda rows: [x_all[0, rows, :]], c1, z_s)
    middle(1, c2, c3, z_s, u_s, here, NB // 2)
    relay(0)
    x_y.wait_recv()
    x_y_core.start()
    x_y_core.wait_recv()
    prepare(1)
    pick(0)
    forward(0)
    for copy in r_loads:
        copy.wait()
    up(1, slot_loader(0, 0, 1), a1, z_ref)
    for copy in c_x[1:]:
        copy.wait_recv()
    for copy in c_fwd[1:]:
        copy.start()
    middle(1, a2, a3, z_ref, u_ref, 0, NB)
    relay(1)
    forward(1)
    down(1, a4, u_ref, slot_storer(0, 0, 1), 0, NB // 2)
    last_hop(0)
    for copy in c_fwd[1:]:
        copy.wait_recv()

    def keep_shared(rows, parts):
        shared_out[rows, :] = parts[0].astype(BF16)

    relay(2)
    middle(1, c2, c3, z_s, u_s, there, NB // 2)
    down(1, c4, u_s, keep_shared, 0, NB // 2)
    forward(2)
    last_hop(1)
    b_there[1].wait_recv()
    up(1, slot_loader(1, 0, 1), b1, z_one)
    forward(3)
    relay(3)
    for copy in x_far_core:
        copy.wait_recv()
    prepare(2)
    pick(1)
    up(1, slot_loader(0, 1, 1), a1, z_s)
    middle(1, a2, a3, z_s, u_s, 0, NB // 2)
    relay(4)
    last_hop(2)
    middle(1, a2, a3, z_s, u_s, NB // 2, NB // 2)
    last_hop(3)
    down(1, a4, u_s, slot_storer(0, 1, 1), 0, NB // 2)
    relay(5)
    for copy in x_last:
        copy.wait_recv()
    prepare(3)
    pick(2)
    up(1, slot_loader(0, 2, 1), a1, z_s)
    middle(1, a2, a3, z_s, u_one, 0, NB // 2)
    relay(6, 7)
    middle(1, a2, a3, z_s, u_one, NB // 2, NB // 2)
    down(1, a4, u_one, slot_storer(0, 2, 1), 0, NB // 4)
    relay(8)
    z_two, u_two = z_ref.at[pl.ds(1, 2)], u_ref.at[pl.ds(1, 2)]
    up(2, slot_loader(1, 1, 2), b1, z_two)
    relay(9)
    expand(b2, z_two, h_ref, here, 32)
    for n in (0, 2, 3, 4):
        b_there[n].wait_recv()
    expand(b2, z_two, h_ref, there, 16)
    relay(10)
    expand(b2, z_two, h_ref, there + 16, 16)
    contract(b3, h_ref, u_two, here, 32, 0)
    relay(11)
    b_there[6].wait_recv()
    b_there[7].wait_recv()
    contract(b3, h_ref, u_two, there, 16, 0)
    b_there[8].wait_recv()
    b_there[9].wait_recv()
    contract(b3, h_ref, u_two, there + 16, 16, 0)
    b_there[5].wait_recv()

    for copy in [x_core, x_y, x_y_core] + x_far + x_far_core + x_far_y + x_last:
        copy.wait_send()

    for copy in c_core + c_x + c_fwd:
        copy.wait_send()

    def sum_copy(send, at, src, dst, i, size, target):
        rows = aligned(i * size, size)
        return remote(src.at[rows], dst.at[rows], send, sum_recv.at[at], target)

    def to_core(q, i):
        if q < 2:
            send = c_send.at[4 * q + i]
        else:
            send = x_send.at[i] if q == 2 else sum_send.at[i]
        at = i + (12 + CHUNKS * (q - 2) if q > 1 else 4 * q)
        size = CHUNK if q > 1 else 1024
        return sum_copy(send, at, x_all.at[2 * q + 1], core_in.at[q], i, size, on_core)

    def to_y(q, i):
        send, at = (sum_send.at[CHUNKS + i], 12 + 2 * CHUNKS + i) if q > 1 else (c_send.at[8 + i], 8 + i)
        size = CHUNK if q > 1 else 1024
        return sum_copy(send, at, x_all.at[2 * q], y_in.at[q // 2], i, size, on_y)

    def to_far(i):
        at = 12 + 3 * CHUNKS + i
        return sum_copy(sum_send.at[2 * CHUNKS + i], at, x_all.at[4], z_in, i, CHUNK, on_far)

    def combine(q, i):
        where = [(tile, half) for tile, half in ((q, 0), (q - 1, 1)) if 0 <= tile < 3]
        first, last = where[0][1] * 2 * T, (where[-1][1] + 1) * 2 * T
        size = CHUNK if q > 1 else 1024
        for j in range(size // 256):
            rows = aligned(i * size + j * 256, 256)
            both = jnp.concatenate([slots[n, tile, rows, :] for tile, _ in where for n in range(2)], axis=1)
            total = dot(both, hot[q, first:last, :]).astype(BF16)
            x_all[2 * q, rows, :] = total[:, :T]
            x_all[2 * q + 1, rows, :] = total[:, T:]
        to_core(q, i).start()

    def summed(q, refs, rows):
        total = x_all[2 * q, rows, :].astype(F32)
        for ref in refs:
            total += ref[rows, :].astype(F32)
        return total

    def add(q, refs, i):
        size = CHUNK if q > 1 else 1024
        for j in range(size // 256):
            rows = aligned(i * size + j * 256, 256)
            x_all[2 * q, rows, :] = summed(q, refs, rows).astype(BF16)

    def over_y(q, i):
        to_core(q, i).wait_recv()
        add(q, [core_in.at[q]], i)
        to_y(q, i).start()

    def over_z(i):
        to_core(2, i).wait_recv()
        to_y(3, i).wait_recv()
        add(2, [core_in.at[2], y_in.at[1]], i)
        to_far(i).start()

    store_b = slot_storer(1, 1, 2)

    def begin(i, ahead, lag):
        down(2, b4, u_two, store_b, CHUNK // 128 * i, CHUNK // 128)
        combine(3, i)
        if ahead:
            over_y(3, i - 1)
        combine(2, i)
        if lag:
            over_z(i - LAG)

    def loop(first, last, body):
        lax.fori_loop(first, last, lambda i, carry: (body(i), carry)[1], 0)

    relay(12)
    begin(0, False, False)
    loop(1, 3, lambda i: begin(i, True, False))
    relay(13)
    loop(3, LAG, lambda i: begin(i, True, False))
    loop(LAG, CHUNKS // 2, lambda i: begin(i, True, True))
    over_y(3, CHUNKS // 2 - 1)
    down(1, a4, u_one, slot_storer(0, 2, 1), NB // 4, NB // 4)
    contract(b3, h_ref, u_two, here, 32, KEPT)
    for n in (10, 11, 12, 13):
        b_there[n].wait_recv()
    contract(b3, h_ref, u_two, there, 32, KEPT)
    begin(CHUNKS // 2, False, True)
    loop(CHUNKS // 2 + 1, CHUNKS, lambda i: begin(i, True, True))
    over_y(3, CHUNKS - 1)
    middle(1, b2, b3, z_one, u_one, 0, NB)
    store_one = slot_storer(1, 0, 1)
    for i in range(4):
        down(1, b4, u_one, store_one, 8 * i, 8)
        combine(1, i)
        if i > 0:
            over_y(1, i - 1)
    over_y(1, 3)
    loop(CHUNKS - LAG, CHUNKS, over_z)
    loop(0, 4, lambda i: combine(0, i))
    for i in range(4):
        to_core(0, i).wait_recv()
        to_y(1, i).wait_recv()

    def to_out(i):
        rows = aligned(i * CHUNK, CHUNK)
        return pltpu.make_async_copy(shared_out.at[rows], out_ref.at[rows], x_recv.at[i])

    def finish(i):
        to_far(i).wait_recv()
        for j in range(CHUNK // 256):
            rows = aligned(i * CHUNK + j * 256, 256)
            total = summed(0, [core_in.at[0], y_in.at[0], shared_out, z_in], rows)
            shared_out[rows, :] = total.astype(BF16)
        to_out(i).start()

    loop(0, CHUNKS, finish)

    def drain(i):
        to_core(2, i).wait_send()
        to_core(3, i).wait_send()
        to_y(3, i).wait_send()
        to_far(i).wait_send()
        to_out(i).wait()

    for copy in b_near + b_x:
        copy.wait_send()
    for i in range(4):
        to_core(0, i).wait_send()
        to_core(1, i).wait_send()
        to_y(1, i).wait_send()
    loop(0, CHUNKS, drain)


def layer_call(tokens, expert_ids, gate_codes, shared, routed):
    hbm = pl.BlockSpec(memory_space=pl.ANY)
    vmem = pl.BlockSpec(memory_space=pltpu.VMEM)
    weights = [
        pltpu.VMEM((NB // 2, NB, 2 * DB), BF16), pltpu.VMEM((NB, NB, HB), BF16),
        pltpu.VMEM((NB, NB, HB), BF16), pltpu.VMEM((NB // 2, DB, 2 * NB), BF16),
    ]
    sems = pltpu.SemaphoreType.DMA
    block = pltpu.VMEM((D, T), BF16)
    legs, sums = 2 * len(LEGS), 12 + 4 * CHUNKS
    routed = (routed[0], routed[1], jnp.swapaxes(routed[2], -1, -2), routed[3])
    shared = (shared[0], shared[1], jnp.swapaxes(shared[2], -1, -2), shared[3])
    return pl.pallas_call(
        layer_kernel,
        out_shape=jax.ShapeDtypeStruct((D, T), BF16),
        in_specs=[hbm, vmem, vmem] + [hbm] * 8,
        out_specs=hbm,
        scratch_shapes=[pltpu.VMEM((8, ROWS, T), BF16)]
        + weights * 3
        + [
            pltpu.VMEM((2, 3, D, T), BF16),
            pltpu.VMEM((3, D, T), F32),
            pltpu.VMEM((3, D, T), F32),
            pltpu.VMEM((4, 4 * T, 2 * T), BF16),
            pltpu.VMEM((3, 4 * T, 2 * T), BF16),
            pltpu.VMEM((2, 3, 8, T), F32),
            block,
            pltpu.VMEM((4, D, T), BF16),
            pltpu.VMEM((2, D, T), BF16),
            block,
            pltpu.VMEM((T, D), BF16),
            pltpu.VMEM((NB, DB, NB), BF16),
            pltpu.VMEM((NB // 4, DB, NB), BF16),
            pltpu.VMEM((NB // 4, NB, DB), BF16),
            pltpu.VMEM((NB, HB, 2 * T), BF16),
            sems((9,)), sems((19,)), sems((19,)), sems((legs,)), sems((legs,)),
            sems((12,)), sems((12,)), sems((3 * CHUNKS,)), sems((sums,)),
        ],
        compiler_params=pltpu.CompilerParams(
            collective_id=2, has_side_effects=True, vmem_limit_bytes=63 * 2**20
        ),
        cost_estimate=pl.CostEstimate(flops=10**11, bytes_accessed=3 * 10**8, transcendentals=0),
        name="layer",
    )(tokens, expert_ids.T, gate_codes.T, *routed, *shared).T


def running(ones, width):
    groups = ones.reshape(ones.shape[0], -1, width).astype(F32)
    inside = jnp.einsum("rgt,tu->rgu", groups, jnp.triu(jnp.ones((width, width), F32)))
    count = groups.shape[1]
    earlier = jnp.triu(jnp.ones((count, count), F32), 1)
    before = jnp.einsum("rg,gh->rh", inside[:, :, -1], earlier, precision=lax.Precision.HIGHEST)
    return (inside + before[:, :, None]).reshape(ones.shape).astype(jnp.int32)


def shards(tokens, expert_ids, gate_codes, *factors):
    shared, routed = factors[:4], factors[4:]
    residents = routed[0].shape[0]
    sources = lax.axis_size("expert")
    tok_rows = tokens.shape[0]
    if sources == 8 and lax.axis_size("dp") == 4 and residents == 2:
        return layer_call(tokens, expert_ids, gate_codes, shared, routed)
    experts_all = residents * sources
    capacity = max(2, 6 * tok_rows // experts_all)
    tiles = -(-sources * capacity // (2 * T))
    depth = tiles * 2 * T
    window = min(depth, -(-(T - 1 + 2 * capacity) // T) * T)

    extra = jnp.concatenate([expert_ids, gate_codes], axis=1).T.astype(BF16)
    extra = jnp.pad(extra, ((0, 16 - extra.shape[0]), (0, 0)))
    x_t = jnp.concatenate([tokens.T, extra], axis=0)
    x_all = gather_tokens(x_t)
    ids_all = x_all[:, D : D + 2].astype(jnp.int32)
    codes = x_all[:, D + 2 : D + 4].astype(F32)
    gates_all = codes / jnp.sum(codes, axis=1, keepdims=True)
    mine = lax.axis_index("expert") * residents + jnp.arange(residents, dtype=jnp.int32)
    match = ids_all[None] == mine[:, None, None, None]
    picked = jnp.any(match, axis=2).reshape(residents, sources * tok_rows)
    gate = jnp.sum(jnp.where(match, gates_all[None], 0.0), axis=2).reshape(residents, sources * tok_rows)
    ones = picked.astype(jnp.int32)
    ranks = running(ones, tok_rows)
    counts = ranks[:, -1]
    starts = (ranks - ones).reshape(residents, sources // 2, 2 * T)[:, :, 0]
    starts = jnp.minimum(starts, depth - window) // T
    pos = jnp.where(picked, ranks - 1, -1)
    slots = jnp.arange(depth, dtype=jnp.int32)
    slot_gates = jnp.sum(
        jnp.where(pos[:, None, :] == slots[None, :, None], gate[:, None, :], 0.0), axis=2
    ).reshape(residents, tiles, 1, 2 * T)
    pos = pos.reshape(residents, sources // 2, 1, 2 * T)

    outs = routed_call(counts, pos, slot_gates, x_all, turned(routed), tiles)
    y = combine_call(starts, pos, outs, sources, depth, window)
    sums = scatter_sums(y)
    whole = tuple(lax.all_gather(w, "dp", axis=0, tiled=True)[None] for w in turned(shared))
    shared_t = shared_call(x_t, whole)
    total = shared_t.astype(F32) + sums.astype(F32)
    return total.astype(BF16).T


def solution(mesh):
    in_specs = (
        P(("expert", "dp"), None),
        P(("expert", "dp"), None),
        P(("expert", "dp"), None),
        P("dp", None, None),
        P("dp", None, None),
        P("dp", None, None),
        P("dp", None, None),
        P("expert", None, None, None),
        P("expert", None, None, None),
        P("expert", None, None, None),
        P("expert", None, None, None),
    )
    out_specs = P(("expert", "dp"), None)
    return jax.shard_map(shards, mesh=mesh, in_specs=in_specs, out_specs=out_specs, check_vma=False)
```

```python
import functools
import math

import jax
import jax.numpy as jnp
from jax import lax
from jax.experimental import pallas as pl
from jax.experimental.pallas import tpu as pltpu
from jax.sharding import PartitionSpec as P

D = 4096
NB = 64
DB = 64
HB = 256
T = 128
F32 = jnp.float32
BF16 = jnp.bfloat16


def tile_monarch(x_ref, lanes, w1_ref, w2_ref, w3_ref, w4_ref, z_refs, u_refs, store):
    def spread(refs, rows, value):
        for i in range(lanes):
            refs[i][rows, :] = value[:, i * T : (i + 1) * T]

    def strided(refs, start):
        parts = [refs[i][pl.ds(start, NB, stride=NB), :] for i in range(lanes)]
        return jnp.concatenate(parts, axis=1).astype(BF16)

    def up(a, carry):
        rows = pl.ds(pl.multiple_of(a * DB, DB), DB)
        x = x_ref[rows, : lanes * T]
        spread(z_refs, rows, jnp.dot(w1_ref[0, a], x, preferred_element_type=F32))
        return carry

    lax.fori_loop(0, NB, up, 0, unroll=8)

    def middle(j, carry):
        hidden = jnp.dot(w2_ref[0, j], strided(z_refs, j), preferred_element_type=F32)
        hidden = (0.5 * hidden) * (1.0 + lax.erf(hidden * (0.5**0.5)))
        u = jnp.dot(w3_ref[0, j], hidden.astype(BF16), preferred_element_type=F32)
        spread(u_refs, pl.ds(pl.multiple_of(j * NB, NB), NB), u)
        return carry

    lax.fori_loop(0, NB, middle, 0, unroll=4)

    def down(k, carry):
        rows = pl.ds(pl.multiple_of(k * DB, DB), DB)
        store(rows, jnp.dot(w4_ref[0, k], strided(u_refs, k), preferred_element_type=F32))
        return carry

    lax.fori_loop(0, NB, down, 0, unroll=8)


def shared_kernel(x_ref, w1_ref, w2_ref, w3_ref, w4_ref, o_ref, z_ref, u_ref):
    def store(rows, value):
        o_ref[rows, :] = value.astype(BF16)

    tile_monarch(x_ref, 1, w1_ref, w2_ref, w3_ref, w4_ref, (z_ref,), (u_ref,), store)


def routed_kernel(
    counts_ref, pos_ref, gate_ref, x_ref, w1_ref, w2_ref, w3_ref, w4_ref,
    o_ref, x_scr, z0_ref, z1_ref, u0_ref, u1_ref,
):
    expert, tile = pl.program_id(0), pl.program_id(1)
    left = counts_ref[expert] - tile * 2 * T
    sources = x_ref.shape[0]

    @pl.when(left <= T)
    def _():
        o_ref[...] = jnp.zeros_like(o_ref)

    def serve(lanes):
        width = lanes * T
        wanted = lax.broadcasted_iota(jnp.int32, (width, 2 * T), 0) + tile * 2 * T
        step = D // 8

        for part in range(8):
            rows = pl.ds(part * step, step)

            def pick(pair, total):
                both = jnp.concatenate([x_ref[2 * pair, rows, :], x_ref[2 * pair + 1, rows, :]], axis=1)
                onehot = (wanted == pos_ref[0, pair, :, :]).astype(F32).astype(BF16)
                return total + lax.dot_general(
                    both, onehot, (((1,), (1,)), ((), ())), preferred_element_type=F32
                )

            total = lax.fori_loop(0, sources // 2, pick, jnp.zeros((step, width), F32))
            x_scr[rows, :width] = total.astype(BF16)

        gate = gate_ref[0, 0][:, :width]

        def store(rows, value):
            o_ref[rows, :width] = (value * gate).astype(BF16)

        tile_monarch(
            x_scr, lanes, w1_ref, w2_ref, w3_ref, w4_ref, (z0_ref, z1_ref), (u0_ref, u1_ref), store
        )

    @pl.when(left > T)
    def _():
        serve(2)

    @pl.when(jnp.logical_and(left > 0, left <= T))
    def _():
        serve(1)


def weight_specs(index_map, buffers=2):
    shapes = ((NB, DB), (HB, NB), (NB, HB), (DB, NB))
    mode = pl.Buffered(buffers)
    return [pl.BlockSpec((1, NB) + shape, index_map, pipeline_mode=mode) for shape in shapes]


def turned(factors):
    return tuple(jnp.swapaxes(w, -1, -2) for w in factors)


def shared_call(x_t, factors):
    return pl.pallas_call(
        shared_kernel,
        out_shape=jax.ShapeDtypeStruct((D, T), BF16),
        grid=(1,),
        in_specs=[pl.BlockSpec((D, T), lambda i: (0, 0))] + weight_specs(lambda i: (0, 0, 0, 0)),
        out_specs=pl.BlockSpec((D, T), lambda i: (0, 0)),
        scratch_shapes=[pltpu.VMEM((D, T), F32), pltpu.VMEM((D, T), F32)],
        compiler_params=pltpu.CompilerParams(vmem_limit_bytes=56 * 2**20),
        cost_estimate=pl.CostEstimate(flops=10**10, bytes_accessed=10**7, transcendentals=0),
        name="shared_expert",
    )(x_t, *factors)


def routed_call(counts, pos, slot_gates, x_all, factors, tiles):
    residents = pos.shape[0]
    sources = x_all.shape[0]
    grid_spec = pltpu.PrefetchScalarGridSpec(
        num_scalar_prefetch=1,
        grid=(residents, tiles),
        in_specs=[
            pl.BlockSpec((1, sources // 2, 1, 2 * T), lambda e, i, c: (e, 0, 0, 0)),
            pl.BlockSpec((1, 1, 1, 2 * T), lambda e, i, c: (e, i, 0, 0)),
            pl.BlockSpec((sources, x_all.shape[1], T), lambda e, i, c: (0, 0, 0), pipeline_mode=pl.Buffered(1)),
        ]
        + weight_specs(lambda e, i, c: (e, 0, 0, 0), 2 if sources <= 8 else 1),
        out_specs=pl.BlockSpec((D, 2 * T), lambda e, i, c: (0, e * tiles + i)),
        scratch_shapes=[pltpu.VMEM((D, 2 * T), BF16)] + [pltpu.VMEM((D, T), F32)] * 4,
    )
    return pl.pallas_call(
        routed_kernel,
        out_shape=jax.ShapeDtypeStruct((D, residents * tiles * 2 * T), BF16),
        grid_spec=grid_spec,
        compiler_params=pltpu.CompilerParams(vmem_limit_bytes=62 * 2**20),
        cost_estimate=pl.CostEstimate(flops=4 * 10**10, bytes_accessed=2 * 10**7, transcendentals=0),
        name="routed_experts",
    )(counts, pos, slot_gates, x_all, *factors)


def combine_kernel(depth, window, starts_ref, pos_ref, o_ref, y_ref):
    residents = starts_ref.shape[0]
    pair = pl.program_id(0)
    wanted = lax.broadcasted_iota(jnp.int32, (window, 2 * T), 0)
    begins = [pl.multiple_of(starts_ref[e, pair] * T, T) for e in range(residents)]
    hots = [
        (wanted + begins[e] == pos_ref[e, 0, :, :]).astype(F32).astype(BF16) for e in range(residents)
    ]
    hot = jnp.concatenate(hots, axis=0)
    step = 512

    def part(i, carry):
        rows = pl.ds(pl.multiple_of(i * step, step), step)
        near = [
            o_ref[rows, pl.ds(pl.multiple_of(begins[e] + e * depth, T), window)] for e in range(residents)
        ]
        total = jnp.dot(jnp.concatenate(near, axis=1), hot, preferred_element_type=F32).astype(BF16)
        y_ref[0, rows, :] = total[:, :T]
        y_ref[1, rows, :] = total[:, T:]
        return carry

    lax.fori_loop(0, D // step, part, 0)


def combine_call(starts, pos, outs, sources, depth, window):
    residents = pos.shape[0]
    grid_spec = pltpu.PrefetchScalarGridSpec(
        num_scalar_prefetch=1,
        grid=(sources // 2,),
        in_specs=[
            pl.BlockSpec((residents, 1, 1, 2 * T), lambda s, c: (0, s, 0, 0)),
            pl.BlockSpec((D, residents * depth), lambda s, c: (0, 0), pipeline_mode=pl.Buffered(1)),
        ],
        out_specs=pl.BlockSpec((2, D, T), lambda s, c: (s, 0, 0)),
    )
    return pl.pallas_call(
        functools.partial(combine_kernel, depth, window),
        out_shape=jax.ShapeDtypeStruct((sources, D, T), BF16),
        grid_spec=grid_spec,
        compiler_params=pltpu.CompilerParams(vmem_limit_bytes=48 * 2**20),
        name="combine",
    )(starts, pos, outs)


def grid_of(count):
    side = math.isqrt(count // 2)
    return count // side, side


def greet(z, y, nz, ny):
    barrier = pltpu.get_barrier_semaphore()
    for other in range(1, ny):
        pl.semaphore_signal(barrier, inc=1, device_id={"expert": z * ny + lax.rem(y + other, ny)})

    @pl.when(z > 0)
    def _():
        pl.semaphore_signal(barrier, inc=1, device_id={"expert": (z - 1) * ny + y})

    @pl.when(z < nz - 1)
    def _():
        pl.semaphore_signal(barrier, inc=1, device_id={"expert": (z + 1) * ny + y})

    peers = ny - 1 + jnp.where(z > 0, 1, 0) + jnp.where(z < nz - 1, 1, 0)
    pl.semaphore_wait(barrier, peers)


def gather_kernel(nz, x_ref, out_ref, own_sem, up_sem, down_sem, side_sem, recv_sem):
    ny = 2
    me = lax.axis_index("expert")
    z, y = me // ny, lax.rem(me, ny)
    beside = z * ny + (1 - y)

    def send(block, src, sem, target):
        return pltpu.make_async_remote_copy(
            src_ref=src, dst_ref=out_ref.at[block], send_sem=sem.at[block],
            recv_sem=recv_sem.at[block], device_id={"expert": target},
        )

    def arrived(block):
        send(block, out_ref.at[block], side_sem, beside).wait_recv()

    greet(z, y, nz, ny)
    own = pltpu.make_async_copy(x_ref, out_ref.at[me], own_sem)
    own.start()

    @pl.when(z < nz - 1)
    def _():
        send(me, x_ref, up_sem, me + ny).start()

    @pl.when(z > 0)
    def _():
        send(me, x_ref, down_sem, me - ny).start()

    send(me, x_ref, side_sem, beside).start()

    for k in range(1, nz):
        block = me - k * ny

        @pl.when(z >= k)
        def _():
            arrived(block)

            @pl.when(z < nz - 1)
            def _():
                send(block, out_ref.at[block], up_sem, me + ny).start()

            send(block, out_ref.at[block], side_sem, beside).start()

        later = me + k * ny

        @pl.when(z + k < nz)
        def _():
            arrived(later)

            @pl.when(z > 0)
            def _():
                send(later, out_ref.at[later], down_sem, me - ny).start()

            send(later, out_ref.at[later], side_sem, beside).start()

    for other in range(nz):
        arrived(other * ny + (1 - y))
    own.wait()
    for other in range(nz):
        block = other * ny + y
        send(block, out_ref.at[block], side_sem, beside).wait_send()

        @pl.when(jnp.logical_and(other <= z, z < nz - 1))
        def _():
            send(block, out_ref.at[block], up_sem, me + ny).wait_send()

        @pl.when(jnp.logical_and(other >= z, z > 0))
        def _():
            send(block, out_ref.at[block], down_sem, me - ny).wait_send()


def gather_tokens(x_t):
    count = lax.axis_size("expert")
    nz, ny = grid_of(count)
    if ny != 2:
        return lax.all_gather(x_t, "expert", axis=0, tiled=False)
    sems = pltpu.SemaphoreType.DMA((count,))
    return pl.pallas_call(
        functools.partial(gather_kernel, nz),
        out_shape=jax.ShapeDtypeStruct((count,) + x_t.shape, x_t.dtype),
        in_specs=[pl.BlockSpec(memory_space=pl.ANY)],
        out_specs=pl.BlockSpec(memory_space=pl.ANY),
        scratch_shapes=[pltpu.SemaphoreType.DMA, sems, sems, sems, sems],
        compiler_params=pltpu.CompilerParams(collective_id=0, has_side_effects=True),
        cost_estimate=pl.CostEstimate(flops=10**11, bytes_accessed=3 * 10**8, transcendentals=0),
        name="gather_tokens",
    )(x_t)


def scatter_kernel(
    nz, y_hbm, out_ref, held, beside_in, below_in, above_in,
    load_sem, side_sem, side_recv, up_sem, up_recv, down_sem, down_recv,
):
    ny = 2
    me = lax.axis_index("expert")
    z, y = me // ny, lax.rem(me, ny)
    beside = z * ny + (1 - y)

    def load(target):
        return pltpu.make_async_copy(y_hbm.at[target * ny + y], held.at[target], load_sem.at[target])

    def side(target):
        return pltpu.make_async_remote_copy(
            src_ref=y_hbm.at[target * ny + (1 - y)], dst_ref=beside_in.at[target],
            send_sem=side_sem.at[target], recv_sem=side_recv.at[target],
            device_id={"expert": beside},
        )

    def up(target):
        return pltpu.make_async_remote_copy(
            src_ref=held.at[target], dst_ref=below_in.at[target], send_sem=up_sem.at[target],
            recv_sem=up_recv.at[target], device_id={"expert": me + ny},
        )

    def down(target):
        return pltpu.make_async_remote_copy(
            src_ref=held.at[target], dst_ref=above_in.at[target], send_sem=down_sem.at[target],
            recv_sem=down_recv.at[target], device_id={"expert": me - ny},
        )

    def add(target, ref):
        step = 512

        def body(i, carry):
            rows = pl.ds(pl.multiple_of(i * step, step), step)
            total = held[target, rows, :].astype(F32) + ref[target, rows, :].astype(F32)
            held[target, rows, :] = total.astype(BF16)
            return carry

        lax.fori_loop(0, D // step, body, 0)

    greet(z, y, nz, ny)
    for k in range(nz - 1, -1, -1):
        @pl.when(z + k < nz)
        def _():
            side(z + k).start()

        if k > 0:
            @pl.when(z - k >= 0)
            def _():
                side(z - k).start()

    for target in range(nz):
        load(target).start()
    for target in range(nz):
        load(target).wait()
    for k in range(nz - 1, 0, -1):
        target = z + k

        @pl.when(z + k < nz)
        def _():
            side(target).wait_recv()
            add(target, beside_in)

            @pl.when(z > 0)
            def _():
                up(target).wait_recv()
                add(target, below_in)

            up(target).start()

        lower = z - k

        @pl.when(z - k >= 0)
        def _():
            side(lower).wait_recv()
            add(lower, beside_in)

            @pl.when(z < nz - 1)
            def _():
                down(lower).wait_recv()
                add(lower, above_in)

            down(lower).start()

    side(z).wait_recv()
    add(z, beside_in)

    @pl.when(z > 0)
    def _():
        up(z).wait_recv()
        add(z, below_in)

    @pl.when(z < nz - 1)
    def _():
        down(z).wait_recv()
        add(z, above_in)

    out_ref[...] = held[z]
    for target in range(nz):
        side(target).wait_send()

        @pl.when(target > z)
        def _():
            up(target).wait_send()

        @pl.when(target < z)
        def _():
            down(target).wait_send()


def scatter_sums(sums):
    count = lax.axis_size("expert")
    nz, ny = grid_of(count)
    if ny != 2:
        return lax.psum_scatter(sums, "expert", scatter_dimension=0, tiled=False)
    block = pltpu.VMEM((nz,) + sums.shape[1:], sums.dtype)
    sems = pltpu.SemaphoreType.DMA((nz,))
    return pl.pallas_call(
        functools.partial(scatter_kernel, nz),
        out_shape=jax.ShapeDtypeStruct(sums.shape[1:], sums.dtype),
        in_specs=[pl.BlockSpec(memory_space=pl.ANY)],
        out_specs=pl.BlockSpec(memory_space=pltpu.VMEM),
        scratch_shapes=[block] * 4 + [sems] * 7,
        compiler_params=pltpu.CompilerParams(
            collective_id=1, has_side_effects=True, vmem_limit_bytes=40 * 2**20
        ),
        cost_estimate=pl.CostEstimate(flops=10**11, bytes_accessed=3 * 10**8, transcendentals=0),
        name="scatter_sums",
    )(sums)


ROWS = D + 16
CAP = 48
CHUNK = 256
CHUNKS = D // CHUNK
LAG = 5
SPANS = ((0, 1024), (1024, 1024), (2048, 1280), (3328, ROWS - 3328))
EIGHTS = (0, 8, 16, 24)
KEPT = NB // 2
LEGS = ((1, 0, 8, 0), (0, 0, 16, 0), (1, 8, 8, 0), (1, 16, 8, 0), (1, 24, 4, 0), (1, 28, 4, 0)) + tuple(
    (3, start, 8, 0) for start in (0, 8)
) + tuple(
    (2, start, 8, k) for k in (0, KEPT) for start in EIGHTS
)


def dot(a, b):
    return jnp.dot(a, b, preferred_element_type=F32)


def dot_turned(w, x):
    return lax.dot_general(w, x, (((0,), (0,)), ((), ())), preferred_element_type=F32)


def gelu(hidden):
    return ((0.5 * hidden) * (1.0 + lax.erf(hidden * (0.5**0.5)))).astype(BF16)


def aligned(start, step):
    return pl.ds(pl.multiple_of(start, step), step)


def apart(upper, lower):
    top, bottom = [], []
    for a, b in zip(upper, lower):
        top += [a, jnp.zeros_like(a)]
        bottom += [jnp.zeros_like(b), b]
    return jnp.concatenate([jnp.concatenate(top, axis=1), jnp.concatenate(bottom, axis=1)], axis=0)


def strided(ref, tiles, start):
    return [ref[i, pl.ds(start, NB, stride=NB), :].astype(BF16) for i in range(tiles)]


def up(tiles, load, w1, z_ref):
    def some(i, carry):
        for q in range(4):
            p = i * 4 + q
            parts = load(aligned(p * 2 * DB, 2 * DB))
            value = dot(w1[p], apart([x[:DB] for x in parts], [x[DB:] for x in parts]))
            for t in range(tiles):
                for side in range(2):
                    at = 2 * t + side
                    z_ref[t, aligned((2 * p + side) * DB, DB), :] = value[:, at * T : (at + 1) * T]
        return carry

    lax.fori_loop(0, NB // 8, some, 0)


def middle(tiles, w2, w3, z_ref, u_ref, first, count):
    batch = min(count, 8 if tiles == 1 else 4)

    def some(i, carry):
        blocks = [first + i * batch + q for q in range(batch)]
        hidden = []
        for j in blocks:
            parts = strided(z_ref, tiles, j)
            rows = parts[0] if tiles == 1 else jnp.concatenate(parts, axis=1)
            hidden.append(gelu(dot_turned(w2[j], rows)))
        for j, h in zip(blocks, hidden):
            value = dot(w3[j], h)
            for t in range(tiles):
                u_ref[t, aligned(j * NB, NB), :] = value[:, t * T : (t + 1) * T]
        return carry

    lax.fori_loop(0, count // batch, some, 0)


def expand(w2, z_ref, h_ref, first, count):
    def some(i, carry):
        for q in range(8):
            j = first + i * 8 + q
            h_ref[j] = gelu(dot_turned(w2[j], jnp.concatenate(strided(z_ref, 2, j), axis=1)))
        return carry

    lax.fori_loop(0, count // 8, some, 0)


def contract(w3, h_ref, u_ref, first, count, start):
    def some(i, carry):
        for q in range(8):
            j = first + i * 8 + q
            value = dot(w3[j, pl.ds(start, KEPT), :], h_ref[j])
            for t in range(2):
                u_ref[t, aligned(j * NB + start, KEPT), :] = value[:, t * T : (t + 1) * T]
        return carry

    lax.fori_loop(0, count // 8, some, 0)


def down(tiles, w4, u_ref, store, first, count):
    batch = min(count, 4)

    def some(i, carry):
        for q in range(batch):
            p = first + i * batch + q
            value = dot(w4[p], apart(strided(u_ref, tiles, 2 * p), strided(u_ref, tiles, 2 * p + 1)))
            for side in range(2):
                parts = [value[:, (2 * t + side) * T : (2 * t + side + 1) * T] for t in range(tiles)]
                store(aligned((2 * p + side) * DB, DB), parts)
        return carry

    lax.fori_loop(0, count // batch, some, 0)


def pack_pairs(src, dst, first, count):
    def some(i, carry):
        for q in range(4):
            p = i * 4 + q
            both = jnp.concatenate([src[2 * p], src[2 * p + 1]], axis=0)
            dst[first + p] = both.T
        return carry

    lax.fori_loop(0, count // 4, some, 0)


def layer_kernel(
    tok, ids, codes, r1, r2, r3, r4, s1, s2, s3, s4, out_ref,
    x_all, a1, a2, a3, a4, b1, b2, b3, b4, c1, c2, c3, c4,
    slots, z_ref, u_ref, hot, hot_t, share, shared_out, core_in, y_in, z_in,
    tok_in, r_in, s1_in, s4_in, h_ref,
    local_sem, x_send, x_recv, b_send, b_recv, c_send, c_recv, sum_send, sum_recv,
):
    e, d = lax.axis_index("expert"), lax.axis_index("dp")
    z, y, x, c = e // 2, lax.rem(e, 2), d // 2, lax.rem(d, 2)
    near_z = e + 2 - 4 * lax.rem(z, 2)
    on_far = {"expert": lax.rem(e + 4, 8), "dp": d}
    on_near = {"expert": near_z, "dp": d}
    on_y = {"expert": e + 1 - 2 * y, "dp": d}
    on_core = {"expert": e, "dp": d + 1 - 2 * c}
    on_x = {"expert": e, "dp": lax.rem(d + 2, 4)}
    own_a, own_b, own_s = (a1, a2, a3, a4), (b1, b2, b3, b4), (c1, c2, c3, c4)

    def remote(src, dst, send, recv, target):
        return pltpu.make_async_remote_copy(
            src_ref=src, dst_ref=dst, send_sem=send, recv_sem=recv, device_id=target
        )

    def x_copy(number, source, slot, rows, target):
        return remote(
            x_all.at[source, rows], x_all.at[slot, rows], x_send.at[number], x_recv.at[number], target
        )

    whole = pl.ds(0, ROWS)
    spans = [pl.ds(*s) for s in SPANS]
    x_core = x_copy(0, 0, 1, whole, on_core)
    x_y = x_copy(1, 0, 2, whole, on_y)
    x_far = [x_copy(2 + i, 0, 4, rows, on_far) for i, rows in enumerate(spans)]
    x_y_core = x_copy(6, 2, 3, whole, on_core)
    x_far_core = [x_copy(7 + i, 4, 5, rows, on_core) for i, rows in enumerate(spans)]
    x_far_y = [x_copy(11 + i, 4, 6, rows, on_y) for i, rows in enumerate(spans)]
    x_last = [x_copy(15 + i, 6, 7, rows, on_core) for i, rows in enumerate(spans)]

    def leg(number, half, first):
        w, start, size, k = LEGS[number]
        rows = pl.ds(half * (16 if w in (0, 3) else 32) + start, size)
        where = (rows, pl.ds(k, KEPT)) if w == 2 else rows
        src = (a1, r2.at[c], r3.at[c], a4)[w] if first else own_b[w]
        at = number if first else number + len(LEGS)
        return remote(
            src.at[where], own_b[w].at[where], b_send.at[at], b_recv.at[at], on_near if first else on_x
        )

    b_near = [leg(n, x, True) for n in range(len(LEGS))]
    b_x = [leg(n, x, False) for n in range(len(LEGS))]
    b_there = [leg(n, 1 - x, False) for n in range(len(LEGS))]

    def quarter(w, at, number, target, src=None):
        size = 8 if w in (0, 3) else 16
        rows = pl.ds(at * size, size)
        src = own_s[w].at[rows] if src is None else src
        return remote(src, own_s[w].at[rows], c_send.at[number], c_recv.at[number], target)

    sources = (None, s2, s3, None)
    c_core = [quarter(w, d, w, on_core, sources[w]) for w in range(4)]
    c_x = [quarter(w, d, 4 + w, on_x, sources[w]) for w in range(4)]
    c_fwd = [quarter(w, lax.rem(d + 2, 4), 8 + w, on_core) for w in range(4)]

    def local(number, src, dst):
        return pltpu.make_async_copy(src, dst, local_sem.at[number])

    here_s = pl.ds(d * 16, 16)
    tok_load = local(0, tok, tok_in)
    r1_load = local(1, r1.at[c], r_in)
    r4_load = local(2, r4.at[c], r_in)
    r_loads = [local(3, r2.at[c], a2), local(4, r3.at[c], a3)]
    s_packs = [local(5, s1, s1_in), local(6, s4, s4_in)]
    s_loads = [local(7, s2, c2.at[here_s]), local(8, s3, c3.at[here_s])]
    for copy in [tok_load, r1_load] + s_packs:
        copy.start()

    barrier = pltpu.get_barrier_semaphore()
    for target in (on_far, on_near, on_y, on_core, on_x):
        pl.semaphore_signal(barrier, inc=1, device_id=target)
    pl.semaphore_wait(barrier, 5)

    b_near[0].start()
    for copy in s_packs:
        copy.wait()
    pack_pairs(s1_in, c1, d * 8, 8)
    for w in range(3):
        c_x[w].start()
    numbers = [ref[...].astype(F32) for ref in (ids, codes)]
    extra = jnp.concatenate(numbers + [jnp.zeros((ROWS - D - 4, T), F32)], axis=0)
    x_all[0, D:ROWS, :] = extra.astype(BF16)
    tok_load.wait()
    for i in range(4):
        for at in range(SPANS[i][0], min(D, sum(SPANS[i])), 256):
            x_all[0, at : at + 256, :] = tok_in[:, at : at + 256].T
        x_far[i].start()
    x_y.start()
    x_core.start()
    r1_load.wait()
    pack_pairs(r_in, a1, 0, 32)
    r4_load.start()
    for n in (1, 2, 3, 4, 5):
        b_near[n].start()
    pack_pairs(s4_in, c4, d * 8, 8)
    c_x[3].start()
    for copy in c_core + r_loads + s_loads:
        copy.start()
    r4_load.wait()
    pack_pairs(r_in, a4, 0, 32)
    for copy in b_near[6:]:
        copy.start()

    ids_a = (2 * e + c).astype(F32)
    ids_b = (2 * near_z + c).astype(F32)

    def prepare(q):
        extra = jnp.concatenate(
            [x_all[2 * q, D:ROWS, :].astype(F32), x_all[2 * q + 1, D:ROWS, :].astype(F32)], axis=1
        )
        id0, id1, code0, code1 = (extra[i : i + 1] for i in range(4))
        lane = lax.broadcasted_iota(jnp.int32, (1, 2 * T), 1)
        before = lax.broadcasted_iota(jnp.int32, (2 * T, 2 * T), 0)
        after = lax.broadcasted_iota(jnp.int32, (2 * T, 2 * T), 1)
        tri = jnp.logical_and(before < after, (before < T) == (after < T))
        tri = tri.astype(F32).astype(BF16)
        row8 = lax.broadcasted_iota(jnp.int32, (8, 2 * T), 0)
        picks = [jnp.logical_or(id0 == n, id1 == n) for n in (ids_a, ids_b)]
        names = [jnp.where(p, 1.0, 0.0) for p in picks]
        codes = [jnp.where(id0 == n, code0, code1) for n in (ids_a, ids_b)]
        stacked = jnp.where(row8 == 0, names[0], jnp.where(row8 == 1, names[1], 0.0))
        ranks = dot(stacked.astype(BF16), tri)
        base = jnp.where(lane < T, 2 * q * CAP, (2 * q + 1) * CAP).astype(F32)
        places = [
            jnp.where(picks[n], ranks[n : n + 1] + base, -1000.0).astype(jnp.int32) for n in range(2)
        ]
        for tile, half in ((q, 0), (q - 1, 1)):
            if not 0 <= tile < 3:
                continue
            wanted = lax.broadcasted_iota(jnp.int32, (T, 2 * T), 0) + tile * T
            for n in range(2):
                own = (wanted == places[n]).astype(F32).astype(BF16)
                hot[q, half * 2 * T + n * T : half * 2 * T + (n + 1) * T, :] = own
                hot_t[tile, half * 2 * T : (half + 1) * 2 * T, n * T : (n + 1) * T] = own.T
                values = jnp.where(
                    row8 == 0, codes[n], jnp.where(row8 == 1, code0, jnp.where(row8 == 2, code1, 0.0))
                )
                got = lax.dot_general(
                    values.astype(BF16), own, (((1,), (1,)), ((), ())), preferred_element_type=F32
                )
                if half == 0:
                    share[n, tile] = got
                else:
                    share[n, tile] += got

    def pick(tile):
        def some(i, carry):
            rows = aligned(i * 512, 512)
            blocks = [x_all[2 * tile + n, rows, :] for n in range(4)]
            total = dot(jnp.concatenate(blocks, axis=1), hot_t[tile])
            total = total.astype(BF16)
            slots[0, tile, rows, :] = total[:, :T]
            slots[1, tile, rows, :] = total[:, T:]
            return carry

        lax.fori_loop(0, D // 512, some, 0)

    def slot_loader(n, first, count):
        return lambda rows: [slots[n, first + i, rows, :] for i in range(count)]

    def slot_storer(n, first, count):
        gates = []
        for i in range(count):
            got = share[n, first + i]
            under = got[1:2] + got[2:3]
            gates.append(jnp.where(under > 0.0, got[0:1] / jnp.maximum(under, 1.0), 0.0))
        gates = [jnp.broadcast_to(g, (DB, T)) for g in gates]

        def store(rows, parts):
            for i in range(count):
                slots[n, first + i, rows, :] = (parts[i] * gates[i]).astype(BF16)

        return store

    def forward(i):
        x_far[i].wait_recv()
        x_far_y[i].start()
        x_far_core[i].start()

    def relay(*numbers):
        for n in numbers:
            b_near[n].wait_recv()
            b_x[n].start()

    def last_hop(i):
        x_far_y[i].wait_recv()
        x_last[i].start()

    here, there = x * 32, 32 - x * 32
    z_s, u_s = z_ref.at[pl.ds(1, 1)], u_ref.at[pl.ds(1, 1)]
    z_one, u_one = z_ref.at[pl.ds(0, 1)], u_ref.at[pl.ds(0, 1)]
    x_core.wait_recv()
    prepare(0)
    for copy in s_loads:
        copy.wait()
    for copy in c_core:
        copy.wait_recv()
    c_x[0].wait_recv()
    c_fwd[0].start()
    c_fwd[0].wait_recv()
    up(1, lambda rows: [x_all[0, rows, :]], c1, z_s)
    middle(1, c2, c3, z_s, u_s, here, NB // 2)
    relay(0)
    x_y.wait_recv()
    x_y_core.start()
    x_y_core.wait_recv()
    prepare(1)
    pick(0)
    forward(0)
    for copy in r_loads:
        copy.wait()
    up(1, slot_loader(0, 0, 1), a1, z_ref)
    for copy in c_x[1:]:
        copy.wait_recv()
    for copy in c_fwd[1:]:
        copy.start()
    middle(1, a2, a3, z_ref, u_ref, 0, NB)
    relay(1)
    forward(1)
    down(1, a4, u_ref, slot_storer(0, 0, 1), 0, NB // 2)
    last_hop(0)
    for copy in c_fwd[1:]:
        copy.wait_recv()

    def keep_shared(rows, parts):
        shared_out[rows, :] = parts[0].astype(BF16)

    relay(2)
    middle(1, c2, c3, z_s, u_s, there, NB // 2)
    down(1, c4, u_s, keep_shared, 0, NB // 2)
    forward(2)
    last_hop(1)
    b_there[1].wait_recv()
    up(1, slot_loader(1, 0, 1), b1, z_one)
    forward(3)
    relay(3)
    for copy in x_far_core:
        copy.wait_recv()
    prepare(2)
    pick(1)
    up(1, slot_loader(0, 1, 1), a1, z_s)
    relay(4)
    middle(1, a2, a3, z_s, u_s, 0, NB // 2)
    relay(5)
    last_hop(2)
    middle(1, a2, a3, z_s, u_s, NB // 2, NB // 2)
    relay(6)
    last_hop(3)
    down(1, a4, u_s, slot_storer(0, 1, 1), 0, NB // 2)
    relay(7)
    for copy in x_last:
        copy.wait_recv()
    prepare(3)
    pick(2)
    up(1, slot_loader(0, 2, 1), a1, z_s)
    relay(8)
    middle(1, a2, a3, z_s, u_one, 0, NB // 2)
    relay(9)
    middle(1, a2, a3, z_s, u_one, NB // 2, NB // 2)
    relay(10)
    down(1, a4, u_one, slot_storer(0, 2, 1), 0, NB // 4)
    z_two, u_two = z_ref.at[pl.ds(1, 2)], u_ref.at[pl.ds(1, 2)]
    up(2, slot_loader(1, 1, 2), b1, z_two)
    relay(11)
    expand(b2, z_two, h_ref, here, 32)
    for n in (0, 2, 3, 4, 5):
        b_there[n].wait_recv()
    expand(b2, z_two, h_ref, there, 16)
    relay(12)
    expand(b2, z_two, h_ref, there + 16, 16)
    contract(b3, h_ref, u_two, here, 32, 0)
    relay(13)
    b_there[8].wait_recv()
    b_there[9].wait_recv()
    contract(b3, h_ref, u_two, there, 16, 0)
    b_there[10].wait_recv()
    b_there[11].wait_recv()
    contract(b3, h_ref, u_two, there + 16, 16, 0)
    b_there[6].wait_recv()
    b_there[7].wait_recv()

    for copy in [x_core, x_y, x_y_core] + x_far + x_far_core + x_far_y + x_last:
        copy.wait_send()

    for copy in c_core + c_x + c_fwd:
        copy.wait_send()

    def sum_copy(send, at, src, dst, i, size, target):
        rows = aligned(i * size, size)
        return remote(src.at[rows], dst.at[rows], send, sum_recv.at[at], target)

    def to_core(q, i):
        if q < 2:
            send = c_send.at[4 * q + i]
        else:
            send = x_send.at[i] if q == 2 else sum_send.at[i]
        at = i + (12 + CHUNKS * (q - 2) if q > 1 else 4 * q)
        size = CHUNK if q > 1 else 1024
        return sum_copy(send, at, x_all.at[2 * q + 1], core_in.at[q], i, size, on_core)

    def to_y(q, i):
        send, at = (sum_send.at[CHUNKS + i], 12 + 2 * CHUNKS + i) if q > 1 else (c_send.at[8 + i], 8 + i)
        size = CHUNK if q > 1 else 1024
        return sum_copy(send, at, x_all.at[2 * q], y_in.at[q // 2], i, size, on_y)

    def to_far(i):
        at = 12 + 3 * CHUNKS + i
        return sum_copy(sum_send.at[2 * CHUNKS + i], at, x_all.at[4], z_in, i, CHUNK, on_far)

    def combine(q, i):
        where = [(tile, half) for tile, half in ((q, 0), (q - 1, 1)) if 0 <= tile < 3]
        first, last = where[0][1] * 2 * T, (where[-1][1] + 1) * 2 * T
        size = CHUNK if q > 1 else 1024
        for j in range(size // 256):
            rows = aligned(i * size + j * 256, 256)
            both = jnp.concatenate([slots[n, tile, rows, :] for tile, _ in where for n in range(2)], axis=1)
            total = dot(both, hot[q, first:last, :]).astype(BF16)
            x_all[2 * q, rows, :] = total[:, :T]
            x_all[2 * q + 1, rows, :] = total[:, T:]
        to_core(q, i).start()

    def summed(q, refs, rows):
        total = x_all[2 * q, rows, :].astype(F32)
        for ref in refs:
            total += ref[rows, :].astype(F32)
        return total

    def add(q, refs, i):
        size = CHUNK if q > 1 else 1024
        for j in range(size // 256):
            rows = aligned(i * size + j * 256, 256)
            x_all[2 * q, rows, :] = summed(q, refs, rows).astype(BF16)

    def over_y(q, i):
        to_core(q, i).wait_recv()
        add(q, [core_in.at[q]], i)
        to_y(q, i).start()

    def over_z(i):
        to_core(2, i).wait_recv()
        to_y(3, i).wait_recv()
        add(2, [core_in.at[2], y_in.at[1]], i)
        to_far(i).start()

    store_b = slot_storer(1, 1, 2)

    def begin(i, ahead, lag):
        down(2, b4, u_two, store_b, CHUNK // 128 * i, CHUNK // 128)
        combine(3, i)
        if ahead:
            over_y(3, i - 1)
        combine(2, i)
        if lag:
            over_z(i - LAG)

    def loop(first, last, body):
        lax.fori_loop(first, last, lambda i, carry: (body(i), carry)[1], 0)

    relay(14)
    begin(0, False, False)
    loop(1, 3, lambda i: begin(i, True, False))
    relay(15)
    loop(3, LAG, lambda i: begin(i, True, False))
    loop(LAG, CHUNKS // 2, lambda i: begin(i, True, True))
    over_y(3, CHUNKS // 2 - 1)
    down(1, a4, u_one, slot_storer(0, 2, 1), NB // 4, NB // 4)
    contract(b3, h_ref, u_two, here, 32, KEPT)
    for n in (12, 13, 14, 15):
        b_there[n].wait_recv()
    contract(b3, h_ref, u_two, there, 32, KEPT)
    begin(CHUNKS // 2, False, True)
    loop(CHUNKS // 2 + 1, CHUNKS, lambda i: begin(i, True, True))
    over_y(3, CHUNKS - 1)
    middle(1, b2, b3, z_one, u_one, 0, NB)
    store_one = slot_storer(1, 0, 1)
    for i in range(4):
        down(1, b4, u_one, store_one, 8 * i, 8)
        combine(1, i)
        if i > 0:
            over_y(1, i - 1)
    over_y(1, 3)
    loop(CHUNKS - LAG, CHUNKS, over_z)
    loop(0, 4, lambda i: combine(0, i))
    for i in range(4):
        to_core(0, i).wait_recv()
        to_y(1, i).wait_recv()

    def to_out(i):
        rows = aligned(i * CHUNK, CHUNK)
        return pltpu.make_async_copy(shared_out.at[rows], out_ref.at[rows], x_recv.at[i])

    def finish(i):
        to_far(i).wait_recv()
        for j in range(CHUNK // 256):
            rows = aligned(i * CHUNK + j * 256, 256)
            total = summed(0, [core_in.at[0], y_in.at[0], shared_out, z_in], rows)
            shared_out[rows, :] = total.astype(BF16)
        to_out(i).start()

    loop(0, CHUNKS, finish)

    def drain(i):
        to_core(2, i).wait_send()
        to_core(3, i).wait_send()
        to_y(3, i).wait_send()
        to_far(i).wait_send()
        to_out(i).wait()

    for copy in b_near + b_x:
        copy.wait_send()
    for i in range(4):
        to_core(0, i).wait_send()
        to_core(1, i).wait_send()
        to_y(1, i).wait_send()
    loop(0, CHUNKS, drain)


def layer_call(tokens, expert_ids, gate_codes, shared, routed):
    hbm = pl.BlockSpec(memory_space=pl.ANY)
    vmem = pl.BlockSpec(memory_space=pltpu.VMEM)
    weights = [
        pltpu.VMEM((NB // 2, NB, 2 * DB), BF16), pltpu.VMEM((NB, NB, HB), BF16),
        pltpu.VMEM((NB, NB, HB), BF16), pltpu.VMEM((NB // 2, DB, 2 * NB), BF16),
    ]
    sems = pltpu.SemaphoreType.DMA
    block = pltpu.VMEM((D, T), BF16)
    legs, sums = 2 * len(LEGS), 12 + 4 * CHUNKS
    routed = (routed[0], routed[1], jnp.swapaxes(routed[2], -1, -2), routed[3])
    shared = (shared[0], shared[1], jnp.swapaxes(shared[2], -1, -2), shared[3])
    return pl.pallas_call(
        layer_kernel,
        out_shape=jax.ShapeDtypeStruct((D, T), BF16),
        in_specs=[hbm, vmem, vmem] + [hbm] * 8,
        out_specs=hbm,
        scratch_shapes=[pltpu.VMEM((8, ROWS, T), BF16)]
        + weights * 3
        + [
            pltpu.VMEM((2, 3, D, T), BF16),
            pltpu.VMEM((3, D, T), F32),
            pltpu.VMEM((3, D, T), F32),
            pltpu.VMEM((4, 4 * T, 2 * T), BF16),
            pltpu.VMEM((3, 4 * T, 2 * T), BF16),
            pltpu.VMEM((2, 3, 8, T), F32),
            block,
            pltpu.VMEM((4, D, T), BF16),
            pltpu.VMEM((2, D, T), BF16),
            block,
            pltpu.VMEM((T, D), BF16),
            pltpu.VMEM((NB, DB, NB), BF16),
            pltpu.VMEM((NB // 4, DB, NB), BF16),
            pltpu.VMEM((NB // 4, NB, DB), BF16),
            pltpu.VMEM((NB, HB, 2 * T), BF16),
            sems((9,)), sems((19,)), sems((19,)), sems((legs,)), sems((legs,)),
            sems((12,)), sems((12,)), sems((3 * CHUNKS,)), sems((sums,)),
        ],
        compiler_params=pltpu.CompilerParams(
            collective_id=2, has_side_effects=True, vmem_limit_bytes=63 * 2**20
        ),
        cost_estimate=pl.CostEstimate(flops=10**11, bytes_accessed=3 * 10**8, transcendentals=0),
        name="layer",
    )(tokens, expert_ids.T, gate_codes.T, *routed, *shared).T


def running(ones, width):
    groups = ones.reshape(ones.shape[0], -1, width).astype(F32)
    inside = jnp.einsum("rgt,tu->rgu", groups, jnp.triu(jnp.ones((width, width), F32)))
    count = groups.shape[1]
    earlier = jnp.triu(jnp.ones((count, count), F32), 1)
    before = jnp.einsum("rg,gh->rh", inside[:, :, -1], earlier, precision=lax.Precision.HIGHEST)
    return (inside + before[:, :, None]).reshape(ones.shape).astype(jnp.int32)


def shards(tokens, expert_ids, gate_codes, *factors):
    shared, routed = factors[:4], factors[4:]
    residents = routed[0].shape[0]
    sources = lax.axis_size("expert")
    tok_rows = tokens.shape[0]
    if sources == 8 and lax.axis_size("dp") == 4 and residents == 2:
        return layer_call(tokens, expert_ids, gate_codes, shared, routed)
    experts_all = residents * sources
    capacity = max(2, 6 * tok_rows // experts_all)
    tiles = -(-sources * capacity // (2 * T))
    depth = tiles * 2 * T
    window = min(depth, -(-(T - 1 + 2 * capacity) // T) * T)

    extra = jnp.concatenate([expert_ids, gate_codes], axis=1).T.astype(BF16)
    extra = jnp.pad(extra, ((0, 16 - extra.shape[0]), (0, 0)))
    x_t = jnp.concatenate([tokens.T, extra], axis=0)
    x_all = gather_tokens(x_t)
    ids_all = x_all[:, D : D + 2].astype(jnp.int32)
    codes = x_all[:, D + 2 : D + 4].astype(F32)
    gates_all = codes / jnp.sum(codes, axis=1, keepdims=True)
    mine = lax.axis_index("expert") * residents + jnp.arange(residents, dtype=jnp.int32)
    match = ids_all[None] == mine[:, None, None, None]
    picked = jnp.any(match, axis=2).reshape(residents, sources * tok_rows)
    gate = jnp.sum(jnp.where(match, gates_all[None], 0.0), axis=2).reshape(residents, sources * tok_rows)
    ones = picked.astype(jnp.int32)
    ranks = running(ones, tok_rows)
    counts = ranks[:, -1]
    starts = (ranks - ones).reshape(residents, sources // 2, 2 * T)[:, :, 0]
    starts = jnp.minimum(starts, depth - window) // T
    pos = jnp.where(picked, ranks - 1, -1)
    slots = jnp.arange(depth, dtype=jnp.int32)
    slot_gates = jnp.sum(
        jnp.where(pos[:, None, :] == slots[None, :, None], gate[:, None, :], 0.0), axis=2
    ).reshape(residents, tiles, 1, 2 * T)
    pos = pos.reshape(residents, sources // 2, 1, 2 * T)

    outs = routed_call(counts, pos, slot_gates, x_all, turned(routed), tiles)
    y = combine_call(starts, pos, outs, sources, depth, window)
    sums = scatter_sums(y)
    whole = tuple(lax.all_gather(w, "dp", axis=0, tiled=True)[None] for w in turned(shared))
    shared_t = shared_call(x_t, whole)
    total = shared_t.astype(F32) + sums.astype(F32)
    return total.astype(BF16).T


def solution(mesh):
    in_specs = (
        P(("expert", "dp"), None),
        P(("expert", "dp"), None),
        P(("expert", "dp"), None),
        P("dp", None, None),
        P("dp", None, None),
        P("dp", None, None),
        P("dp", None, None),
        P("expert", None, None, None),
        P("expert", None, None, None),
        P("expert", None, None, None),
        P("expert", None, None, None),
    )
    out_specs = P(("expert", "dp"), None)
    return jax.shard_map(shards, mesh=mesh, in_specs=in_specs, out_specs=out_specs, check_vma=False)
```

```python
import functools
import math

import jax
import jax.numpy as jnp
from jax import lax
from jax.experimental import pallas as pl
from jax.experimental.pallas import tpu as pltpu
from jax.sharding import PartitionSpec as P

D = 4096
NB = 64
DB = 64
HB = 256
T = 128
F32 = jnp.float32
BF16 = jnp.bfloat16


def tile_monarch(x_ref, lanes, w1_ref, w2_ref, w3_ref, w4_ref, z_refs, u_refs, store):
    def spread(refs, rows, value):
        for i in range(lanes):
            refs[i][rows, :] = value[:, i * T : (i + 1) * T]

    def strided(refs, start):
        parts = [refs[i][pl.ds(start, NB, stride=NB), :] for i in range(lanes)]
        return jnp.concatenate(parts, axis=1).astype(BF16)

    def up(a, carry):
        rows = pl.ds(pl.multiple_of(a * DB, DB), DB)
        x = x_ref[rows, : lanes * T]
        spread(z_refs, rows, jnp.dot(w1_ref[0, a], x, preferred_element_type=F32))
        return carry

    lax.fori_loop(0, NB, up, 0, unroll=8)

    def middle(j, carry):
        hidden = jnp.dot(w2_ref[0, j], strided(z_refs, j), preferred_element_type=F32)
        hidden = (0.5 * hidden) * (1.0 + lax.erf(hidden * (0.5**0.5)))
        u = jnp.dot(w3_ref[0, j], hidden.astype(BF16), preferred_element_type=F32)
        spread(u_refs, pl.ds(pl.multiple_of(j * NB, NB), NB), u)
        return carry

    lax.fori_loop(0, NB, middle, 0, unroll=4)

    def down(k, carry):
        rows = pl.ds(pl.multiple_of(k * DB, DB), DB)
        store(rows, jnp.dot(w4_ref[0, k], strided(u_refs, k), preferred_element_type=F32))
        return carry

    lax.fori_loop(0, NB, down, 0, unroll=8)


def shared_kernel(x_ref, w1_ref, w2_ref, w3_ref, w4_ref, o_ref, z_ref, u_ref):
    def store(rows, value):
        o_ref[rows, :] = value.astype(BF16)

    tile_monarch(x_ref, 1, w1_ref, w2_ref, w3_ref, w4_ref, (z_ref,), (u_ref,), store)


def routed_kernel(
    counts_ref, pos_ref, gate_ref, x_ref, w1_ref, w2_ref, w3_ref, w4_ref,
    o_ref, x_scr, z0_ref, z1_ref, u0_ref, u1_ref,
):
    expert, tile = pl.program_id(0), pl.program_id(1)
    left = counts_ref[expert] - tile * 2 * T
    sources = x_ref.shape[0]

    @pl.when(left <= T)
    def _():
        o_ref[...] = jnp.zeros_like(o_ref)

    def serve(lanes):
        width = lanes * T
        wanted = lax.broadcasted_iota(jnp.int32, (width, 2 * T), 0) + tile * 2 * T
        step = D // 8

        for part in range(8):
            rows = pl.ds(part * step, step)

            def pick(pair, total):
                both = jnp.concatenate([x_ref[2 * pair, rows, :], x_ref[2 * pair + 1, rows, :]], axis=1)
                onehot = (wanted == pos_ref[0, pair, :, :]).astype(F32).astype(BF16)
                return total + lax.dot_general(
                    both, onehot, (((1,), (1,)), ((), ())), preferred_element_type=F32
                )

            total = lax.fori_loop(0, sources // 2, pick, jnp.zeros((step, width), F32))
            x_scr[rows, :width] = total.astype(BF16)

        gate = gate_ref[0, 0][:, :width]

        def store(rows, value):
            o_ref[rows, :width] = (value * gate).astype(BF16)

        tile_monarch(
            x_scr, lanes, w1_ref, w2_ref, w3_ref, w4_ref, (z0_ref, z1_ref), (u0_ref, u1_ref), store
        )

    @pl.when(left > T)
    def _():
        serve(2)

    @pl.when(jnp.logical_and(left > 0, left <= T))
    def _():
        serve(1)


def weight_specs(index_map, buffers=2):
    shapes = ((NB, DB), (HB, NB), (NB, HB), (DB, NB))
    mode = pl.Buffered(buffers)
    return [pl.BlockSpec((1, NB) + shape, index_map, pipeline_mode=mode) for shape in shapes]


def turned(factors):
    return tuple(jnp.swapaxes(w, -1, -2) for w in factors)


def shared_call(x_t, factors):
    return pl.pallas_call(
        shared_kernel,
        out_shape=jax.ShapeDtypeStruct((D, T), BF16),
        grid=(1,),
        in_specs=[pl.BlockSpec((D, T), lambda i: (0, 0))] + weight_specs(lambda i: (0, 0, 0, 0)),
        out_specs=pl.BlockSpec((D, T), lambda i: (0, 0)),
        scratch_shapes=[pltpu.VMEM((D, T), F32), pltpu.VMEM((D, T), F32)],
        compiler_params=pltpu.CompilerParams(vmem_limit_bytes=56 * 2**20),
        cost_estimate=pl.CostEstimate(flops=10**10, bytes_accessed=10**7, transcendentals=0),
        name="shared_expert",
    )(x_t, *factors)


def routed_call(counts, pos, slot_gates, x_all, factors, tiles):
    residents = pos.shape[0]
    sources = x_all.shape[0]
    grid_spec = pltpu.PrefetchScalarGridSpec(
        num_scalar_prefetch=1,
        grid=(residents, tiles),
        in_specs=[
            pl.BlockSpec((1, sources // 2, 1, 2 * T), lambda e, i, c: (e, 0, 0, 0)),
            pl.BlockSpec((1, 1, 1, 2 * T), lambda e, i, c: (e, i, 0, 0)),
            pl.BlockSpec((sources, x_all.shape[1], T), lambda e, i, c: (0, 0, 0), pipeline_mode=pl.Buffered(1)),
        ]
        + weight_specs(lambda e, i, c: (e, 0, 0, 0), 2 if sources <= 8 else 1),
        out_specs=pl.BlockSpec((D, 2 * T), lambda e, i, c: (0, e * tiles + i)),
        scratch_shapes=[pltpu.VMEM((D, 2 * T), BF16)] + [pltpu.VMEM((D, T), F32)] * 4,
    )
    return pl.pallas_call(
        routed_kernel,
        out_shape=jax.ShapeDtypeStruct((D, residents * tiles * 2 * T), BF16),
        grid_spec=grid_spec,
        compiler_params=pltpu.CompilerParams(vmem_limit_bytes=62 * 2**20),
        cost_estimate=pl.CostEstimate(flops=4 * 10**10, bytes_accessed=2 * 10**7, transcendentals=0),
        name="routed_experts",
    )(counts, pos, slot_gates, x_all, *factors)


def combine_kernel(depth, window, starts_ref, pos_ref, o_ref, y_ref):
    residents = starts_ref.shape[0]
    pair = pl.program_id(0)
    wanted = lax.broadcasted_iota(jnp.int32, (window, 2 * T), 0)
    begins = [pl.multiple_of(starts_ref[e, pair] * T, T) for e in range(residents)]
    hots = [
        (wanted + begins[e] == pos_ref[e, 0, :, :]).astype(F32).astype(BF16) for e in range(residents)
    ]
    hot = jnp.concatenate(hots, axis=0)
    step = 512

    def part(i, carry):
        rows = pl.ds(pl.multiple_of(i * step, step), step)
        near = [
            o_ref[rows, pl.ds(pl.multiple_of(begins[e] + e * depth, T), window)] for e in range(residents)
        ]
        total = jnp.dot(jnp.concatenate(near, axis=1), hot, preferred_element_type=F32).astype(BF16)
        y_ref[0, rows, :] = total[:, :T]
        y_ref[1, rows, :] = total[:, T:]
        return carry

    lax.fori_loop(0, D // step, part, 0)


def combine_call(starts, pos, outs, sources, depth, window):
    residents = pos.shape[0]
    grid_spec = pltpu.PrefetchScalarGridSpec(
        num_scalar_prefetch=1,
        grid=(sources // 2,),
        in_specs=[
            pl.BlockSpec((residents, 1, 1, 2 * T), lambda s, c: (0, s, 0, 0)),
            pl.BlockSpec((D, residents * depth), lambda s, c: (0, 0), pipeline_mode=pl.Buffered(1)),
        ],
        out_specs=pl.BlockSpec((2, D, T), lambda s, c: (s, 0, 0)),
    )
    return pl.pallas_call(
        functools.partial(combine_kernel, depth, window),
        out_shape=jax.ShapeDtypeStruct((sources, D, T), BF16),
        grid_spec=grid_spec,
        compiler_params=pltpu.CompilerParams(vmem_limit_bytes=48 * 2**20),
        name="combine",
    )(starts, pos, outs)


def grid_of(count):
    side = math.isqrt(count // 2)
    return count // side, side


def greet(z, y, nz, ny):
    barrier = pltpu.get_barrier_semaphore()
    for other in range(1, ny):
        pl.semaphore_signal(barrier, inc=1, device_id={"expert": z * ny + lax.rem(y + other, ny)})

    @pl.when(z > 0)
    def _():
        pl.semaphore_signal(barrier, inc=1, device_id={"expert": (z - 1) * ny + y})

    @pl.when(z < nz - 1)
    def _():
        pl.semaphore_signal(barrier, inc=1, device_id={"expert": (z + 1) * ny + y})

    peers = ny - 1 + jnp.where(z > 0, 1, 0) + jnp.where(z < nz - 1, 1, 0)
    pl.semaphore_wait(barrier, peers)


def gather_kernel(nz, x_ref, out_ref, own_sem, up_sem, down_sem, side_sem, recv_sem):
    ny = 2
    me = lax.axis_index("expert")
    z, y = me // ny, lax.rem(me, ny)
    beside = z * ny + (1 - y)

    def send(block, src, sem, target):
        return pltpu.make_async_remote_copy(
            src_ref=src, dst_ref=out_ref.at[block], send_sem=sem.at[block],
            recv_sem=recv_sem.at[block], device_id={"expert": target},
        )

    def arrived(block):
        send(block, out_ref.at[block], side_sem, beside).wait_recv()

    greet(z, y, nz, ny)
    own = pltpu.make_async_copy(x_ref, out_ref.at[me], own_sem)
    own.start()

    @pl.when(z < nz - 1)
    def _():
        send(me, x_ref, up_sem, me + ny).start()

    @pl.when(z > 0)
    def _():
        send(me, x_ref, down_sem, me - ny).start()

    send(me, x_ref, side_sem, beside).start()

    for k in range(1, nz):
        block = me - k * ny

        @pl.when(z >= k)
        def _():
            arrived(block)

            @pl.when(z < nz - 1)
            def _():
                send(block, out_ref.at[block], up_sem, me + ny).start()

            send(block, out_ref.at[block], side_sem, beside).start()

        later = me + k * ny

        @pl.when(z + k < nz)
        def _():
            arrived(later)

            @pl.when(z > 0)
            def _():
                send(later, out_ref.at[later], down_sem, me - ny).start()

            send(later, out_ref.at[later], side_sem, beside).start()

    for other in range(nz):
        arrived(other * ny + (1 - y))
    own.wait()
    for other in range(nz):
        block = other * ny + y
        send(block, out_ref.at[block], side_sem, beside).wait_send()

        @pl.when(jnp.logical_and(other <= z, z < nz - 1))
        def _():
            send(block, out_ref.at[block], up_sem, me + ny).wait_send()

        @pl.when(jnp.logical_and(other >= z, z > 0))
        def _():
            send(block, out_ref.at[block], down_sem, me - ny).wait_send()


def gather_tokens(x_t):
    count = lax.axis_size("expert")
    nz, ny = grid_of(count)
    if ny != 2:
        return lax.all_gather(x_t, "expert", axis=0, tiled=False)
    sems = pltpu.SemaphoreType.DMA((count,))
    return pl.pallas_call(
        functools.partial(gather_kernel, nz),
        out_shape=jax.ShapeDtypeStruct((count,) + x_t.shape, x_t.dtype),
        in_specs=[pl.BlockSpec(memory_space=pl.ANY)],
        out_specs=pl.BlockSpec(memory_space=pl.ANY),
        scratch_shapes=[pltpu.SemaphoreType.DMA, sems, sems, sems, sems],
        compiler_params=pltpu.CompilerParams(collective_id=0, has_side_effects=True),
        cost_estimate=pl.CostEstimate(flops=10**11, bytes_accessed=3 * 10**8, transcendentals=0),
        name="gather_tokens",
    )(x_t)


def scatter_kernel(
    nz, y_hbm, out_ref, held, beside_in, below_in, above_in,
    load_sem, side_sem, side_recv, up_sem, up_recv, down_sem, down_recv,
):
    ny = 2
    me = lax.axis_index("expert")
    z, y = me // ny, lax.rem(me, ny)
    beside = z * ny + (1 - y)

    def load(target):
        return pltpu.make_async_copy(y_hbm.at[target * ny + y], held.at[target], load_sem.at[target])

    def side(target):
        return pltpu.make_async_remote_copy(
            src_ref=y_hbm.at[target * ny + (1 - y)], dst_ref=beside_in.at[target],
            send_sem=side_sem.at[target], recv_sem=side_recv.at[target],
            device_id={"expert": beside},
        )

    def up(target):
        return pltpu.make_async_remote_copy(
            src_ref=held.at[target], dst_ref=below_in.at[target], send_sem=up_sem.at[target],
            recv_sem=up_recv.at[target], device_id={"expert": me + ny},
        )

    def down(target):
        return pltpu.make_async_remote_copy(
            src_ref=held.at[target], dst_ref=above_in.at[target], send_sem=down_sem.at[target],
            recv_sem=down_recv.at[target], device_id={"expert": me - ny},
        )

    def add(target, ref):
        step = 512

        def body(i, carry):
            rows = pl.ds(pl.multiple_of(i * step, step), step)
            total = held[target, rows, :].astype(F32) + ref[target, rows, :].astype(F32)
            held[target, rows, :] = total.astype(BF16)
            return carry

        lax.fori_loop(0, D // step, body, 0)

    greet(z, y, nz, ny)
    for k in range(nz - 1, -1, -1):
        @pl.when(z + k < nz)
        def _():
            side(z + k).start()

        if k > 0:
            @pl.when(z - k >= 0)
            def _():
                side(z - k).start()

    for target in range(nz):
        load(target).start()
    for target in range(nz):
        load(target).wait()
    for k in range(nz - 1, 0, -1):
        target = z + k

        @pl.when(z + k < nz)
        def _():
            side(target).wait_recv()
            add(target, beside_in)

            @pl.when(z > 0)
            def _():
                up(target).wait_recv()
                add(target, below_in)

            up(target).start()

        lower = z - k

        @pl.when(z - k >= 0)
        def _():
            side(lower).wait_recv()
            add(lower, beside_in)

            @pl.when(z < nz - 1)
            def _():
                down(lower).wait_recv()
                add(lower, above_in)

            down(lower).start()

    side(z).wait_recv()
    add(z, beside_in)

    @pl.when(z > 0)
    def _():
        up(z).wait_recv()
        add(z, below_in)

    @pl.when(z < nz - 1)
    def _():
        down(z).wait_recv()
        add(z, above_in)

    out_ref[...] = held[z]
    for target in range(nz):
        side(target).wait_send()

        @pl.when(target > z)
        def _():
            up(target).wait_send()

        @pl.when(target < z)
        def _():
            down(target).wait_send()


def scatter_sums(sums):
    count = lax.axis_size("expert")
    nz, ny = grid_of(count)
    if ny != 2:
        return lax.psum_scatter(sums, "expert", scatter_dimension=0, tiled=False)
    block = pltpu.VMEM((nz,) + sums.shape[1:], sums.dtype)
    sems = pltpu.SemaphoreType.DMA((nz,))
    return pl.pallas_call(
        functools.partial(scatter_kernel, nz),
        out_shape=jax.ShapeDtypeStruct(sums.shape[1:], sums.dtype),
        in_specs=[pl.BlockSpec(memory_space=pl.ANY)],
        out_specs=pl.BlockSpec(memory_space=pltpu.VMEM),
        scratch_shapes=[block] * 4 + [sems] * 7,
        compiler_params=pltpu.CompilerParams(
            collective_id=1, has_side_effects=True, vmem_limit_bytes=40 * 2**20
        ),
        cost_estimate=pl.CostEstimate(flops=10**11, bytes_accessed=3 * 10**8, transcendentals=0),
        name="scatter_sums",
    )(sums)


ROWS = D + 16
CAP = 48
CHUNK = 256
CHUNKS = D // CHUNK
LAG = 5
SPANS = ((0, 1024), (1024, 1024), (2048, 1280), (3328, ROWS - 3328))
EIGHTS = (0, 8, 16, 24)
KEPT = NB // 2
LEGS = ((1, 0, 8, 0), (0, 0, 16, 0), (1, 8, 8, 0), (1, 16, 8, 0), (1, 24, 4, 0), (1, 28, 4, 0)) + tuple(
    (3, start, 8, 0) for start in (0, 8)
) + tuple(
    (2, start, 8, k) for k in (0, KEPT) for start in EIGHTS
)


def dot(a, b):
    return jnp.dot(a, b, preferred_element_type=F32)


def dot_turned(w, x):
    return lax.dot_general(w, x, (((0,), (0,)), ((), ())), preferred_element_type=F32)


def gelu(hidden):
    return ((0.5 * hidden) * (1.0 + lax.erf(hidden * (0.5**0.5)))).astype(BF16)


def aligned(start, step):
    return pl.ds(pl.multiple_of(start, step), step)


def apart(upper, lower):
    top, bottom = [], []
    for a, b in zip(upper, lower):
        top += [a, jnp.zeros_like(a)]
        bottom += [jnp.zeros_like(b), b]
    return jnp.concatenate([jnp.concatenate(top, axis=1), jnp.concatenate(bottom, axis=1)], axis=0)


def strided(ref, tiles, start):
    return [ref[i, pl.ds(start, NB, stride=NB), :].astype(BF16) for i in range(tiles)]


def up(tiles, load, w1, z_ref):
    def some(i, carry):
        for q in range(8):
            p = i * 8 + q
            parts = load(aligned(p * 2 * DB, 2 * DB))
            value = dot(w1[p], apart([x[:DB] for x in parts], [x[DB:] for x in parts]))
            for t in range(tiles):
                for side in range(2):
                    at = 2 * t + side
                    z_ref[t, aligned((2 * p + side) * DB, DB), :] = value[:, at * T : (at + 1) * T]
        return carry

    lax.fori_loop(0, NB // 16, some, 0)


def middle(tiles, w2, w3, z_ref, u_ref, first, count):
    batch = min(count, 8 if tiles == 1 else 4)

    def some(i, carry):
        blocks = [first + i * batch + q for q in range(batch)]
        hidden = []
        for j in blocks:
            parts = strided(z_ref, tiles, j)
            rows = parts[0] if tiles == 1 else jnp.concatenate(parts, axis=1)
            hidden.append(gelu(dot_turned(w2[j], rows)))
        for j, h in zip(blocks, hidden):
            value = dot(w3[j], h)
            for t in range(tiles):
                u_ref[t, aligned(j * NB, NB), :] = value[:, t * T : (t + 1) * T]
        return carry

    lax.fori_loop(0, count // batch, some, 0)


def expand(w2, z_ref, h_ref, first, count):
    def some(i, carry):
        for q in range(8):
            j = first + i * 8 + q
            h_ref[j] = gelu(dot_turned(w2[j], jnp.concatenate(strided(z_ref, 2, j), axis=1)))
        return carry

    lax.fori_loop(0, count // 8, some, 0)


def contract(w3, h_ref, u_ref, first, count, start):
    def some(i, carry):
        for q in range(8):
            j = first + i * 8 + q
            value = dot(w3[j, pl.ds(start, KEPT), :], h_ref[j])
            for t in range(2):
                u_ref[t, aligned(j * NB + start, KEPT), :] = value[:, t * T : (t + 1) * T]
        return carry

    lax.fori_loop(0, count // 8, some, 0)


def down(tiles, w4, u_ref, store, first, count):
    batch = min(count, 8)

    def some(i, carry):
        for q in range(batch):
            p = first + i * batch + q
            value = dot(w4[p], apart(strided(u_ref, tiles, 2 * p), strided(u_ref, tiles, 2 * p + 1)))
            for side in range(2):
                parts = [value[:, (2 * t + side) * T : (2 * t + side + 1) * T] for t in range(tiles)]
                store(aligned((2 * p + side) * DB, DB), parts)
        return carry

    lax.fori_loop(0, count // batch, some, 0)


def pack_pairs(src, dst, first, count):
    def some(i, carry):
        for q in range(4):
            p = i * 4 + q
            both = jnp.concatenate([src[2 * p], src[2 * p + 1]], axis=0)
            dst[first + p] = both.T
        return carry

    lax.fori_loop(0, count // 4, some, 0)


def layer_kernel(
    tok, ids, codes, r1, r2, r3, r4, s1, s2, s3, s4, out_ref,
    x_all, a1, a2, a3, a4, b1, b2, b3, b4, c1, c2, c3, c4,
    slots, z_ref, u_ref, hot, hot_t, share, shared_out, core_in, y_in, z_in,
    tok_in, r_in, s1_in, s4_in, h_ref,
    local_sem, x_send, x_recv, b_send, b_recv, c_send, c_recv, sum_send, sum_recv,
):
    e, d = lax.axis_index("expert"), lax.axis_index("dp")
    z, y, x, c = e // 2, lax.rem(e, 2), d // 2, lax.rem(d, 2)
    near_z = e + 2 - 4 * lax.rem(z, 2)
    on_far = {"expert": lax.rem(e + 4, 8), "dp": d}
    on_near = {"expert": near_z, "dp": d}
    on_y = {"expert": e + 1 - 2 * y, "dp": d}
    on_core = {"expert": e, "dp": d + 1 - 2 * c}
    on_x = {"expert": e, "dp": lax.rem(d + 2, 4)}
    own_a, own_b, own_s = (a1, a2, a3, a4), (b1, b2, b3, b4), (c1, c2, c3, c4)

    def remote(src, dst, send, recv, target):
        return pltpu.make_async_remote_copy(
            src_ref=src, dst_ref=dst, send_sem=send, recv_sem=recv, device_id=target
        )

    def x_copy(number, source, slot, rows, target):
        return remote(
            x_all.at[source, rows], x_all.at[slot, rows], x_send.at[number], x_recv.at[number], target
        )

    whole = pl.ds(0, ROWS)
    spans = [pl.ds(*s) for s in SPANS]
    x_core = x_copy(0, 0, 1, whole, on_core)
    x_y = x_copy(1, 0, 2, whole, on_y)
    x_far = [x_copy(2 + i, 0, 4, rows, on_far) for i, rows in enumerate(spans)]
    x_y_core = x_copy(6, 2, 3, whole, on_core)
    x_far_core = [x_copy(7 + i, 4, 5, rows, on_core) for i, rows in enumerate(spans)]
    x_far_y = [x_copy(11 + i, 4, 6, rows, on_y) for i, rows in enumerate(spans)]
    x_last = [x_copy(15 + i, 6, 7, rows, on_core) for i, rows in enumerate(spans)]

    def leg(number, half, first):
        w, start, size, k = LEGS[number]
        rows = pl.ds(half * (16 if w in (0, 3) else 32) + start, size)
        where = (rows, pl.ds(k, KEPT)) if w == 2 else rows
        src = (a1, r2.at[c], r3.at[c], a4)[w] if first else own_b[w]
        at = number if first else number + len(LEGS)
        return remote(
            src.at[where], own_b[w].at[where], b_send.at[at], b_recv.at[at], on_near if first else on_x
        )

    b_near = [leg(n, x, True) for n in range(len(LEGS))]
    b_x = [leg(n, x, False) for n in range(len(LEGS))]
    b_there = [leg(n, 1 - x, False) for n in range(len(LEGS))]

    def quarter(w, at, number, target, src=None):
        size = 8 if w in (0, 3) else 16
        rows = pl.ds(at * size, size)
        src = own_s[w].at[rows] if src is None else src
        return remote(src, own_s[w].at[rows], c_send.at[number], c_recv.at[number], target)

    sources = (None, s2, s3, None)
    c_core = [quarter(w, d, w, on_core, sources[w]) for w in range(4)]
    c_x = [quarter(w, d, 4 + w, on_x, sources[w]) for w in range(4)]
    c_fwd = [quarter(w, lax.rem(d + 2, 4), 8 + w, on_core) for w in range(4)]

    def local(number, src, dst):
        return pltpu.make_async_copy(src, dst, local_sem.at[number])

    here_s = pl.ds(d * 16, 16)
    tok_load = local(0, tok, tok_in)
    r1_load = local(1, r1.at[c], r_in)
    r4_load = local(2, r4.at[c], r_in)
    r_loads = [local(3, r2.at[c], a2), local(4, r3.at[c], a3)]
    s_packs = [local(5, s1, s1_in), local(6, s4, s4_in)]
    s_loads = [local(7, s2, c2.at[here_s]), local(8, s3, c3.at[here_s])]
    for copy in [tok_load, r1_load] + s_packs:
        copy.start()

    barrier = pltpu.get_barrier_semaphore()
    for target in (on_far, on_near, on_y, on_core, on_x):
        pl.semaphore_signal(barrier, inc=1, device_id=target)
    pl.semaphore_wait(barrier, 5)

    b_near[0].start()
    for copy in s_packs:
        copy.wait()
    pack_pairs(s1_in, c1, d * 8, 8)
    for w in range(3):
        c_x[w].start()
    numbers = [ref[...].astype(F32) for ref in (ids, codes)]
    extra = jnp.concatenate(numbers + [jnp.zeros((ROWS - D - 4, T), F32)], axis=0)
    x_all[0, D:ROWS, :] = extra.astype(BF16)
    tok_load.wait()
    for i in range(4):
        for at in range(SPANS[i][0], min(D, sum(SPANS[i])), 256):
            x_all[0, at : at + 256, :] = tok_in[:, at : at + 256].T
        x_far[i].start()
    x_y.start()
    x_core.start()
    r1_load.wait()
    pack_pairs(r_in, a1, 0, 32)
    r4_load.start()
    for n in (1, 2, 3, 4, 5):
        b_near[n].start()
    pack_pairs(s4_in, c4, d * 8, 8)
    c_x[3].start()
    for copy in c_core + r_loads + s_loads:
        copy.start()
    r4_load.wait()
    pack_pairs(r_in, a4, 0, 32)
    for copy in b_near[6:]:
        copy.start()

    ids_a = (2 * e + c).astype(F32)
    ids_b = (2 * near_z + c).astype(F32)

    def prepare(q):
        extra = jnp.concatenate(
            [x_all[2 * q, D:ROWS, :].astype(F32), x_all[2 * q + 1, D:ROWS, :].astype(F32)], axis=1
        )
        id0, id1, code0, code1 = (extra[i : i + 1] for i in range(4))
        lane = lax.broadcasted_iota(jnp.int32, (1, 2 * T), 1)
        before = lax.broadcasted_iota(jnp.int32, (2 * T, 2 * T), 0)
        after = lax.broadcasted_iota(jnp.int32, (2 * T, 2 * T), 1)
        tri = jnp.logical_and(before < after, (before < T) == (after < T))
        tri = tri.astype(F32).astype(BF16)
        row8 = lax.broadcasted_iota(jnp.int32, (8, 2 * T), 0)
        picks = [jnp.logical_or(id0 == n, id1 == n) for n in (ids_a, ids_b)]
        names = [jnp.where(p, 1.0, 0.0) for p in picks]
        codes = [jnp.where(id0 == n, code0, code1) for n in (ids_a, ids_b)]
        stacked = jnp.where(row8 == 0, names[0], jnp.where(row8 == 1, names[1], 0.0))
        ranks = dot(stacked.astype(BF16), tri)
        base = jnp.where(lane < T, 2 * q * CAP, (2 * q + 1) * CAP).astype(F32)
        places = [
            jnp.where(picks[n], ranks[n : n + 1] + base, -1000.0).astype(jnp.int32) for n in range(2)
        ]
        for tile, half in ((q, 0), (q - 1, 1)):
            if not 0 <= tile < 3:
                continue
            wanted = lax.broadcasted_iota(jnp.int32, (T, 2 * T), 0) + tile * T
            for n in range(2):
                own = (wanted == places[n]).astype(F32).astype(BF16)
                hot[q, half * 2 * T + n * T : half * 2 * T + (n + 1) * T, :] = own
                hot_t[tile, half * 2 * T : (half + 1) * 2 * T, n * T : (n + 1) * T] = own.T
                values = jnp.where(
                    row8 == 0, codes[n], jnp.where(row8 == 1, code0, jnp.where(row8 == 2, code1, 0.0))
                )
                got = lax.dot_general(
                    values.astype(BF16), own, (((1,), (1,)), ((), ())), preferred_element_type=F32
                )
                if half == 0:
                    share[n, tile] = got
                else:
                    share[n, tile] += got

    def pick(tile):
        def some(i, carry):
            rows = aligned(i * 512, 512)
            blocks = [x_all[2 * tile + n, rows, :] for n in range(4)]
            total = dot(jnp.concatenate(blocks, axis=1), hot_t[tile])
            total = total.astype(BF16)
            slots[0, tile, rows, :] = total[:, :T]
            slots[1, tile, rows, :] = total[:, T:]
            return carry

        lax.fori_loop(0, D // 512, some, 0)

    def slot_loader(n, first, count):
        return lambda rows: [slots[n, first + i, rows, :] for i in range(count)]

    def slot_storer(n, first, count):
        gates = []
        for i in range(count):
            got = share[n, first + i]
            under = got[1:2] + got[2:3]
            gates.append(jnp.where(under > 0.0, got[0:1] / jnp.maximum(under, 1.0), 0.0))
        gates = [jnp.broadcast_to(g, (DB, T)) for g in gates]

        def store(rows, parts):
            for i in range(count):
                slots[n, first + i, rows, :] = (parts[i] * gates[i]).astype(BF16)

        return store

    def forward(i):
        x_far[i].wait_recv()
        x_far_y[i].start()
        x_far_core[i].start()

    def relay(*numbers):
        for n in numbers:
            b_near[n].wait_recv()
            b_x[n].start()

    def last_hop(i):
        x_far_y[i].wait_recv()
        x_last[i].start()

    here, there = x * 32, 32 - x * 32
    z_s, u_s = z_ref.at[pl.ds(1, 1)], u_ref.at[pl.ds(1, 1)]
    z_one, u_one = z_ref.at[pl.ds(0, 1)], u_ref.at[pl.ds(0, 1)]
    x_core.wait_recv()
    prepare(0)
    for copy in s_loads:
        copy.wait()
    for copy in c_core:
        copy.wait_recv()
    c_x[0].wait_recv()
    c_fwd[0].start()
    c_fwd[0].wait_recv()
    up(1, lambda rows: [x_all[0, rows, :]], c1, z_s)
    middle(1, c2, c3, z_s, u_s, here, NB // 2)
    relay(0)
    x_y.wait_recv()
    x_y_core.start()
    x_y_core.wait_recv()
    prepare(1)
    pick(0)
    forward(0)
    for copy in r_loads:
        copy.wait()
    up(1, slot_loader(0, 0, 1), a1, z_ref)
    for copy in c_x[1:]:
        copy.wait_recv()
    for copy in c_fwd[1:]:
        copy.start()
    middle(1, a2, a3, z_ref, u_ref, 0, NB)
    relay(1)
    forward(1)
    down(1, a4, u_ref, slot_storer(0, 0, 1), 0, NB // 2)
    last_hop(0)
    for copy in c_fwd[1:]:
        copy.wait_recv()

    def keep_shared(rows, parts):
        shared_out[rows, :] = parts[0].astype(BF16)

    relay(2)
    middle(1, c2, c3, z_s, u_s, there, NB // 2)
    down(1, c4, u_s, keep_shared, 0, NB // 2)
    forward(2)
    last_hop(1)
    b_there[1].wait_recv()
    up(1, slot_loader(1, 0, 1), b1, z_one)
    forward(3)
    relay(3)
    for copy in x_far_core:
        copy.wait_recv()
    prepare(2)
    pick(1)
    up(1, slot_loader(0, 1, 1), a1, z_s)
    relay(4)
    middle(1, a2, a3, z_s, u_s, 0, NB // 2)
    relay(5)
    last_hop(2)
    middle(1, a2, a3, z_s, u_s, NB // 2, NB // 2)
    relay(6)
    last_hop(3)
    down(1, a4, u_s, slot_storer(0, 1, 1), 0, NB // 2)
    relay(7)
    for copy in x_last:
        copy.wait_recv()
    prepare(3)
    pick(2)
    up(1, slot_loader(0, 2, 1), a1, z_s)
    relay(8)
    middle(1, a2, a3, z_s, u_one, 0, NB // 2)
    relay(9)
    middle(1, a2, a3, z_s, u_one, NB // 2, NB // 2)
    relay(10)
    down(1, a4, u_one, slot_storer(0, 2, 1), 0, NB // 4)
    z_two, u_two = z_ref.at[pl.ds(1, 2)], u_ref.at[pl.ds(1, 2)]
    up(2, slot_loader(1, 1, 2), b1, z_two)
    relay(11)
    expand(b2, z_two, h_ref, here, 32)
    for n in (0, 2, 3, 4, 5):
        b_there[n].wait_recv()
    expand(b2, z_two, h_ref, there, 16)
    relay(12)
    expand(b2, z_two, h_ref, there + 16, 16)
    contract(b3, h_ref, u_two, here, 32, 0)
    relay(13)
    b_there[8].wait_recv()
    b_there[9].wait_recv()
    contract(b3, h_ref, u_two, there, 16, 0)
    b_there[10].wait_recv()
    b_there[11].wait_recv()
    contract(b3, h_ref, u_two, there + 16, 16, 0)
    b_there[6].wait_recv()
    b_there[7].wait_recv()

    for copy in [x_core, x_y, x_y_core] + x_far + x_far_core + x_far_y + x_last:
        copy.wait_send()

    for copy in c_core + c_x + c_fwd:
        copy.wait_send()

    def sum_copy(send, at, src, dst, i, size, target):
        rows = aligned(i * size, size)
        return remote(src.at[rows], dst.at[rows], send, sum_recv.at[at], target)

    def to_core(q, i):
        if q < 2:
            send = c_send.at[4 * q + i]
        else:
            send = x_send.at[i] if q == 2 else sum_send.at[i]
        at = i + (12 + CHUNKS * (q - 2) if q > 1 else 4 * q)
        size = CHUNK if q > 1 else 1024
        return sum_copy(send, at, x_all.at[2 * q + 1], core_in.at[q], i, size, on_core)

    def to_y(q, i):
        send, at = (sum_send.at[CHUNKS + i], 12 + 2 * CHUNKS + i) if q > 1 else (c_send.at[8 + i], 8 + i)
        size = CHUNK if q > 1 else 1024
        return sum_copy(send, at, x_all.at[2 * q], y_in.at[q // 2], i, size, on_y)

    def to_far(i):
        at = 12 + 3 * CHUNKS + i
        return sum_copy(sum_send.at[2 * CHUNKS + i], at, x_all.at[4], z_in, i, CHUNK, on_far)

    def combine(q, i):
        where = [(tile, half) for tile, half in ((q, 0), (q - 1, 1)) if 0 <= tile < 3]
        first, last = where[0][1] * 2 * T, (where[-1][1] + 1) * 2 * T
        size = CHUNK if q > 1 else 1024
        for j in range(size // 256):
            rows = aligned(i * size + j * 256, 256)
            both = jnp.concatenate([slots[n, tile, rows, :] for tile, _ in where for n in range(2)], axis=1)
            total = dot(both, hot[q, first:last, :]).astype(BF16)
            x_all[2 * q, rows, :] = total[:, :T]
            x_all[2 * q + 1, rows, :] = total[:, T:]
        to_core(q, i).start()

    def summed(q, refs, rows):
        total = x_all[2 * q, rows, :].astype(F32)
        for ref in refs:
            total += ref[rows, :].astype(F32)
        return total

    def add(q, refs, i):
        size = CHUNK if q > 1 else 1024
        for j in range(size // 256):
            rows = aligned(i * size + j * 256, 256)
            x_all[2 * q, rows, :] = summed(q, refs, rows).astype(BF16)

    def over_y(q, i):
        to_core(q, i).wait_recv()
        add(q, [core_in.at[q]], i)
        to_y(q, i).start()

    def over_z(i):
        to_core(2, i).wait_recv()
        to_y(3, i).wait_recv()
        add(2, [core_in.at[2], y_in.at[1]], i)
        to_far(i).start()

    store_b = slot_storer(1, 1, 2)

    def begin(i, ahead, lag):
        down(2, b4, u_two, store_b, CHUNK // 128 * i, CHUNK // 128)
        combine(3, i)
        if ahead:
            over_y(3, i - 1)
        combine(2, i)
        if lag:
            over_z(i - LAG)

    def loop(first, last, body):
        lax.fori_loop(first, last, lambda i, carry: (body(i), carry)[1], 0)

    relay(14)
    begin(0, False, False)
    loop(1, 3, lambda i: begin(i, True, False))
    relay(15)
    loop(3, LAG, lambda i: begin(i, True, False))
    loop(LAG, CHUNKS // 2, lambda i: begin(i, True, True))
    over_y(3, CHUNKS // 2 - 1)
    down(1, a4, u_one, slot_storer(0, 2, 1), NB // 4, NB // 4)
    contract(b3, h_ref, u_two, here, 32, KEPT)
    for n in (12, 13, 14, 15):
        b_there[n].wait_recv()
    contract(b3, h_ref, u_two, there, 32, KEPT)
    begin(CHUNKS // 2, False, True)
    loop(CHUNKS // 2 + 1, CHUNKS, lambda i: begin(i, True, True))
    over_y(3, CHUNKS - 1)
    middle(1, b2, b3, z_one, u_one, 0, NB)
    store_one = slot_storer(1, 0, 1)
    for i in range(4):
        down(1, b4, u_one, store_one, 8 * i, 8)
        combine(1, i)
        if i > 0:
            over_y(1, i - 1)
    over_y(1, 3)
    loop(CHUNKS - LAG, CHUNKS, over_z)
    loop(0, 4, lambda i: combine(0, i))
    for i in range(4):
        to_core(0, i).wait_recv()
        to_y(1, i).wait_recv()

    def to_out(i):
        rows = aligned(i * CHUNK, CHUNK)
        return pltpu.make_async_copy(shared_out.at[rows], out_ref.at[rows], x_recv.at[i])

    def finish(i):
        to_far(i).wait_recv()
        for j in range(CHUNK // 256):
            rows = aligned(i * CHUNK + j * 256, 256)
            total = summed(0, [core_in.at[0], y_in.at[0], shared_out, z_in], rows)
            shared_out[rows, :] = total.astype(BF16)
        to_out(i).start()

    loop(0, CHUNKS, finish)

    def drain(i):
        to_core(2, i).wait_send()
        to_core(3, i).wait_send()
        to_y(3, i).wait_send()
        to_far(i).wait_send()
        to_out(i).wait()

    for copy in b_near + b_x:
        copy.wait_send()
    for i in range(4):
        to_core(0, i).wait_send()
        to_core(1, i).wait_send()
        to_y(1, i).wait_send()
    loop(0, CHUNKS, drain)


def layer_call(tokens, expert_ids, gate_codes, shared, routed):
    hbm = pl.BlockSpec(memory_space=pl.ANY)
    vmem = pl.BlockSpec(memory_space=pltpu.VMEM)
    weights = [
        pltpu.VMEM((NB // 2, NB, 2 * DB), BF16), pltpu.VMEM((NB, NB, HB), BF16),
        pltpu.VMEM((NB, NB, HB), BF16), pltpu.VMEM((NB // 2, DB, 2 * NB), BF16),
    ]
    sems = pltpu.SemaphoreType.DMA
    block = pltpu.VMEM((D, T), BF16)
    legs, sums = 2 * len(LEGS), 12 + 4 * CHUNKS
    routed = (routed[0], routed[1], jnp.swapaxes(routed[2], -1, -2), routed[3])
    shared = (shared[0], shared[1], jnp.swapaxes(shared[2], -1, -2), shared[3])
    return pl.pallas_call(
        layer_kernel,
        out_shape=jax.ShapeDtypeStruct((D, T), BF16),
        in_specs=[hbm, vmem, vmem] + [hbm] * 8,
        out_specs=hbm,
        scratch_shapes=[pltpu.VMEM((8, ROWS, T), BF16)]
        + weights * 3
        + [
            pltpu.VMEM((2, 3, D, T), BF16),
            pltpu.VMEM((3, D, T), F32),
            pltpu.VMEM((3, D, T), F32),
            pltpu.VMEM((4, 4 * T, 2 * T), BF16),
            pltpu.VMEM((3, 4 * T, 2 * T), BF16),
            pltpu.VMEM((2, 3, 8, T), F32),
            block,
            pltpu.VMEM((4, D, T), BF16),
            pltpu.VMEM((2, D, T), BF16),
            block,
            pltpu.VMEM((T, D), BF16),
            pltpu.VMEM((NB, DB, NB), BF16),
            pltpu.VMEM((NB // 4, DB, NB), BF16),
            pltpu.VMEM((NB // 4, NB, DB), BF16),
            pltpu.VMEM((NB, HB, 2 * T), BF16),
            sems((9,)), sems((19,)), sems((19,)), sems((legs,)), sems((legs,)),
            sems((12,)), sems((12,)), sems((3 * CHUNKS,)), sems((sums,)),
        ],
        compiler_params=pltpu.CompilerParams(
            collective_id=2, has_side_effects=True, vmem_limit_bytes=63 * 2**20
        ),
        cost_estimate=pl.CostEstimate(flops=10**11, bytes_accessed=3 * 10**8, transcendentals=0),
        name="layer",
    )(tokens, expert_ids.T, gate_codes.T, *routed, *shared).T


def running(ones, width):
    groups = ones.reshape(ones.shape[0], -1, width).astype(F32)
    inside = jnp.einsum("rgt,tu->rgu", groups, jnp.triu(jnp.ones((width, width), F32)))
    count = groups.shape[1]
    earlier = jnp.triu(jnp.ones((count, count), F32), 1)
    before = jnp.einsum("rg,gh->rh", inside[:, :, -1], earlier, precision=lax.Precision.HIGHEST)
    return (inside + before[:, :, None]).reshape(ones.shape).astype(jnp.int32)


def shards(tokens, expert_ids, gate_codes, *factors):
    shared, routed = factors[:4], factors[4:]
    residents = routed[0].shape[0]
    sources = lax.axis_size("expert")
    tok_rows = tokens.shape[0]
    if sources == 8 and lax.axis_size("dp") == 4 and residents == 2:
        return layer_call(tokens, expert_ids, gate_codes, shared, routed)
    experts_all = residents * sources
    capacity = max(2, 6 * tok_rows // experts_all)
    tiles = -(-sources * capacity // (2 * T))
    depth = tiles * 2 * T
    window = min(depth, -(-(T - 1 + 2 * capacity) // T) * T)

    extra = jnp.concatenate([expert_ids, gate_codes], axis=1).T.astype(BF16)
    extra = jnp.pad(extra, ((0, 16 - extra.shape[0]), (0, 0)))
    x_t = jnp.concatenate([tokens.T, extra], axis=0)
    x_all = gather_tokens(x_t)
    ids_all = x_all[:, D : D + 2].astype(jnp.int32)
    codes = x_all[:, D + 2 : D + 4].astype(F32)
    gates_all = codes / jnp.sum(codes, axis=1, keepdims=True)
    mine = lax.axis_index("expert") * residents + jnp.arange(residents, dtype=jnp.int32)
    match = ids_all[None] == mine[:, None, None, None]
    picked = jnp.any(match, axis=2).reshape(residents, sources * tok_rows)
    gate = jnp.sum(jnp.where(match, gates_all[None], 0.0), axis=2).reshape(residents, sources * tok_rows)
    ones = picked.astype(jnp.int32)
    ranks = running(ones, tok_rows)
    counts = ranks[:, -1]
    starts = (ranks - ones).reshape(residents, sources // 2, 2 * T)[:, :, 0]
    starts = jnp.minimum(starts, depth - window) // T
    pos = jnp.where(picked, ranks - 1, -1)
    slots = jnp.arange(depth, dtype=jnp.int32)
    slot_gates = jnp.sum(
        jnp.where(pos[:, None, :] == slots[None, :, None], gate[:, None, :], 0.0), axis=2
    ).reshape(residents, tiles, 1, 2 * T)
    pos = pos.reshape(residents, sources // 2, 1, 2 * T)

    outs = routed_call(counts, pos, slot_gates, x_all, turned(routed), tiles)
    y = combine_call(starts, pos, outs, sources, depth, window)
    sums = scatter_sums(y)
    whole = tuple(lax.all_gather(w, "dp", axis=0, tiled=True)[None] for w in turned(shared))
    shared_t = shared_call(x_t, whole)
    total = shared_t.astype(F32) + sums.astype(F32)
    return total.astype(BF16).T


def solution(mesh):
    in_specs = (
        P(("expert", "dp"), None),
        P(("expert", "dp"), None),
        P(("expert", "dp"), None),
        P("dp", None, None),
        P("dp", None, None),
        P("dp", None, None),
        P("dp", None, None),
        P("expert", None, None, None),
        P("expert", None, None, None),
        P("expert", None, None, None),
        P("expert", None, None, None),
    )
    out_specs = P(("expert", "dp"), None)
    return jax.shard_map(shards, mesh=mesh, in_specs=in_specs, out_specs=out_specs, check_vma=False)
```
